32 devices in a mesh: seq: 4 (over z), exp: 8 (over y, x, core).
Axes of the slice: x: 2, y: 2, z: 4, core: 2. Of those that a mesh axis runs over, the one named last changes fastest.
Arguments:
- queries: bfloat16 [8, 512, 2048], P('exp', 'seq'), may hold values from -100 to 100
- keys: bfloat16 [8, 512, 2048], P('exp', 'seq'), may hold values from -4 to 4
- values: bfloat16 [8, 512, 2048], P('exp', 'seq'), may hold values from -6 to 6
- resid: bfloat16 [8, 512, 2048], P('exp', 'seq'), may hold values from -6 to 6
- norm_gain: float32 [2048], replicated, may hold values from 0.1 to 1.9
- w_gate: bfloat16 [8, 2048, 704], P('exp', 'seq'), may hold values from -0.125 to 0.125
- w_up: bfloat16 [8, 2048, 704], P('exp', 'seq'), may hold values from -0.125 to 0.125
- w_down: bfloat16 [8, 704, 2048], P('exp', None, 'seq'), may hold values from -0.21875 to 0.21875
- expert_ids: int32 [8, 512, 2], P('exp', 'seq'), may hold values from 0 to 7, all different within a row; in each aligned block of 128 rows (0 to 127, 128 to 255, ..., all dimensions but the last counted through in order) at most 40 rows name the same one
- route_weights: float32 [8, 512, 2], P('exp', 'seq'), may hold values from 0.25 to 1
- cotangent: bfloat16 [8, 512, 2048], P('exp', 'seq'), may hold values from -6 to 6
Outputs:
- output: bfloat16 [8, 512, 2048], P('exp', 'seq')
- stream_grad: bfloat16 [8, 512, 2048], P('exp', 'seq')
The draws below stay inside these ranges and needn't reach their ends.
Inputs may be any that keep to these rules, and one draw needn't show every extreme that they name: `expert_ids`: within the positions of one device (aligned blocks of 128 positions, taken in order over sequences and positions) no expert is chosen more than 40 times, a bound that some block reaches; the two choices of a position differ.
All inputs are finite; a program needn't handle non-finite values.
Results may differ from the reference program's by a relative error of at most 0.009.
Values may be sent and summed in bfloat16 or wider, within the bound.
No kernel may reach another device: no remote copies, remote signals or barrier semaphores. Data moves between devices by JAX's collectives and lax.ppermute only.
A program may use at most 64 MiB of HBM per device.

```python
import math
import jax
import jax.numpy as jnp
import numpy as np
from jax import lax

H = 16
HD = 128
D = 2048
FFW = 704
TOK_DEV = 128
LEN = 512
SEQS = 8
EXPERTS = 8
CAP = 40


def paired_fields(key):
    base = jax.random.fold_in(key, 7)
    query_key, key_key = jax.random.split(base, 2)
    shaped = (SEQS, LEN, D)
    base_keys = jax.random.truncated_normal(key_key, -4.0, 4.0, shaped, jnp.float32)
    base_queries = jax.random.truncated_normal(query_key, -4.0, 4.0, shaped, jnp.float32)
    keys_out = base_keys
    queries_out = base_queries
    return (queries_out, keys_out)


def draw_queries(key, part):
    return paired_fields(key)[0].astype(jnp.bfloat16)


def draw_keys(key, part):
    return paired_fields(key)[1].astype(jnp.bfloat16)


def shard_levels(rng, dims, cuts, smallest, top_value):
    def one(dim, parts):
        draws = jax.random.uniform(jax.random.fold_in(jax.random.fold_in(rng, 6), dim), (parts,), jnp.float32, smallest / len(cuts), top_value / len(cuts))
        return jnp.repeat(jnp.exp(draws), dims[dim] // parts).reshape((-1,) + (1,) * (len(dims) - dim - 1))

    gain = one(*cuts[0])
    for cut in cuts[1:]:
        gain = gain * one(*cut)
    return gain


def shared_out(rng, own, number, rows, amount, top, bound, slope):
    order = jax.random.permutation(rng, amount)
    heavy_load, common = portions_of(amount, rows * top, bound, slope, True), portions_of(amount, rows * top, bound, slope, False)
    places = jnp.arange(amount)

    def named(tallies, turn):
        used = int((tallies > 0).sum())
        fixed = max(1, used // 4)
        passed = fixed + (places - fixed + turn * (used - fixed)) % max(1, amount - fixed)
        return jnp.zeros((amount,), jnp.int32).at[order[jnp.where(places < fixed, places, passed)]].set(jnp.asarray(tallies, jnp.int32))

    tallies = jnp.where(number % 4 == 0, named(heavy_load, number // 4), named(common, number - number // 4 - 1))
    mixed = jax.random.permutation(jax.random.fold_in(own, 3), amount)
    giver, taker = mixed[0:amount // 2 * 2:2], mixed[1:amount // 2 * 2:2]
    margin = jnp.minimum(tallies[giver] - 1, bound - tallies[taker]) // 2
    margin = jnp.where((giver == order[0]) | (taker == order[0]) | (tallies[taker] == 0), 0, jnp.maximum(margin, 0))
    passed = jax.random.randint(jax.random.fold_in(own, 4), (amount // 2,), 0, 1 << 20) % (margin + 1)
    tallies = tallies.at[giver].add(-passed).at[taker].add(passed)
    labels = jnp.searchsorted(jnp.cumsum(tallies), jnp.arange(rows * top), side="right").astype(jnp.int32)
    listing = labels.reshape(top, rows).T
    listing = listing[jax.random.permutation(jax.random.fold_in(own, 1), rows)]
    turn = jax.random.randint(jax.random.fold_in(own, 2), (rows, 1), 0, top)
    return jnp.take_along_axis(listing, (jnp.arange(top)[None, :] + turn) % top, axis=1)


def portions_of(amount, total, limit, lean, full):
    portions = [(1 << 20) // math.isqrt(rank ** lean) + 1 for rank in range(1, amount + 1)]
    largest = limit if full else min(limit, max(-(-total // amount), total * portions[0] // sum(portions)))
    least = 1 if total - largest >= amount - 1 else 0
    given, spare = [largest] + [least] * (amount - 1), total - largest - least * (amount - 1)
    while spare > 0:
        candidates = [i for i in range(1, amount) if given[i] < largest] or [i for i in range(1, amount) if given[i] < limit]
        whole, left = sum([portions[i] for i in candidates]), spare
        for i in candidates:
            extra = min(limit - given[i], max(1, left * portions[i] // whole), spare)
            given[i] = given[i] + extra
            spare = spare - extra
    return np.array(given)


def scatter_about(key, extent, spread, bound, cuts=(), kind=jnp.bfloat16):
    result = spread * jax.random.normal(key, extent, jnp.float32)
    if cuts:
        result = result * shard_levels(key, extent, cuts, -0.22, 0.18)
    return jnp.clip(result, -bound, bound).astype(kind)


def setup_inputs(seed: int = 0) -> dict:
    key_of = jax.random.split(jax.random.key(seed), 12)
    queries = draw_queries(jax.random.fold_in(key_of[11], 71), 0)
    keys = draw_keys(jax.random.fold_in(key_of[11], 71), 0)
    values = scatter_about(key_of[2], (SEQS, LEN, D), 1.0, 6.0, ((0, 8), (1, 4)))
    resid = scatter_about(key_of[3], (SEQS, LEN, D), 1.0, 6.0, ((0, 8), (1, 4)))
    norm_gain = jnp.clip(1.0 + 0.18 * jax.random.normal(key_of[4], (D,), jnp.float32), 0.1, 1.9)
    w_gate = scatter_about(key_of[5], (EXPERTS, D, FFW), D ** -0.5, 0.125, ((0, 8), (1, 4)))
    w_up = scatter_about(key_of[6], (EXPERTS, D, FFW), D ** -0.5, 0.125, ((0, 8), (1, 4)))
    w_down = scatter_about(key_of[7], (EXPERTS, FFW, D), FFW ** -0.5, 0.21875, ((0, 8), (2, 4)))
    expert_ids_keys = jax.random.split(jax.random.fold_in(key_of[8], 1), SEQS * LEN // TOK_DEV)
    expert_ids_turns = jax.random.permutation(jax.random.fold_in(key_of[8], 3), SEQS * LEN // TOK_DEV)
    expert_ids = jax.vmap(lambda own, number: shared_out(jax.random.fold_in(key_of[8], 2), own, number, TOK_DEV, EXPERTS, 2, CAP, 2))(expert_ids_keys, expert_ids_turns).reshape((SEQS, LEN, 2))
    route_weights = jnp.clip(0.25 + 0.75 * jax.random.uniform(key_of[9], (SEQS, LEN, 2), jnp.float32) ** shard_levels(key_of[9], (SEQS, LEN, 2), ((0, 8), (1, 4)), -0.2, 0.2), 0.25, 1.0)
    cotangent = scatter_about(key_of[10], (SEQS, LEN, D), 1.0, 6.0, ((0, 8), (1, 4)))
    return {"queries": queries, "keys": keys, "values": values, "resid": resid, "norm_gain": norm_gain, "w_gate": w_gate, "w_up": w_up, "w_down": w_down, "expert_ids": expert_ids, "route_weights": route_weights, "cotangent": cotangent}


def keep_bf16(values_in):
    return lax.optimization_barrier(values_in.astype(jnp.bfloat16))

def causal_attention(query_rows, key_rows, value_rows):
    length = query_rows.shape[0]
    block_rows = min(512, length)
    score_scale = HD ** (-0.5)
    pieces = []
    for block in range(length // block_rows):
        start = block * block_rows
        finish = start + block_rows
        query_part = query_rows[start:finish].astype(jnp.float32)
        key_part = key_rows[:finish].astype(jnp.float32)
        value_part = value_rows[:finish].astype(jnp.float32)
        scores = jnp.einsum('qhd,khd->hqk', query_part, key_part) * score_scale
        row_pos = start + lax.broadcasted_iota(jnp.int32, (block_rows, finish), 0)
        col_pos = lax.broadcasted_iota(jnp.int32, (block_rows, finish), 1)
        scores = jnp.where((col_pos <= row_pos)[None], scores, -jnp.inf)
        row_max = lax.optimization_barrier(jnp.max(scores, axis=-1, keepdims=True))
        exp_terms = jnp.exp(scores - row_max)
        totals = lax.optimization_barrier(jnp.sum(exp_terms, axis=-1, keepdims=True))
        prob_rows = keep_bf16(exp_terms / totals)
        context = jnp.einsum('hqk,khd->qhd', prob_rows.astype(jnp.float32), value_part)
        pieces.append(context.astype(jnp.bfloat16))
    return jnp.concatenate(pieces, axis=0)

def reference(queries, keys, values, resid, norm_gain, w_gate, w_up, w_down, expert_ids, route_weights, cotangent):

    def one_sequence(triple):
        query_seq, key_seq, value_seq = triple
        shaped = (LEN, H, HD)
        context = causal_attention(query_seq.reshape(shaped), key_seq.reshape(shaped), value_seq.reshape(shaped))
        return context.reshape(LEN, D)
    context = lax.map(one_sequence, (queries, keys, values))
    stream = keep_bf16(resid.astype(jnp.float32) + context.astype(jnp.float32))
    stream_f = stream.astype(jnp.float32)
    inv_rms = lax.rsqrt(lax.optimization_barrier(jnp.mean(stream_f * stream_f, axis=-1, keepdims=True)) + 1e-05)
    unit_rows = stream_f * inv_rms
    normed = keep_bf16(unit_rows * norm_gain)
    blocks = SEQS * LEN // TOK_DEV
    pair_count = 2 * TOK_DEV
    choices_flat = expert_ids.reshape(blocks, pair_count)
    member = (choices_flat[..., None] == jnp.arange(EXPERTS, dtype=jnp.int32)).astype(jnp.int32)
    before = jnp.cumsum(member, axis=1) - member
    slot_of = lax.optimization_barrier(jnp.sum(before * member, axis=-1)).astype(jnp.int32)
    target = (choices_flat * CAP + slot_of).astype(jnp.int32)
    block_index = jnp.arange(blocks, dtype=jnp.int32)[:, None]
    pair_index = jnp.broadcast_to(jnp.arange(pair_count, dtype=jnp.int32)[None], (blocks, pair_count))
    table = jnp.full((blocks, EXPERTS * CAP), pair_count, jnp.int32).at[block_index, target].set(pair_index)
    normed_blocks = normed.reshape(blocks, TOK_DEV, D)
    cot_f = cotangent.astype(jnp.float32)
    scaled_cot = keep_bf16(route_weights[..., None] * cot_f[:, :, None, :])
    scaled_blocks = scaled_cot.reshape(blocks, pair_count, D)

    def one_expert(expert):
        chosen = lax.dynamic_slice_in_dim(table, expert * CAP, CAP, 1)
        present = (chosen < pair_count)[..., None]
        safe_pair = jnp.where(chosen < pair_count, chosen, 0).astype(jnp.int32)
        token_rows = jnp.take_along_axis(normed_blocks, (safe_pair // 2)[..., None], axis=1)
        token_rows = jnp.where(present, token_rows.astype(jnp.float32), 0.0)
        cot_rows = jnp.take_along_axis(scaled_blocks, safe_pair[..., None], axis=1)
        cot_rows = jnp.where(present, cot_rows.astype(jnp.float32), 0.0)
        gate_w = w_gate[expert].astype(jnp.float32)
        up_w = w_up[expert].astype(jnp.float32)
        down_w = w_down[expert].astype(jnp.float32)
        gate_pre = jnp.einsum('bcd,df->bcf', token_rows, gate_w)
        up_pre = jnp.einsum('bcd,df->bcf', token_rows, up_w)
        sigma = jax.nn.sigmoid(gate_pre)
        silu_vals = gate_pre * sigma
        hidden = keep_bf16(silu_vals * up_pre)
        out_rows = jnp.einsum('bcf,fd->bcd', hidden.astype(jnp.float32), down_w).astype(jnp.bfloat16)
        d_hidden = jnp.einsum('bcd,fd->bcf', cot_rows, down_w)
        d_gate = keep_bf16(d_hidden * up_pre * sigma * (1.0 + gate_pre * (1.0 - sigma)))
        d_up = keep_bf16(d_hidden * silu_vals)
        d_rows = jnp.einsum('bcf,df->bcd', d_gate.astype(jnp.float32), gate_w)
        d_rows = d_rows + jnp.einsum('bcf,df->bcd', d_up.astype(jnp.float32), up_w)
        return (out_rows, d_rows.astype(jnp.bfloat16))
    expert_outs, expert_grads = lax.map(one_expert, jnp.arange(EXPERTS, dtype=jnp.int32))
    pair_out = expert_outs[choices_flat, block_index, slot_of].reshape(SEQS, LEN, 2, D).astype(jnp.float32)
    pair_grad = expert_grads[choices_flat, block_index, slot_of].reshape(SEQS, LEN, 2, D).astype(jnp.float32)
    output = (stream_f + lax.optimization_barrier(jnp.sum(route_weights[..., None] * pair_out, axis=2))).astype(jnp.bfloat16)
    d_normed = lax.optimization_barrier(jnp.sum(pair_grad, axis=2))
    gained = d_normed * norm_gain
    d_stream = inv_rms * (gained - unit_rows * lax.optimization_barrier(jnp.mean(gained * unit_rows, axis=-1, keepdims=True)))
    stream_grad = (cot_f + d_stream).astype(jnp.bfloat16)
    return (output, stream_grad)
```

```python
import functools

import jax
import jax.numpy as jnp
from jax import lax
from jax.experimental import pallas as pl
from jax.experimental.pallas import tpu as pltpu
from jax.sharding import PartitionSpec as P

HD = 128
BF = jnp.bfloat16
F32 = jnp.float32
MIB = 1 << 20
ANY = pl.BlockSpec(memory_space=pl.ANY)
VMEM = pl.BlockSpec(memory_space=pltpu.VMEM)
SMEM = pl.BlockSpec(memory_space=pltpu.SMEM)
NT = (((1,), (1,)), ((), ()))
NN = (((1,), (0,)), ((), ()))


def mm(a, b, dims):
    return lax.dot_general(a, b, dims, preferred_element_type=F32)


def call(kernel, outs, args, in_specs, scratch=(), flops=0, moved=0, vmem=40):
    return pl.pallas_call(
        kernel,
        out_shape=outs,
        in_specs=in_specs,
        out_specs=jax.tree.map(lambda _: VMEM, outs),
        scratch_shapes=list(scratch),
        compiler_params=pltpu.CompilerParams(vmem_limit_bytes=vmem * MIB),
        cost_estimate=pl.CostEstimate(flops=flops, bytes_accessed=moved, transcendentals=0),
    )(*args)


def sds(shape, dtype=BF):
    return jax.ShapeDtypeStruct(shape, dtype)


def pack_kernel(q_ref, k_ref, v_ref, o_ref):
    rows = q_ref.shape[0]
    o_ref[0, 0:rows] = q_ref[...]
    o_ref[0, rows : 2 * rows] = k_ref[...]
    o_ref[0, 2 * rows : 3 * rows] = v_ref[...]


def pack(q, k, v, groups):
    rows, width = q.shape
    part = width // groups
    spec = pl.BlockSpec((rows, part), lambda g: (0, g))
    return pl.pallas_call(
        pack_kernel,
        grid=(groups,),
        out_shape=sds((groups, 3 * rows, part)),
        in_specs=[spec] * 3,
        out_specs=pl.BlockSpec((1, 3 * rows, part), lambda g: (g, 0, 0)),
        cost_estimate=pl.CostEstimate(
            flops=0, bytes_accessed=12 * rows * width, transcendentals=0
        ),
    )(q, k, v)


def attend_kernel(x_ref, o_ref):
    blocks, three, hd = x_ref.shape
    rows = three // 3
    scale = HD ** (-0.5)
    keys = x_ref[:, rows : 2 * rows, :].reshape(blocks * rows, hd)
    vals = x_ref[:, 2 * rows : 3 * rows, :].reshape(blocks * rows, hd)
    row_ids = lax.broadcasted_iota(jnp.int32, (rows, rows), 0)
    col_ids = lax.broadcasted_iota(jnp.int32, (rows, rows), 1)
    keep = col_ids <= row_ids
    for b in range(blocks):
        query = x_ref[b, 0:rows, :]
        end = b * rows
        diag = mm(query, keys[end : end + rows], NT) * scale
        diag = jnp.where(keep, diag, -jnp.inf)
        top = jnp.max(diag, axis=-1, keepdims=True)
        if b:
            early = mm(query, keys[:end], NT) * scale
            top = jnp.maximum(top, jnp.max(early, axis=-1, keepdims=True))
        diag = jnp.exp(diag - top)
        total = jnp.sum(diag, axis=-1, keepdims=True)
        if b:
            early = jnp.exp(early - top)
            total = total + jnp.sum(early, axis=-1, keepdims=True)
        inverse = 1.0 / total
        ctx = mm((diag * inverse).astype(BF), vals[end : end + rows], NN)
        if b:
            ctx = ctx + mm((early * inverse).astype(BF), vals[:end], NN)
        o_ref[b] = ctx.astype(BF)


def attend(x):
    blocks, three, part = x.shape
    rows = three // 3
    length = blocks * rows
    return pl.pallas_call(
        attend_kernel,
        grid=(part // HD,),
        out_shape=sds((blocks, rows, part)),
        in_specs=[pl.BlockSpec((blocks, three, HD), lambda h: (0, 0, h))],
        out_specs=pl.BlockSpec((blocks, rows, HD), lambda h: (0, 0, h)),
        compiler_params=pltpu.CompilerParams(vmem_limit_bytes=40 * MIB),
        cost_estimate=pl.CostEstimate(
            flops=4 * length * length * part,
            bytes_accessed=8 * length * part,
            transcendentals=length * length * part // HD,
        ),
    )(x)


def slot_rows(ids_t, owners, cap):
    tokens = ids_t.shape[1]
    experts = lax.broadcasted_iota(jnp.int32, (owners, tokens), 0)
    first = (experts == ids_t[0:1]).astype(F32)
    second = (experts == ids_t[1:2]).astype(F32)
    src = lax.broadcasted_iota(jnp.int32, (tokens, tokens), 0)
    dst = lax.broadcasted_iota(jnp.int32, (tokens, tokens), 1)
    earlier = (src < dst).astype(F32).astype(BF)
    count = mm((first + second).astype(BF), earlier, NN)
    slot0 = jnp.sum(first * count, axis=0, keepdims=True).astype(jnp.int32)
    slot1 = jnp.sum(second * count, axis=0, keepdims=True).astype(jnp.int32)
    return ids_t[0:1] * cap + slot0, ids_t[1:2] * cap + slot1


def slot_cols(ids, owners, cap):
    tokens = ids.shape[0]
    experts = lax.broadcasted_iota(jnp.int32, (tokens, owners), 1)
    first = (experts == ids[:, 0:1]).astype(F32)
    second = (experts == ids[:, 1:2]).astype(F32)
    dst = lax.broadcasted_iota(jnp.int32, (tokens, tokens), 0)
    src = lax.broadcasted_iota(jnp.int32, (tokens, tokens), 1)
    earlier = (src < dst).astype(F32).astype(BF)
    count = mm(earlier, (first + second).astype(BF), NN)
    slot0 = jnp.sum(first * count, axis=1, keepdims=True).astype(jnp.int32)
    slot1 = jnp.sum(second * count, axis=1, keepdims=True).astype(jnp.int32)
    return ids[:, 0:1] * cap + slot0, ids[:, 1:2] * cap + slot1


def one_hot(hit):
    return jnp.where(hit, 1.0, 0.0).astype(BF)


def send_cot_kernel(owners, cap, ids_ref, w_ref, cot_ref, o_ref):
    tokens = cot_ref.shape[0]
    at0, at1 = slot_rows(ids_ref[...], owners, cap)
    rows = lax.broadcasted_iota(jnp.int32, (owners * cap, tokens), 0)
    cot = cot_ref[...].astype(F32)
    o_ref[...] = (
        mm(one_hot(rows == at0), (w_ref[:, 0:1] * cot).astype(BF), NN)
        + mm(one_hot(rows == at1), (w_ref[:, 1:2] * cot).astype(BF), NN)
    ).astype(BF)


def norm_kernel(owners, cap, ids_ref, ctx_ref, resid_ref, gain_ref, stream_ref, o_ref):
    groups, tokens, part = ctx_ref.shape
    width = groups * part
    square = jnp.zeros((tokens, 1), F32)
    for g in range(groups):
        cols = slice(g * part, (g + 1) * part)
        stream = (resid_ref[:, cols].astype(F32) + ctx_ref[g].astype(F32)).astype(BF)
        stream_ref[:, cols] = stream
        stream = stream.astype(F32)
        square = square + jnp.sum(stream * stream, axis=-1, keepdims=True)
    inv_rms = lax.rsqrt(square / width + 1e-05)
    at0, at1 = slot_rows(ids_ref[...], owners, cap)
    rows = lax.broadcasted_iota(jnp.int32, (owners * cap, tokens), 0)
    pick = one_hot((rows == at0) | (rows == at1))
    for g in range(groups):
        cols = slice(g * part, (g + 1) * part)
        normed = ((stream_ref[:, cols].astype(F32) * inv_rms) * gain_ref[:, cols]).astype(BF)
        o_ref[:, cols] = mm(pick, normed, NN).astype(BF)


def fetch(inner, choices, dst, sem):
    if len(choices) == 1:
        pltpu.make_async_copy(choices[0], dst, sem).start()
        return

    @pl.when(inner == 1)
    def _():
        pltpu.make_async_copy(choices[0], dst, sem).start()

    @pl.when(inner == 0)
    def _():
        pltpu.make_async_copy(choices[1], dst, sem).start()


def arrived(choices, dst, sem):
    pltpu.make_async_copy(choices[0], dst, sem).wait()


def regroup(refs, shape):
    refs = list(refs)
    return [[refs.pop(0) for _ in range(size)] for size in shape], refs


def cols_of(place_ref, slot, part):
    return pl.ds(pl.multiple_of(place_ref[1 + slot] * part, part), part)


def up_kernel(shape, place_ref, x_ref, *refs):
    slots = len(shape)
    gate_in, refs = regroup(refs, shape)
    up_in, refs = regroup(refs, shape)
    hidden_ref, to_gate_ref, to_up_ref, gate_w, up_w, sems = refs
    part = gate_w.shape[2]
    inner = place_ref[0]
    for j in range(slots):
        fetch(inner, gate_in[j], gate_w.at[j], sems.at[0, j])
        fetch(inner, up_in[j], up_w.at[j], sems.at[1, j])
    gate = up = None
    for j in range(slots):
        rows = x_ref[:, cols_of(place_ref, j, part)]
        arrived(gate_in[j], gate_w.at[j], sems.at[0, j])
        term = mm(rows, gate_w[j], NT)
        gate = term if gate is None else gate + term
        arrived(up_in[j], up_w.at[j], sems.at[1, j])
        term = mm(rows, up_w[j], NT)
        up = term if up is None else up + term
    sigma = 1.0 / (1.0 + jnp.exp(-gate))
    silu = gate * sigma
    hidden_ref[...] = (silu * up).astype(BF)
    to_gate_ref[...] = up * sigma * (1.0 + gate * (1.0 - sigma))
    to_up_ref[...] = silu


def down_kernel(shape, place_ref, hidden_ref, cot_ref, *refs):
    slots = len(shape)
    down_in, refs = regroup(refs, shape)
    out_ref, d_hidden_ref, down_w, sems = refs
    part = down_w.shape[2]
    inner = place_ref[0]
    for j in range(slots):
        fetch(inner, down_in[j], down_w.at[j], sems.at[j])
    total = None
    for j in range(slots):
        rows = cot_ref[:, cols_of(place_ref, j, part)]
        arrived(down_in[j], down_w.at[j], sems.at[j])
        term = mm(rows, down_w[j], NT)
        total = term if total is None else total + term
        out_ref[:, j * part : (j + 1) * part] = mm(hidden_ref[...], down_w[j], NN).astype(BF)
    d_hidden_ref[...] = total


def grad_kernel(
    shape, place_ref, hidden_ref, cot_ref, d_hidden_ref, to_gate_ref, to_up_ref, *refs
):
    slots = len(shape)
    down_in, refs = regroup(refs, shape[-1:])
    gate_in, refs = regroup(refs, shape)
    up_in, refs = regroup(refs, shape)
    o_ref, down_w, gate_w, up_w, sems = refs
    part = down_w.shape[1]
    inner = place_ref[0]
    fetch(inner, down_in[0], down_w, sems.at[2, 0])
    for j in range(slots):
        fetch(inner, gate_in[j], gate_w.at[j], sems.at[0, j])
        fetch(inner, up_in[j], up_w.at[j], sems.at[1, j])
    rows = cot_ref[:, cols_of(place_ref, slots - 1, part)]
    arrived(down_in[0], down_w, sems.at[2, 0])
    d_hidden = d_hidden_ref[...] + mm(rows, down_w[...], NT)
    d_gate = (d_hidden * to_gate_ref[...]).astype(BF)
    d_up = (d_hidden * to_up_ref[...]).astype(BF)
    o_ref[:, slots * part :] = mm(hidden_ref[...], down_w[...], NN).astype(BF)
    for j in range(slots):
        arrived(gate_in[j], gate_w.at[j], sems.at[0, j])
        arrived(up_in[j], up_w.at[j], sems.at[1, j])
        o_ref[:, j * part : (j + 1) * part] = (
            mm(d_gate, gate_w[j], NN) + mm(d_up, up_w[j], NN)
        ).astype(BF)


def final_kernel(
    owners,
    cap,
    place_ref,
    ids_ref,
    w_ref,
    gain_ref,
    stream_ref,
    cot_ref,
    first_ref,
    last_ref,
    output_ref,
    grad_ref,
    d_normed_ref,
):
    tokens, width = stream_ref.shape
    done = first_ref.shape[1]
    part = width - done
    slots = width // part
    at0, at1 = slot_cols(ids_ref[...], owners, cap)
    rows = lax.broadcasted_iota(jnp.int32, (tokens, owners * cap), 1)
    pick0, pick1 = one_hot(rows == at0), one_hot(rows == at1)
    both = pick0 + pick1
    w0, w1 = w_ref[:, 0:1], w_ref[:, 1:2]
    square = jnp.zeros((tokens, 1), F32)
    dot = jnp.zeros((tokens, 1), F32)
    for j in range(slots):
        cols = cols_of(place_ref, j, part)
        if j < slots - 1:
            pairs = first_ref[:, j * part : (j + 1) * part]
        else:
            pairs = last_ref[:, width : width + part]
        stream = stream_ref[:, cols].astype(F32)
        mixed = w0 * mm(pick0, pairs, NN) + w1 * mm(pick1, pairs, NN)
        output_ref[:, cols] = (stream + mixed).astype(BF)
        gained = mm(both, last_ref[:, j * part : (j + 1) * part], NN) * gain_ref[:, cols]
        d_normed_ref[:, cols] = gained
        square = square + jnp.sum(stream * stream, axis=-1, keepdims=True)
        dot = dot + jnp.sum(gained * stream, axis=-1, keepdims=True)
    inv_rms = lax.rsqrt(square / width + 1e-05)
    mean = dot * inv_rms / width
    unit_rows = stream_ref[...].astype(F32) * inv_rms
    d_stream = inv_rms * (d_normed_ref[...] - unit_rows * mean)
    grad_ref[...] = (cot_ref[...].astype(F32) + d_stream).astype(BF)


def gather_line(shard, groups):
    if groups == 4:
        near = lax.ppermute(shard, "seq", [(0, 1), (1, 0), (2, 3), (3, 2)])
        across = lax.ppermute(shard, "seq", [(1, 2), (2, 1)])
        across_near = lax.ppermute(near, "seq", [(1, 2), (2, 1)])
        far = lax.ppermute(across, "seq", [(1, 0), (2, 3)])
        far_near = lax.ppermute(across_near, "seq", [(1, 0), (2, 3)])
        return [[shard], [near], [across, far], [across_near, far_near]]
    whole = lax.all_gather(shard, "seq", axis=0)
    return [[whole[j]] for j in range(groups)]


def places(groups):
    if groups == 4:
        own = lax.axis_index("seq")
        table = jnp.array(
            [[0, 0, 1, 2, 3], [1, 1, 0, 2, 3], [1, 2, 3, 1, 0], [0, 3, 2, 1, 0]], jnp.int32
        )
        return table[own]
    return jnp.arange(-1, groups, dtype=jnp.int32)


def exchange(rows, owners, axis):
    total, width = rows.shape
    rows = rows.reshape(owners, total // owners, width)
    rows = lax.all_to_all(rows, axis, split_axis=0, concat_axis=0, tiled=True)
    return rows.reshape(total, width)


def flat(slots):
    return [ref for choices in slots for ref in choices]


def per_device(
    queries,
    keys,
    values,
    resid,
    norm_gain,
    w_gate,
    w_up,
    w_down,
    expert_ids,
    route_weights,
    cotangent,
):
    groups = lax.axis_size("seq")
    owners = lax.axis_size("exp")
    tokens, width = queries.shape[1:]
    ffw = w_gate.shape[2]
    part = width // groups
    cap = max(2, tokens * 10 // (4 * owners))
    total = owners * cap
    ids = expert_ids[0]
    ids_t = ids.T
    weights = route_weights[0]
    gain = norm_gain[None]
    cot = cotangent[0]
    place = places(groups)

    packed = pack(queries[0], keys[0], values[0], groups)
    heads = lax.all_to_all(packed, "seq", split_axis=0, concat_axis=0, tiled=True)
    gate_in = gather_line(w_gate[0].T, groups)
    up_in = gather_line(w_up[0].T, groups)
    down_in = gather_line(w_down[0], groups)
    shape = [len(choices) for choices in gate_in]
    ctx = attend(heads)
    ctx = lax.all_to_all(ctx, "seq", split_axis=0, concat_axis=0, tiled=True)

    one = 2 * total * width * ffw
    send_cot = call(
        functools.partial(send_cot_kernel, owners, cap),
        sds((total, width)),
        (ids_t, weights, cot),
        [VMEM] * 3,
        flops=4 * total * tokens * width,
        moved=2 * (total + tokens) * width,
    )
    cot_rows = exchange(send_cot, owners, "exp")
    stream, send_rows = call(
        functools.partial(norm_kernel, owners, cap),
        (sds((tokens, width)), sds((total, width))),
        (ids_t, ctx, resid[0], gain),
        [VMEM] * 4,
        flops=2 * total * tokens * width,
        moved=2 * (total + 3 * tokens) * width,
    )
    rows = exchange(send_rows, owners, "exp")

    full_w = pltpu.VMEM((groups, ffw, part), BF)
    hidden, to_gate, to_up = call(
        functools.partial(up_kernel, shape),
        (sds((total, ffw)), sds((total, ffw), F32), sds((total, ffw), F32)),
        (place, rows, *flat(gate_in), *flat(up_in)),
        [SMEM, VMEM] + [ANY] * (2 * sum(shape)),
        [full_w, full_w, pltpu.SemaphoreType.DMA((2, groups))],
        flops=2 * one,
        moved=4 * width * ffw + 2 * total * width + 10 * total * ffw,
    )
    out_first, d_hidden = call(
        functools.partial(down_kernel, shape[:-1]),
        (sds((total, width - part)), sds((total, ffw), F32)),
        (place, hidden, cot_rows, *flat(down_in[:-1])),
        [SMEM, VMEM, VMEM] + [ANY] * sum(shape[:-1]),
        [
            pltpu.VMEM((groups - 1, ffw, part), BF),
            pltpu.SemaphoreType.DMA((groups - 1,)),
        ],
        flops=2 * one * (groups - 1) // groups,
        moved=2 * width * ffw + 4 * total * width + 6 * total * ffw,
    )
    back_first = exchange(out_first, owners, "exp")
    back = call(
        functools.partial(grad_kernel, shape),
        sds((total, width + part)),
        (
            place,
            hidden,
            cot_rows,
            d_hidden,
            to_gate,
            to_up,
            *flat(down_in[-1:]),
            *flat(gate_in),
            *flat(up_in),
        ),
        [SMEM] + [VMEM] * 5 + [ANY] * (shape[-1] + 2 * sum(shape)),
        [
            pltpu.VMEM((ffw, part), BF),
            full_w,
            full_w,
            pltpu.SemaphoreType.DMA((3, groups)),
        ],
        flops=2 * one + 2 * one // groups,
        moved=4 * width * ffw + 4 * total * width + 14 * total * ffw,
    )
    back_last = exchange(back, owners, "exp")
    output, stream_grad = call(
        functools.partial(final_kernel, owners, cap),
        (sds((tokens, width)), sds((tokens, width))),
        (place, ids, weights, gain, stream, cot, back_first, back_last),
        [SMEM] + [VMEM] * 7,
        [pltpu.VMEM((tokens, width), F32)],
        flops=6 * total * tokens * width,
        moved=4 * total * width + 8 * tokens * width,
    )
    return (output[None], stream_grad[None])


def solution(mesh):
    placed = (
        P("exp", "seq", None),
        P("exp", "seq", None),
        P("exp", "seq", None),
        P("exp", "seq", None),
        P(),
        P("exp", "seq", None),
        P("exp", "seq", None),
        P("exp", None, "seq"),
        P("exp", "seq", None),
        P("exp", "seq", None),
        P("exp", "seq", None),
    )
    return jax.shard_map(
        per_device,
        mesh=mesh,
        in_specs=placed,
        out_specs=(P("exp", "seq", None), P("exp", "seq", None)),
        check_vma=False,
    )
```

```python
import functools

import jax
import jax.numpy as jnp
from jax import lax
from jax.experimental import pallas as pl
from jax.experimental.pallas import tpu as pltpu
from jax.sharding import PartitionSpec as P

HD = 128
BF = jnp.bfloat16
F32 = jnp.float32
MIB = 1 << 20
HBM = pl.BlockSpec(memory_space=pltpu.HBM)
VMEM = pl.BlockSpec(memory_space=pltpu.VMEM)
SMEM = pl.BlockSpec(memory_space=pltpu.SMEM)
NT = (((1,), (1,)), ((), ()))
NN = (((1,), (0,)), ((), ()))


def mm(a, b, dims):
    return lax.dot_general(a, b, dims, preferred_element_type=F32)


def call(kernel, outs, args, in_specs, scratch=(), flops=0, moved=0, vmem=16, after=()):
    count, extra = len(args), len(after)

    def body(*refs):
        kernel(*refs[:count], *refs[count + extra :])

    return pl.pallas_call(
        body,
        out_shape=outs,
        in_specs=[*in_specs, *[HBM] * extra],
        out_specs=jax.tree.map(lambda _: VMEM, outs),
        scratch_shapes=list(scratch),
        compiler_params=pltpu.CompilerParams(vmem_limit_bytes=vmem * MIB),
        cost_estimate=pl.CostEstimate(flops=flops, bytes_accessed=moved, transcendentals=0),
    )(*args, *after)


def sds(shape, dtype=BF):
    return jax.ShapeDtypeStruct(shape, dtype)


def pack_kernel(q_ref, k_ref, v_ref, o_ref):
    rows = q_ref.shape[0]
    o_ref[0, 0:rows] = q_ref[...]
    o_ref[0, rows : 2 * rows] = k_ref[...]
    o_ref[0, 2 * rows : 3 * rows] = v_ref[...]


def pack(q, k, v, groups):
    rows, width = q.shape
    part = width // groups
    spec = pl.BlockSpec((rows, part), lambda g: (0, g))
    return pl.pallas_call(
        pack_kernel,
        grid=(groups,),
        out_shape=sds((groups, 3 * rows, part)),
        in_specs=[spec] * 3,
        out_specs=pl.BlockSpec((1, 3 * rows, part), lambda g: (g, 0, 0)),
        cost_estimate=pl.CostEstimate(
            flops=0, bytes_accessed=12 * rows * width, transcendentals=0
        ),
    )(q, k, v)


def attend_head(blocks, query_of, keys, vals, store):
    rows = keys.shape[0] // blocks
    scale = HD ** (-0.5)
    row_ids = lax.broadcasted_iota(jnp.int32, (rows, rows), 0)
    col_ids = lax.broadcasted_iota(jnp.int32, (rows, rows), 1)
    keep = col_ids <= row_ids
    for b in range(blocks):
        query = query_of(b)
        end = b * rows
        diag = mm(query, keys[end : end + rows], NT) * scale
        diag = jnp.where(keep, diag, -jnp.inf)
        top = jnp.max(diag, axis=-1, keepdims=True)
        if b:
            early = mm(query, keys[:end], NT) * scale
            top = jnp.maximum(top, jnp.max(early, axis=-1, keepdims=True))
        diag = jnp.exp(diag - top)
        total = jnp.sum(diag, axis=-1, keepdims=True)
        if b:
            early = jnp.exp(early - top)
            total = total + jnp.sum(early, axis=-1, keepdims=True)
        inverse = 1.0 / total
        ctx = mm((diag * inverse).astype(BF), vals[end : end + rows], NN)
        if b:
            ctx = ctx + mm((early * inverse).astype(BF), vals[:end], NN)
        store(b, ctx.astype(BF))


def attend_kernel(x_ref, o_ref):
    blocks, three, hd = x_ref.shape
    rows = three // 3

    def store(b, ctx):
        o_ref[b] = ctx

    attend_head(
        blocks,
        lambda b: x_ref[b, 0:rows, :],
        x_ref[:, rows : 2 * rows, :].reshape(blocks * rows, hd),
        x_ref[:, 2 * rows : 3 * rows, :].reshape(blocks * rows, hd),
        store,
    )


def attend(x):
    blocks, three, part = x.shape
    rows = three // 3
    length = blocks * rows
    return pl.pallas_call(
        attend_kernel,
        grid=(part // HD,),
        out_shape=sds((blocks, rows, part)),
        in_specs=[pl.BlockSpec((blocks, three, HD), lambda h: (0, 0, h))],
        out_specs=pl.BlockSpec((blocks, rows, HD), lambda h: (0, 0, h)),
        compiler_params=pltpu.CompilerParams(vmem_limit_bytes=40 * MIB),
        cost_estimate=pl.CostEstimate(
            flops=4 * length * length * part,
            bytes_accessed=8 * length * part,
            transcendentals=length * length * part // HD,
        ),
    )(x)


INNER, COLS, PLANE, ATTEND = 0, 1, 5, 6


def halves_kernel(place_ref, q_ref, k_ref, v_ref, first_ref, second_ref):
    rows, width = q_ref.shape
    half = width // 2

    def copy(lower, upper):
        for i, ref in enumerate((q_ref, k_ref, v_ref)):
            lower[i * rows : (i + 1) * rows] = ref[:, :half]
            upper[i * rows : (i + 1) * rows] = ref[:, half:]

    @pl.when(place_ref[PLANE] < 2)
    def _():
        copy(first_ref, second_ref)

    @pl.when(place_ref[PLANE] >= 2)
    def _():
        copy(second_ref, first_ref)


def middle_kernel(place_ref, own_in, near_in, mid_in, far_in, *refs):
    *outs, x_ref, ctx_ref, sems = refs
    blocks, three, half = x_ref.shape
    rows = three // 3

    @pl.when(place_ref[INNER] == 1)
    def _():
        copies = [
            pltpu.make_async_copy(ref, x_ref.at[place_ref[ATTEND + i]], sems.at[i])
            for i, ref in enumerate((own_in, near_in, mid_in, far_in))
        ]
        for copy in copies:
            copy.start()
        for copy in copies:
            copy.wait()

        def step(i, carry):
            for j in range(2):
                cols = pl.ds(pl.multiple_of((2 * i + j) * HD, HD), HD)

                def store(b, ctx, cols=cols):
                    ctx_ref[b, :, cols] = ctx

                attend_head(
                    blocks,
                    lambda b, cols=cols: x_ref[b, 0:rows, cols],
                    x_ref[:, rows : 2 * rows, cols].reshape(blocks * rows, HD),
                    x_ref[:, 2 * rows : 3 * rows, cols].reshape(blocks * rows, HD),
                    store,
                )
            return carry

        lax.fori_loop(0, half // HD // 2, step, 0)
        for i, out in enumerate(outs):
            out[...] = ctx_ref[place_ref[ATTEND + i]]


def attend_middle(place, queries, keys, values, after):
    rows, width = queries.shape
    half = width // 2
    block = sds((3 * rows, half))
    first, second = call(
        halves_kernel,
        (block, block),
        (place, queries, keys, values),
        [SMEM, VMEM, VMEM, VMEM],
        moved=12 * rows * width,
    )
    near = lax.ppermute(first, "seq", [(0, 1), (3, 2)])
    mid = lax.ppermute(second, "seq", [(1, 2), (2, 1)])
    far = lax.ppermute(second, "seq", [(0, 2), (3, 1)])
    piece = sds((rows, half))
    own, near, mid, far = call(
        middle_kernel,
        (piece,) * 4,
        (place, first, near, mid, far),
        [SMEM] + [HBM] * 4,
        [
            pltpu.VMEM((4, 3 * rows, half), BF),
            pltpu.VMEM((4, rows, half), BF),
            pltpu.SemaphoreType.DMA((4,)),
        ],
        flops=64 * rows * rows * half,
        moved=32 * rows * half,
        after=after,
    )
    near = lax.ppermute(near, "seq", [(1, 0), (2, 3)])
    mid = lax.ppermute(mid, "seq", [(1, 2), (2, 1)])
    far = lax.ppermute(far, "seq", [(2, 0), (1, 3)])
    return own, near, mid, far


def join_middle(place_ref, pieces, ctx_ref):
    own, near, mid, far = pieces
    half = own.shape[1]
    for plane, (lower, upper) in enumerate(((near, far), (own, mid), (mid, own), (far, near))):

        @pl.when(place_ref[PLANE] == plane)
        def _(lower=lower, upper=upper):
            ctx_ref[:, :half] = lower[...]
            ctx_ref[:, half:] = upper[...]


def join_groups(place_ref, pieces, ctx_ref):
    (ctx,) = pieces
    groups, _, part = ctx.shape
    for g in range(groups):
        ctx_ref[:, g * part : (g + 1) * part] = ctx[g]


def slot_rows(ids_t, owners, cap):
    tokens = ids_t.shape[1]
    experts = lax.broadcasted_iota(jnp.int32, (owners, tokens), 0)
    first = (experts == ids_t[0:1]).astype(F32)
    second = (experts == ids_t[1:2]).astype(F32)
    src = lax.broadcasted_iota(jnp.int32, (tokens, tokens), 0)
    dst = lax.broadcasted_iota(jnp.int32, (tokens, tokens), 1)
    earlier = (src < dst).astype(F32).astype(BF)
    count = mm((first + second).astype(BF), earlier, NN)
    slot0 = jnp.sum(first * count, axis=0, keepdims=True).astype(jnp.int32)
    slot1 = jnp.sum(second * count, axis=0, keepdims=True).astype(jnp.int32)
    return ids_t[0:1] * cap + slot0, ids_t[1:2] * cap + slot1


def slot_cols(ids, owners, cap):
    tokens = ids.shape[0]
    experts = lax.broadcasted_iota(jnp.int32, (tokens, owners), 1)
    first = (experts == ids[:, 0:1]).astype(F32)
    second = (experts == ids[:, 1:2]).astype(F32)
    dst = lax.broadcasted_iota(jnp.int32, (tokens, tokens), 0)
    src = lax.broadcasted_iota(jnp.int32, (tokens, tokens), 1)
    earlier = (src < dst).astype(F32).astype(BF)
    count = mm(earlier, (first + second).astype(BF), NN)
    slot0 = jnp.sum(first * count, axis=1, keepdims=True).astype(jnp.int32)
    slot1 = jnp.sum(second * count, axis=1, keepdims=True).astype(jnp.int32)
    return ids[:, 0:1] * cap + slot0, ids[:, 1:2] * cap + slot1


def one_hot(hit):
    return jnp.where(hit, 1.0, 0.0).astype(BF)


def send_cot_kernel(owners, cap, ids_ref, w_ref, cot_ref, o_ref):
    tokens = cot_ref.shape[0]
    at0, at1 = slot_rows(ids_ref[...], owners, cap)
    rows = lax.broadcasted_iota(jnp.int32, (owners * cap, tokens), 0)
    cot = cot_ref[...].astype(F32)
    o_ref[...] = (
        mm(one_hot(rows == at0), (w_ref[:, 0:1] * cot).astype(BF), NN)
        + mm(one_hot(rows == at1), (w_ref[:, 1:2] * cot).astype(BF), NN)
    ).astype(BF)


def norm_kernel(owners, cap, join, place_ref, ids_ref, resid_ref, gain_ref, *refs):
    *pieces, stream_ref, o_ref, ctx_ref = refs
    tokens, width = resid_ref.shape
    join(place_ref, pieces, ctx_ref)
    stream = (resid_ref[...].astype(F32) + ctx_ref[...].astype(F32)).astype(BF)
    stream_ref[...] = stream
    stream = stream.astype(F32)
    square = jnp.sum(stream * stream, axis=-1, keepdims=True)
    inv_rms = lax.rsqrt(square / width + 1e-05)
    at0, at1 = slot_rows(ids_ref[...], owners, cap)
    rows = lax.broadcasted_iota(jnp.int32, (owners * cap, tokens), 0)
    pick = one_hot((rows == at0) | (rows == at1))
    normed = ((stream_ref[...].astype(F32) * inv_rms) * gain_ref[...]).astype(BF)
    o_ref[...] = mm(pick, normed, NN).astype(BF)


def fetch(inner, choices, dst, sem):
    if len(choices) == 1:
        pltpu.make_async_copy(choices[0], dst, sem).start()
        return

    @pl.when(inner == 1)
    def _():
        pltpu.make_async_copy(choices[0], dst, sem).start()

    @pl.when(inner == 0)
    def _():
        pltpu.make_async_copy(choices[1], dst, sem).start()


def arrived(choices, dst, sem):
    pltpu.make_async_copy(choices[0], dst, sem).wait()


def regroup(refs, shape):
    refs = list(refs)
    return [[refs.pop(0) for _ in range(size)] for size in shape], refs


def cols_of(place_ref, slot, part):
    return pl.ds(pl.multiple_of(place_ref[COLS + slot] * part, part), part)


def up_kernel(shape, place_ref, x_ref, *refs):
    slots = len(shape)
    gate_in, refs = regroup(refs, shape)
    up_in, refs = regroup(refs, shape)
    hidden_ref, to_gate_ref, to_up_ref, gate_w, up_w, sems = refs
    part = gate_w.shape[2]
    inner = place_ref[INNER]
    for j in range(slots):
        fetch(inner, gate_in[j], gate_w.at[j], sems.at[0, j])
        fetch(inner, up_in[j], up_w.at[j], sems.at[1, j])
    gate = up = None
    for j in range(slots):
        rows = x_ref[:, cols_of(place_ref, j, part)]
        arrived(gate_in[j], gate_w.at[j], sems.at[0, j])
        term = mm(rows, gate_w[j], NT)
        gate = term if gate is None else gate + term
        arrived(up_in[j], up_w.at[j], sems.at[1, j])
        term = mm(rows, up_w[j], NT)
        up = term if up is None else up + term
    sigma = 1.0 / (1.0 + jnp.exp(-gate))
    silu = gate * sigma
    hidden_ref[...] = (silu * up).astype(BF)
    to_gate_ref[...] = up * sigma * (1.0 + gate * (1.0 - sigma))
    to_up_ref[...] = silu


def down_kernel(shape, place_ref, hidden_ref, cot_ref, *refs):
    slots = len(shape)
    down_in, refs = regroup(refs, shape)
    out_ref, d_hidden_ref, down_w, sems = refs
    part = down_w.shape[2]
    inner = place_ref[INNER]
    for j in range(slots):
        fetch(inner, down_in[j], down_w.at[j], sems.at[j])
    total = None
    for j in range(slots):
        rows = cot_ref[:, cols_of(place_ref, j, part)]
        arrived(down_in[j], down_w.at[j], sems.at[j])
        term = mm(rows, down_w[j], NT)
        total = term if total is None else total + term
        out_ref[:, j * part : (j + 1) * part] = mm(hidden_ref[...], down_w[j], NN).astype(BF)
    d_hidden_ref[...] = total


def grad_kernel(
    shape, place_ref, hidden_ref, cot_ref, d_hidden_ref, to_gate_ref, to_up_ref, *refs
):
    slots = len(shape)
    down_in, refs = regroup(refs, shape[-1:])
    gate_in, refs = regroup(refs, shape)
    up_in, refs = regroup(refs, shape)
    o_ref, down_w, gate_w, up_w, sems = refs
    part = down_w.shape[1]
    inner = place_ref[INNER]
    fetch(inner, down_in[0], down_w, sems.at[2, 0])
    for j in range(slots):
        fetch(inner, gate_in[j], gate_w.at[j], sems.at[0, j])
        fetch(inner, up_in[j], up_w.at[j], sems.at[1, j])
    rows = cot_ref[:, cols_of(place_ref, slots - 1, part)]
    arrived(down_in[0], down_w, sems.at[2, 0])
    d_hidden = d_hidden_ref[...] + mm(rows, down_w[...], NT)
    d_gate = (d_hidden * to_gate_ref[...]).astype(BF)
    d_up = (d_hidden * to_up_ref[...]).astype(BF)
    o_ref[:, slots * part :] = mm(hidden_ref[...], down_w[...], NN).astype(BF)
    for j in range(slots):
        arrived(gate_in[j], gate_w.at[j], sems.at[0, j])
        arrived(up_in[j], up_w.at[j], sems.at[1, j])
        o_ref[:, j * part : (j + 1) * part] = (
            mm(d_gate, gate_w[j], NN) + mm(d_up, up_w[j], NN)
        ).astype(BF)


def final_kernel(
    owners,
    cap,
    place_ref,
    ids_ref,
    w_ref,
    gain_ref,
    stream_ref,
    cot_ref,
    first_ref,
    last_ref,
    output_ref,
    grad_ref,
    d_normed_ref,
):
    tokens, width = stream_ref.shape
    done = first_ref.shape[1]
    part = width - done
    slots = width // part
    at0, at1 = slot_cols(ids_ref[...], owners, cap)
    rows = lax.broadcasted_iota(jnp.int32, (tokens, owners * cap), 1)
    pick0, pick1 = one_hot(rows == at0), one_hot(rows == at1)
    both = pick0 + pick1
    w0, w1 = w_ref[:, 0:1], w_ref[:, 1:2]
    square = jnp.zeros((tokens, 1), F32)
    dot = jnp.zeros((tokens, 1), F32)
    for j in range(slots):
        cols = cols_of(place_ref, j, part)
        if j < slots - 1:
            pairs = first_ref[:, j * part : (j + 1) * part]
        else:
            pairs = last_ref[:, width : width + part]
        stream = stream_ref[:, cols].astype(F32)
        mixed = w0 * mm(pick0, pairs, NN) + w1 * mm(pick1, pairs, NN)
        output_ref[:, cols] = (stream + mixed).astype(BF)
        gained = mm(both, last_ref[:, j * part : (j + 1) * part], NN) * gain_ref[:, cols]
        d_normed_ref[:, cols] = gained
        square = square + jnp.sum(stream * stream, axis=-1, keepdims=True)
        dot = dot + jnp.sum(gained * stream, axis=-1, keepdims=True)
    inv_rms = lax.rsqrt(square / width + 1e-05)
    mean = dot * inv_rms / width
    unit_rows = stream_ref[...].astype(F32) * inv_rms
    d_stream = inv_rms * (d_normed_ref[...] - unit_rows * mean)
    grad_ref[...] = (cot_ref[...].astype(F32) + d_stream).astype(BF)


def gather_line(shard, groups):
    if groups == 4:
        near = lax.ppermute(shard, "seq", [(0, 1), (1, 0), (2, 3), (3, 2)])
        across = lax.ppermute(shard, "seq", [(1, 2), (2, 1)])
        across_near = lax.ppermute(near, "seq", [(1, 2), (2, 1)])
        far = lax.ppermute(across, "seq", [(1, 0), (2, 3)])
        far_near = lax.ppermute(across_near, "seq", [(1, 0), (2, 3)])
        return [[shard], [near], [across, far], [across_near, far_near]]
    whole = lax.all_gather(shard, "seq", axis=0)
    return [[whole[j]] for j in range(groups)]


def places(groups):
    if groups == 4:
        own = lax.axis_index("seq")
        table = jnp.array(
            [
                [0, 0, 1, 2, 3, 0, 0, 0, 0, 0],
                [1, 1, 0, 2, 3, 1, 1, 0, 2, 3],
                [1, 2, 3, 1, 0, 2, 2, 3, 1, 0],
                [0, 3, 2, 1, 0, 3, 0, 0, 0, 0],
            ],
            jnp.int32,
        )
        return table[own]
    return jnp.arange(-1, groups, dtype=jnp.int32)


def exchange(rows, owners, axis):
    total, width = rows.shape
    rows = rows.reshape(owners, total // owners, width)
    rows = lax.all_to_all(rows, axis, split_axis=0, concat_axis=0, tiled=True)
    return rows.reshape(total, width)


def flat(slots):
    return [ref for choices in slots for ref in choices]


def per_device(
    queries,
    keys,
    values,
    resid,
    norm_gain,
    w_gate,
    w_up,
    w_down,
    expert_ids,
    route_weights,
    cotangent,
):
    groups = lax.axis_size("seq")
    owners = lax.axis_size("exp")
    tokens, width = queries.shape[1:]
    ffw = w_gate.shape[2]
    part = width // groups
    cap = max(2, tokens * 10 // (4 * owners))
    total = owners * cap
    ids = expert_ids[0]
    ids_t = ids.T
    weights = route_weights[0]
    gain = norm_gain[None]
    cot = cotangent[0]
    place = places(groups)

    gate_in = gather_line(w_gate[0].T, groups)
    up_in = gather_line(w_up[0].T, groups)
    down_in = gather_line(w_down[0], groups)
    shape = [len(choices) for choices in gate_in]
    if groups == 4:
        join = join_middle
        pieces = attend_middle(
            place, queries[0], keys[0], values[0], (gate_in[1][0], gate_in[2][0])
        )
        before_norm = (up_in[1][0], up_in[2][0], down_in[1][0], gate_in[3][0], gate_in[2][1])
    else:
        join = join_groups
        packed = pack(queries[0], keys[0], values[0], groups)
        heads = lax.all_to_all(packed, "seq", split_axis=0, concat_axis=0, tiled=True)
        ctx = attend(heads)
        pieces = (lax.all_to_all(ctx, "seq", split_axis=0, concat_axis=0, tiled=True),)
        before_norm = ()

    one = 2 * total * width * ffw
    send_cot = call(
        functools.partial(send_cot_kernel, owners, cap),
        sds((total, width)),
        (ids_t, weights, cot),
        [VMEM] * 3,
        flops=4 * total * tokens * width,
        moved=2 * (total + tokens) * width,
    )
    cot_rows = exchange(send_cot, owners, "exp")
    stream, send_rows = call(
        functools.partial(norm_kernel, owners, cap, join),
        (sds((tokens, width)), sds((total, width))),
        (place, ids_t, resid[0], gain, *pieces),
        [SMEM] + [VMEM] * (3 + len(pieces)),
        [pltpu.VMEM((tokens, width), BF)],
        flops=2 * total * tokens * width,
        moved=2 * (total + 3 * tokens) * width,
        after=before_norm,
    )
    rows = exchange(send_rows, owners, "exp")

    full_w = pltpu.VMEM((groups, ffw, part), BF)
    hidden, to_gate, to_up = call(
        functools.partial(up_kernel, shape),
        (sds((total, ffw)), sds((total, ffw), F32), sds((total, ffw), F32)),
        (place, rows, *flat(gate_in), *flat(up_in)),
        [SMEM, VMEM] + [HBM] * (2 * sum(shape)),
        [full_w, full_w, pltpu.SemaphoreType.DMA((2, groups))],
        flops=2 * one,
        moved=4 * width * ffw + 2 * total * width + 10 * total * ffw,
        vmem=20,
    )
    out_first, d_hidden = call(
        functools.partial(down_kernel, shape[:-1]),
        (sds((total, width - part)), sds((total, ffw), F32)),
        (place, hidden, cot_rows, *flat(down_in[:-1])),
        [SMEM, VMEM, VMEM] + [HBM] * sum(shape[:-1]),
        [
            pltpu.VMEM((groups - 1, ffw, part), BF),
            pltpu.SemaphoreType.DMA((groups - 1,)),
        ],
        flops=2 * one * (groups - 1) // groups,
        moved=2 * width * ffw + 4 * total * width + 6 * total * ffw,
    )
    back_first = exchange(out_first, owners, "exp")
    back = call(
        functools.partial(grad_kernel, shape),
        sds((total, width + part)),
        (
            place,
            hidden,
            cot_rows,
            d_hidden,
            to_gate,
            to_up,
            *flat(down_in[-1:]),
            *flat(gate_in),
            *flat(up_in),
        ),
        [SMEM] + [VMEM] * 5 + [HBM] * (shape[-1] + 2 * sum(shape)),
        [
            pltpu.VMEM((ffw, part), BF),
            full_w,
            full_w,
            pltpu.SemaphoreType.DMA((3, groups)),
        ],
        flops=2 * one + 2 * one // groups,
        moved=4 * width * ffw + 4 * total * width + 14 * total * ffw,
        vmem=22,
    )
    back_last = exchange(back, owners, "exp")
    output, stream_grad = call(
        functools.partial(final_kernel, owners, cap),
        (sds((tokens, width)), sds((tokens, width))),
        (place, ids, weights, gain, stream, cot, back_first, back_last),
        [SMEM] + [VMEM] * 7,
        [pltpu.VMEM((tokens, width), F32)],
        flops=6 * total * tokens * width,
        moved=4 * total * width + 8 * tokens * width,
    )
    return (output[None], stream_grad[None])


def solution(mesh):
    placed = (
        P("exp", "seq", None),
        P("exp", "seq", None),
        P("exp", "seq", None),
        P("exp", "seq", None),
        P(),
        P("exp", "seq", None),
        P("exp", "seq", None),
        P("exp", None, "seq"),
        P("exp", "seq", None),
        P("exp", "seq", None),
        P("exp", "seq", None),
    )
    return jax.shard_map(
        per_device,
        mesh=mesh,
        in_specs=placed,
        out_specs=(P("exp", "seq", None), P("exp", "seq", None)),
        check_vma=False,
    )
```

```python
import functools

import jax
import jax.numpy as jnp
from jax import lax
from jax.experimental import pallas as pl
from jax.experimental.pallas import tpu as pltpu
from jax.sharding import PartitionSpec as P

HD = 128
BF = jnp.bfloat16
F32 = jnp.float32
MIB = 1 << 20
HBM = pl.BlockSpec(memory_space=pltpu.HBM)
VMEM = pl.BlockSpec(memory_space=pltpu.VMEM)
SMEM = pl.BlockSpec(memory_space=pltpu.SMEM)
NT = (((1,), (1,)), ((), ()))
NN = (((1,), (0,)), ((), ()))


def mm(a, b, dims):
    return lax.dot_general(a, b, dims, preferred_element_type=F32)


def whole(array):
    return pl.BlockSpec(array.shape, lambda i: (0,) * len(array.shape))


def call(kernel, outs, args, in_specs, scratch=(), flops=0, moved=0, vmem=56, after=()):
    count, extra = len(args), len(after)

    def body(*refs):
        kernel(*refs[:count], *refs[count + extra :])

    return pl.pallas_call(
        body,
        grid=(1,),
        out_shape=outs,
        in_specs=[
            *[whole(arg) if spec is VMEM else spec for arg, spec in zip(args, in_specs)],
            *[HBM] * extra,
        ],
        out_specs=jax.tree.map(whole, outs),
        scratch_shapes=list(scratch),
        compiler_params=pltpu.CompilerParams(vmem_limit_bytes=vmem * MIB),
        cost_estimate=pl.CostEstimate(flops=flops, bytes_accessed=moved, transcendentals=0),
    )(*args, *after)


def gated(array, *first):
    return lax.optimization_barrier((array, *first))[0] if first else array


def sds(shape, dtype=BF):
    return jax.ShapeDtypeStruct(shape, dtype)


def pack_kernel(q_ref, k_ref, v_ref, o_ref):
    rows = q_ref.shape[0]
    o_ref[0, 0:rows] = q_ref[...]
    o_ref[0, rows : 2 * rows] = k_ref[...]
    o_ref[0, 2 * rows : 3 * rows] = v_ref[...]


def pack(q, k, v, groups):
    rows, width = q.shape
    part = width // groups
    spec = pl.BlockSpec((rows, part), lambda g: (0, g))
    return pl.pallas_call(
        pack_kernel,
        grid=(groups,),
        out_shape=sds((groups, 3 * rows, part)),
        in_specs=[spec] * 3,
        out_specs=pl.BlockSpec((1, 3 * rows, part), lambda g: (g, 0, 0)),
        cost_estimate=pl.CostEstimate(
            flops=0, bytes_accessed=12 * rows * width, transcendentals=0
        ),
    )(q, k, v)


def attend_head(blocks, query_of, keys, vals, store):
    rows = keys.shape[0] // blocks
    scale = HD ** (-0.5)
    row_ids = lax.broadcasted_iota(jnp.int32, (rows, rows), 0)
    col_ids = lax.broadcasted_iota(jnp.int32, (rows, rows), 1)
    keep = col_ids <= row_ids
    for b in range(blocks):
        query = query_of(b)
        end = b * rows
        diag = mm(query, keys[end : end + rows], NT) * scale
        diag = jnp.where(keep, diag, -jnp.inf)
        top = jnp.max(diag, axis=-1, keepdims=True)
        if b:
            early = mm(query, keys[:end], NT) * scale
            top = jnp.maximum(top, jnp.max(early, axis=-1, keepdims=True))
        diag = jnp.exp(diag - top)
        total = jnp.sum(diag, axis=-1, keepdims=True)
        if b:
            early = jnp.exp(early - top)
            total = total + jnp.sum(early, axis=-1, keepdims=True)
        inverse = 1.0 / total
        ctx = mm((diag * inverse).astype(BF), vals[end : end + rows], NN)
        if b:
            ctx = ctx + mm((early * inverse).astype(BF), vals[:end], NN)
        store(b, ctx.astype(BF))


def attend_kernel(x_ref, o_ref):
    blocks, three, hd = x_ref.shape
    rows = three // 3

    def store(b, ctx):
        o_ref[b] = ctx

    attend_head(
        blocks,
        lambda b: x_ref[b, 0:rows, :],
        x_ref[:, rows : 2 * rows, :].reshape(blocks * rows, hd),
        x_ref[:, 2 * rows : 3 * rows, :].reshape(blocks * rows, hd),
        store,
    )


def attend(x):
    blocks, three, part = x.shape
    rows = three // 3
    length = blocks * rows
    return pl.pallas_call(
        attend_kernel,
        grid=(part // HD,),
        out_shape=sds((blocks, rows, part)),
        in_specs=[pl.BlockSpec((blocks, three, HD), lambda h: (0, 0, h))],
        out_specs=pl.BlockSpec((blocks, rows, HD), lambda h: (0, 0, h)),
        compiler_params=pltpu.CompilerParams(vmem_limit_bytes=40 * MIB),
        cost_estimate=pl.CostEstimate(
            flops=4 * length * length * part,
            bytes_accessed=8 * length * part,
            transcendentals=length * length * part // HD,
        ),
    )(x)


INNER, COLS, PLANE, ATTEND = 0, 1, 5, 6


def halves_kernel(place_ref, q_ref, k_ref, v_ref, first_ref, second_ref):
    rows, width = q_ref.shape
    half = width // 2

    def copy(lower, upper):
        for i, ref in enumerate((q_ref, k_ref, v_ref)):
            lower[i * rows : (i + 1) * rows] = ref[:, :half]
            upper[i * rows : (i + 1) * rows] = ref[:, half:]

    @pl.when(place_ref[PLANE] < 2)
    def _():
        copy(first_ref, second_ref)

    @pl.when(place_ref[PLANE] >= 2)
    def _():
        copy(second_ref, first_ref)


def middle_kernel(place_ref, own_in, near_in, mid_in, far_in, *refs):
    *outs, x_ref, ctx_ref, sems = refs
    blocks, three, half = x_ref.shape
    rows = three // 3

    @pl.when(place_ref[INNER] == 1)
    def _():
        copies = [
            pltpu.make_async_copy(ref, x_ref.at[place_ref[ATTEND + i]], sems.at[i])
            for i, ref in enumerate((own_in, near_in, mid_in, far_in))
        ]
        for copy in copies:
            copy.start()
        for copy in copies:
            copy.wait()

        def step(i, carry):
            for j in range(2):
                cols = pl.ds(pl.multiple_of((2 * i + j) * HD, HD), HD)

                def store(b, ctx, cols=cols):
                    ctx_ref[b, :, cols] = ctx

                attend_head(
                    blocks,
                    lambda b, cols=cols: x_ref[b, 0:rows, cols],
                    x_ref[:, rows : 2 * rows, cols].reshape(blocks * rows, HD),
                    x_ref[:, 2 * rows : 3 * rows, cols].reshape(blocks * rows, HD),
                    store,
                )
            return carry

        lax.fori_loop(0, half // HD // 2, step, 0)
        for i, out in enumerate(outs):
            out[...] = ctx_ref[place_ref[ATTEND + i]]


def line_of_four(place, queries, keys, values, gate, up, down):
    rows, width = queries.shape
    half = width // 2
    block = sds((3 * rows, half))
    first, second = call(
        halves_kernel,
        (block, block),
        (place, queries, keys, values),
        [SMEM, VMEM, VMEM, VMEM],
        moved=12 * rows * width,
    )
    gate_end = send(gate, OUTWARD)
    up_end = send(up, OUTWARD)
    near = send(first, INWARD)
    mid = send(second, MIDDLE)
    far = send(second, [(0, 2), (3, 1)])
    piece = sds((rows, half))
    pieces = call(
        middle_kernel,
        (piece,) * 4,
        (place, first, near, mid, far),
        [SMEM] + [HBM] * 4,
        [
            pltpu.VMEM((4, 3 * rows, half), BF),
            pltpu.VMEM((4, rows, half), BF),
            pltpu.SemaphoreType.DMA((4,)),
        ],
        flops=64 * rows * rows * half,
        moved=32 * rows * half,
        after=(gate_end, up_end),
    )
    gate_inner = send(gate, INWARD, near, far)
    gate_mid = send(gate, MIDDLE, mid, far)
    down_end = send(down, OUTWARD, gate_end, up_end)
    own, near, mid, far = lax.optimization_barrier((*pieces, gate_mid, gate_inner, down_end))[:4]
    near = send(near, OUTWARD)
    mid = send(mid, MIDDLE)
    far = send(far, [(2, 0), (1, 3)])
    gate_mid_near = send(gate_inner, MIDDLE, gate_mid)
    gate_far = send(gate_mid, OUTWARD, down_end)
    up_mid = send(up, MIDDLE, gate_mid)
    up_inner = send(up, INWARD, gate_inner)
    norm_after = (gate_mid_near, gate_far, up_mid, up_inner)
    gate_far_near = send(gate_mid_near, OUTWARD, gate_far)
    up_far = send(up_mid, OUTWARD, gate_far)
    up_mid_near = send(up_inner, MIDDLE, gate_mid_near)
    down_mid = send(down, MIDDLE, up_mid)
    down_inner = send(down, INWARD, up_inner)
    up_far_near = send(up_mid_near, OUTWARD, gate_far_near)
    down_far = send(down_mid, OUTWARD, up_far)
    down_mid_near = send(down_inner, MIDDLE, down_mid)
    up_after = (down_mid_near,)
    down_far_near = send(down_mid_near, OUTWARD, up_far_near)
    gate_in = [
        [gate],
        [gate_inner, gate_end],
        [gate_mid, gate_far],
        [gate_mid_near, gate_far_near],
    ]
    up_in = [[up], [up_inner, up_end], [up_mid, up_far], [up_mid_near, up_far_near]]
    down_in = [
        [down],
        [down_inner, down_end],
        [down_mid, down_far],
        [down_mid_near, down_far_near],
    ]
    return (own, near, mid, far), gate_in, up_in, down_in, norm_after, up_after


def join_middle(place_ref, pieces, ctx_ref):
    own, near, mid, far = pieces
    half = own.shape[1]
    for plane, (lower, upper) in enumerate(((near, far), (own, mid), (mid, own), (far, near))):

        @pl.when(place_ref[PLANE] == plane)
        def _(lower=lower, upper=upper):
            ctx_ref[:, :half] = lower[...]
            ctx_ref[:, half:] = upper[...]


def join_groups(place_ref, pieces, ctx_ref):
    (ctx,) = pieces
    groups, _, part = ctx.shape
    for g in range(groups):
        ctx_ref[:, g * part : (g + 1) * part] = ctx[g]


def slot_rows(ids_t, owners, cap):
    tokens = ids_t.shape[1]
    experts = lax.broadcasted_iota(jnp.int32, (owners, tokens), 0)
    first = (experts == ids_t[0:1]).astype(F32)
    second = (experts == ids_t[1:2]).astype(F32)
    src = lax.broadcasted_iota(jnp.int32, (tokens, tokens), 0)
    dst = lax.broadcasted_iota(jnp.int32, (tokens, tokens), 1)
    earlier = (src < dst).astype(F32).astype(BF)
    count = mm((first + second).astype(BF), earlier, NN)
    slot0 = jnp.sum(first * count, axis=0, keepdims=True).astype(jnp.int32)
    slot1 = jnp.sum(second * count, axis=0, keepdims=True).astype(jnp.int32)
    return ids_t[0:1] * cap + slot0, ids_t[1:2] * cap + slot1


def slot_cols(ids, owners, cap):
    tokens = ids.shape[0]
    experts = lax.broadcasted_iota(jnp.int32, (tokens, owners), 1)
    first = (experts == ids[:, 0:1]).astype(F32)
    second = (experts == ids[:, 1:2]).astype(F32)
    dst = lax.broadcasted_iota(jnp.int32, (tokens, tokens), 0)
    src = lax.broadcasted_iota(jnp.int32, (tokens, tokens), 1)
    earlier = (src < dst).astype(F32).astype(BF)
    count = mm(earlier, (first + second).astype(BF), NN)
    slot0 = jnp.sum(first * count, axis=1, keepdims=True).astype(jnp.int32)
    slot1 = jnp.sum(second * count, axis=1, keepdims=True).astype(jnp.int32)
    return ids[:, 0:1] * cap + slot0, ids[:, 1:2] * cap + slot1


def one_hot(hit):
    return jnp.where(hit, 1.0, 0.0).astype(BF)


def send_cot_kernel(owners, cap, ids_ref, w_ref, cot_ref, o_ref):
    tokens = cot_ref.shape[0]
    at0, at1 = slot_rows(ids_ref[...], owners, cap)
    rows = lax.broadcasted_iota(jnp.int32, (owners * cap, tokens), 0)
    cot = cot_ref[...].astype(F32)
    o_ref[...] = (
        mm(one_hot(rows == at0), (w_ref[:, 0:1] * cot).astype(BF), NN)
        + mm(one_hot(rows == at1), (w_ref[:, 1:2] * cot).astype(BF), NN)
    ).astype(BF)


def norm_kernel(owners, cap, join, place_ref, ids_ref, resid_ref, gain_ref, *refs):
    *pieces, stream_ref, o_ref, ctx_ref = refs
    tokens, width = resid_ref.shape
    join(place_ref, pieces, ctx_ref)
    stream = (resid_ref[...].astype(F32) + ctx_ref[...].astype(F32)).astype(BF)
    stream_ref[...] = stream
    stream = stream.astype(F32)
    square = jnp.sum(stream * stream, axis=-1, keepdims=True)
    inv_rms = lax.rsqrt(square / width + 1e-05)
    at0, at1 = slot_rows(ids_ref[...], owners, cap)
    rows = lax.broadcasted_iota(jnp.int32, (owners * cap, tokens), 0)
    pick = one_hot((rows == at0) | (rows == at1))
    normed = ((stream_ref[...].astype(F32) * inv_rms) * gain_ref[...]).astype(BF)
    o_ref[...] = mm(pick, normed, NN).astype(BF)


def fetch(inner, choices, dst, sem):
    if len(choices) == 1:
        pltpu.make_async_copy(choices[0], dst, sem).start()
        return

    @pl.when(inner == 1)
    def _():
        pltpu.make_async_copy(choices[0], dst, sem).start()

    @pl.when(inner == 0)
    def _():
        pltpu.make_async_copy(choices[1], dst, sem).start()


def arrived(choices, dst, sem):
    pltpu.make_async_copy(choices[0], dst, sem).wait()


def regroup(refs, shape):
    refs = list(refs)
    return [[refs.pop(0) for _ in range(size)] for size in shape], refs


def cols_of(place_ref, slot, part):
    return pl.ds(pl.multiple_of(place_ref[COLS + slot] * part, part), part)


def up_kernel(shape, place_ref, x_ref, *refs):
    slots = len(shape)
    gate_in, refs = regroup(refs, shape)
    up_in, refs = regroup(refs, shape)
    hidden_ref, to_gate_ref, to_up_ref, gate_w, up_w, sems = refs
    part = gate_w.shape[2]
    inner = place_ref[INNER]
    for j in range(slots):
        fetch(inner, gate_in[j], gate_w.at[j], sems.at[0, j])
        fetch(inner, up_in[j], up_w.at[j], sems.at[1, j])
    gate = up = None
    for j in range(slots):
        rows = x_ref[:, cols_of(place_ref, j, part)]
        arrived(gate_in[j], gate_w.at[j], sems.at[0, j])
        term = mm(rows, gate_w[j], NT)
        gate = term if gate is None else gate + term
        arrived(up_in[j], up_w.at[j], sems.at[1, j])
        term = mm(rows, up_w[j], NT)
        up = term if up is None else up + term
    sigma = 1.0 / (1.0 + jnp.exp(-gate))
    silu = gate * sigma
    hidden_ref[...] = (silu * up).astype(BF)
    to_gate_ref[...] = up * sigma * (1.0 + gate * (1.0 - sigma))
    to_up_ref[...] = silu


def down_kernel(shape, place_ref, hidden_ref, cot_ref, *refs):
    slots = len(shape)
    down_in, refs = regroup(refs, shape)
    out_ref, d_hidden_ref, down_w, sems = refs
    part = down_w.shape[2]
    inner = place_ref[INNER]
    for j in range(slots):
        fetch(inner, down_in[j], down_w.at[j], sems.at[j])
    total = None
    for j in range(slots):
        rows = cot_ref[:, cols_of(place_ref, j, part)]
        arrived(down_in[j], down_w.at[j], sems.at[j])
        term = mm(rows, down_w[j], NT)
        total = term if total is None else total + term
        out_ref[:, j * part : (j + 1) * part] = mm(hidden_ref[...], down_w[j], NN).astype(BF)
    d_hidden_ref[...] = total


def grad_kernel(
    shape, place_ref, hidden_ref, cot_ref, d_hidden_ref, to_gate_ref, to_up_ref, *refs
):
    slots = len(shape)
    down_in, refs = regroup(refs, shape[-1:])
    gate_in, refs = regroup(refs, shape)
    up_in, refs = regroup(refs, shape)
    o_ref, down_w, gate_w, up_w, sems = refs
    part = down_w.shape[1]
    inner = place_ref[INNER]
    fetch(inner, down_in[0], down_w, sems.at[2, 0])
    for j in range(slots):
        fetch(inner, gate_in[j], gate_w.at[j], sems.at[0, j])
        fetch(inner, up_in[j], up_w.at[j], sems.at[1, j])
    rows = cot_ref[:, cols_of(place_ref, slots - 1, part)]
    arrived(down_in[0], down_w, sems.at[2, 0])
    d_hidden = d_hidden_ref[...] + mm(rows, down_w[...], NT)
    d_gate = (d_hidden * to_gate_ref[...]).astype(BF)
    d_up = (d_hidden * to_up_ref[...]).astype(BF)
    o_ref[:, slots * part :] = mm(hidden_ref[...], down_w[...], NN).astype(BF)
    for j in range(slots):
        arrived(gate_in[j], gate_w.at[j], sems.at[0, j])
        arrived(up_in[j], up_w.at[j], sems.at[1, j])
        o_ref[:, j * part : (j + 1) * part] = (
            mm(d_gate, gate_w[j], NN) + mm(d_up, up_w[j], NN)
        ).astype(BF)


def final_kernel(
    owners,
    cap,
    place_ref,
    ids_ref,
    w_ref,
    gain_ref,
    stream_ref,
    cot_ref,
    first_ref,
    last_ref,
    output_ref,
    grad_ref,
    d_normed_ref,
):
    tokens, width = stream_ref.shape
    done = first_ref.shape[1]
    part = width - done
    slots = width // part
    at0, at1 = slot_cols(ids_ref[...], owners, cap)
    rows = lax.broadcasted_iota(jnp.int32, (tokens, owners * cap), 1)
    pick0, pick1 = one_hot(rows == at0), one_hot(rows == at1)
    both = pick0 + pick1
    w0, w1 = w_ref[:, 0:1], w_ref[:, 1:2]
    square = jnp.zeros((tokens, 1), F32)
    dot = jnp.zeros((tokens, 1), F32)
    for j in range(slots):
        cols = cols_of(place_ref, j, part)
        if j < slots - 1:
            pairs = first_ref[:, j * part : (j + 1) * part]
        else:
            pairs = last_ref[:, width : width + part]
        stream = stream_ref[:, cols].astype(F32)
        mixed = w0 * mm(pick0, pairs, NN) + w1 * mm(pick1, pairs, NN)
        output_ref[:, cols] = (stream + mixed).astype(BF)
        gained = mm(both, last_ref[:, j * part : (j + 1) * part], NN) * gain_ref[:, cols]
        d_normed_ref[:, cols] = gained
        square = square + jnp.sum(stream * stream, axis=-1, keepdims=True)
        dot = dot + jnp.sum(gained * stream, axis=-1, keepdims=True)
    inv_rms = lax.rsqrt(square / width + 1e-05)
    mean = dot * inv_rms / width
    unit_rows = stream_ref[...].astype(F32) * inv_rms
    d_stream = inv_rms * (d_normed_ref[...] - unit_rows * mean)
    grad_ref[...] = (cot_ref[...].astype(F32) + d_stream).astype(BF)


MIDDLE = [(1, 2), (2, 1)]
OUTWARD = [(1, 0), (2, 3)]
INWARD = [(0, 1), (3, 2)]


def gather_all(shard, groups):
    whole_weight = lax.all_gather(shard, "seq", axis=0)
    return [[whole_weight[j]] for j in range(groups)]


def send(array, pairs, *first):
    return lax.ppermute(gated(array, *first), "seq", pairs)


def places(groups):
    if groups == 4:
        own = lax.axis_index("seq")
        table = jnp.array(
            [
                [0, 0, 1, 2, 3, 0, 0, 0, 0, 0],
                [1, 1, 0, 2, 3, 1, 1, 0, 2, 3],
                [1, 2, 3, 1, 0, 2, 2, 3, 1, 0],
                [0, 3, 2, 1, 0, 3, 0, 0, 0, 0],
            ],
            jnp.int32,
        )
        return table[own]
    return jnp.arange(-1, groups, dtype=jnp.int32)


def exchange(rows, owners, axis):
    total, width = rows.shape
    rows = rows.reshape(owners, total // owners, width)
    rows = lax.all_to_all(rows, axis, split_axis=0, concat_axis=0, tiled=True)
    return rows.reshape(total, width)


def flat(slots):
    return [ref for choices in slots for ref in choices]


def per_device(
    queries,
    keys,
    values,
    resid,
    norm_gain,
    w_gate,
    w_up,
    w_down,
    expert_ids,
    route_weights,
    cotangent,
):
    groups = lax.axis_size("seq")
    owners = lax.axis_size("exp")
    tokens, width = queries.shape[1:]
    ffw = w_gate.shape[2]
    part = width // groups
    cap = max(2, tokens * 10 // (4 * owners))
    total = owners * cap
    ids = expert_ids[0]
    ids_t = ids.T
    weights = route_weights[0]
    gain = norm_gain[None]
    cot = cotangent[0]
    place = places(groups)

    shards = (w_gate[0].T, w_up[0].T, w_down[0])
    if groups == 4:
        join = join_middle
        pieces, gate_in, up_in, down_in, norm_after, up_after = line_of_four(
            place, queries[0], keys[0], values[0], *shards
        )
    else:
        join = join_groups
        gate_in, up_in, down_in = [gather_all(shard, groups) for shard in shards]
        packed = pack(queries[0], keys[0], values[0], groups)
        heads = lax.all_to_all(packed, "seq", split_axis=0, concat_axis=0, tiled=True)
        ctx = attend(heads)
        pieces = (lax.all_to_all(ctx, "seq", split_axis=0, concat_axis=0, tiled=True),)
        norm_after = up_after = ()
    shape = [len(choices) for choices in gate_in]

    one = 2 * total * width * ffw
    send_cot = call(
        functools.partial(send_cot_kernel, owners, cap),
        sds((total, width)),
        (ids_t, weights, cot),
        [VMEM] * 3,
        flops=4 * total * tokens * width,
        moved=2 * (total + tokens) * width,
    )
    cot_rows = exchange(send_cot, owners, "exp")
    stream, send_rows = call(
        functools.partial(norm_kernel, owners, cap, join),
        (sds((tokens, width)), sds((total, width))),
        (place, ids_t, resid[0], gain, *pieces),
        [SMEM] + [VMEM] * (3 + len(pieces)),
        [pltpu.VMEM((tokens, width), BF)],
        flops=2 * total * tokens * width,
        moved=2 * (total + 3 * tokens) * width,
        after=norm_after,
    )
    rows = exchange(send_rows, owners, "exp")

    full_w = pltpu.VMEM((groups, ffw, part), BF)
    hidden, to_gate, to_up = call(
        functools.partial(up_kernel, shape),
        (sds((total, ffw)), sds((total, ffw), F32), sds((total, ffw), F32)),
        (place, rows, *flat(gate_in), *flat(up_in)),
        [SMEM, VMEM] + [HBM] * (2 * sum(shape)),
        [full_w, full_w, pltpu.SemaphoreType.DMA((2, groups))],
        flops=2 * one,
        moved=4 * width * ffw + 2 * total * width + 10 * total * ffw,
        after=up_after,

    )
    out_first, d_hidden = call(
        functools.partial(down_kernel, shape[:-1]),
        (sds((total, width - part)), sds((total, ffw), F32)),
        (place, hidden, cot_rows, *flat(down_in[:-1])),
        [SMEM, VMEM, VMEM] + [HBM] * sum(shape[:-1]),
        [
            pltpu.VMEM((groups - 1, ffw, part), BF),
            pltpu.SemaphoreType.DMA((groups - 1,)),
        ],
        flops=2 * one * (groups - 1) // groups,
        moved=2 * width * ffw + 4 * total * width + 6 * total * ffw,
    )
    back_first = exchange(out_first, owners, "exp")
    back = call(
        functools.partial(grad_kernel, shape),
        sds((total, width + part)),
        (
            place,
            hidden,
            cot_rows,
            d_hidden,
            to_gate,
            to_up,
            *flat(down_in[-1:]),
            *flat(gate_in),
            *flat(up_in),
        ),
        [SMEM] + [VMEM] * 5 + [HBM] * (shape[-1] + 2 * sum(shape)),
        [
            pltpu.VMEM((ffw, part), BF),
            full_w,
            full_w,
            pltpu.SemaphoreType.DMA((3, groups)),
        ],
        flops=2 * one + 2 * one // groups,
        moved=4 * width * ffw + 4 * total * width + 14 * total * ffw,

    )
    back_last = exchange(back, owners, "exp")
    output, stream_grad = call(
        functools.partial(final_kernel, owners, cap),
        (sds((tokens, width)), sds((tokens, width))),
        (place, ids, weights, gain, stream, cot, back_first, back_last),
        [SMEM] + [VMEM] * 7,
        [pltpu.VMEM((tokens, width), F32)],
        flops=6 * total * tokens * width,
        moved=4 * total * width + 8 * tokens * width,
    )
    return (output[None], stream_grad[None])


def solution(mesh):
    placed = (
        P("exp", "seq", None),
        P("exp", "seq", None),
        P("exp", "seq", None),
        P("exp", "seq", None),
        P(),
        P("exp", "seq", None),
        P("exp", "seq", None),
        P("exp", None, "seq"),
        P("exp", "seq", None),
        P("exp", "seq", None),
        P("exp", "seq", None),
    )
    return jax.shard_map(
        per_device,
        mesh=mesh,
        in_specs=placed,
        out_specs=(P("exp", "seq", None), P("exp", "seq", None)),
        check_vma=False,
    )
```

```python
import functools

import jax
import jax.numpy as jnp
from jax import lax
from jax.experimental import pallas as pl
from jax.experimental.pallas import tpu as pltpu
from jax.sharding import PartitionSpec as P

HD = 128
BF = jnp.bfloat16
F32 = jnp.float32
MIB = 1 << 20
HBM = pl.BlockSpec(memory_space=pltpu.HBM)
VMEM = pl.BlockSpec(memory_space=pltpu.VMEM)
SMEM = pl.BlockSpec(memory_space=pltpu.SMEM)
NT = (((1,), (1,)), ((), ()))
NN = (((1,), (0,)), ((), ()))


def mm(a, b, dims):
    return lax.dot_general(a, b, dims, preferred_element_type=F32)


def whole(array):
    return pl.BlockSpec(array.shape, lambda i: (0,) * len(array.shape))


def call(kernel, outs, args, in_specs, scratch=(), flops=0, moved=0, vmem=56, after=(), held=False):
    count, extra = len(args), len(after)

    def body(*refs):
        kernel(*refs[:count], *refs[count + extra :])

    return pl.pallas_call(
        body,
        grid=() if held else (1,),
        out_shape=outs,
        in_specs=[
            *[
                whole(arg) if spec is VMEM and not held else spec
                for arg, spec in zip(args, in_specs)
            ],
            *[HBM] * extra,
        ],
        out_specs=jax.tree.map(lambda out: VMEM if held else whole(out), outs),
        scratch_shapes=list(scratch),
        compiler_params=pltpu.CompilerParams(vmem_limit_bytes=vmem * MIB),
        cost_estimate=pl.CostEstimate(flops=flops, bytes_accessed=moved, transcendentals=0),
    )(*args, *after)


def gated(array, *first):
    return lax.optimization_barrier((array, *first))[0] if first else array


def sds(shape, dtype=BF):
    return jax.ShapeDtypeStruct(shape, dtype)


def pack_kernel(q_ref, k_ref, v_ref, o_ref):
    rows = q_ref.shape[0]
    o_ref[0, 0:rows] = q_ref[...]
    o_ref[0, rows : 2 * rows] = k_ref[...]
    o_ref[0, 2 * rows : 3 * rows] = v_ref[...]


def pack(q, k, v, groups):
    rows, width = q.shape
    part = width // groups
    spec = pl.BlockSpec((rows, part), lambda g: (0, g))
    return pl.pallas_call(
        pack_kernel,
        grid=(groups,),
        out_shape=sds((groups, 3 * rows, part)),
        in_specs=[spec] * 3,
        out_specs=pl.BlockSpec((1, 3 * rows, part), lambda g: (g, 0, 0)),
        cost_estimate=pl.CostEstimate(
            flops=0, bytes_accessed=12 * rows * width, transcendentals=0
        ),
    )(q, k, v)


def attend_head(blocks, query_of, keys, vals, store):
    rows = keys.shape[0] // blocks
    scale = HD ** (-0.5)
    row_ids = lax.broadcasted_iota(jnp.int32, (rows, rows), 0)
    col_ids = lax.broadcasted_iota(jnp.int32, (rows, rows), 1)
    keep = col_ids <= row_ids
    for b in range(blocks):
        query = query_of(b)
        end = b * rows
        diag = mm(query, keys[end : end + rows], NT) * scale
        diag = jnp.where(keep, diag, -jnp.inf)
        top = jnp.max(diag, axis=-1, keepdims=True)
        if b:
            early = mm(query, keys[:end], NT) * scale
            top = jnp.maximum(top, jnp.max(early, axis=-1, keepdims=True))
        diag = jnp.exp(diag - top)
        total = jnp.sum(diag, axis=-1, keepdims=True)
        if b:
            early = jnp.exp(early - top)
            total = total + jnp.sum(early, axis=-1, keepdims=True)
        inverse = 1.0 / total
        ctx = mm((diag * inverse).astype(BF), vals[end : end + rows], NN)
        if b:
            ctx = ctx + mm((early * inverse).astype(BF), vals[:end], NN)
        store(b, ctx.astype(BF))


def attend_kernel(x_ref, o_ref):
    blocks, three, hd = x_ref.shape
    rows = three // 3

    def store(b, ctx):
        o_ref[b] = ctx

    attend_head(
        blocks,
        lambda b: x_ref[b, 0:rows, :],
        x_ref[:, rows : 2 * rows, :].reshape(blocks * rows, hd),
        x_ref[:, 2 * rows : 3 * rows, :].reshape(blocks * rows, hd),
        store,
    )


def attend(x):
    blocks, three, part = x.shape
    rows = three // 3
    length = blocks * rows
    return pl.pallas_call(
        attend_kernel,
        grid=(part // HD,),
        out_shape=sds((blocks, rows, part)),
        in_specs=[pl.BlockSpec((blocks, three, HD), lambda h: (0, 0, h))],
        out_specs=pl.BlockSpec((blocks, rows, HD), lambda h: (0, 0, h)),
        compiler_params=pltpu.CompilerParams(vmem_limit_bytes=40 * MIB),
        cost_estimate=pl.CostEstimate(
            flops=4 * length * length * part,
            bytes_accessed=8 * length * part,
            transcendentals=length * length * part // HD,
        ),
    )(x)


INNER, COLS, PLANE, ATTEND = 0, 1, 5, 6


def halves_kernel(place_ref, q_ref, k_ref, v_ref, first_ref, second_ref):
    rows, width = q_ref.shape
    half = width // 2

    def copy(lower, upper):
        for i, ref in enumerate((q_ref, k_ref, v_ref)):
            lower[i * rows : (i + 1) * rows] = ref[:, :half]
            upper[i * rows : (i + 1) * rows] = ref[:, half:]

    @pl.when(place_ref[PLANE] < 2)
    def _():
        copy(first_ref, second_ref)

    @pl.when(place_ref[PLANE] >= 2)
    def _():
        copy(second_ref, first_ref)


def middle_kernel(place_ref, own_in, near_in, mid_in, far_in, *refs):
    *outs, x_ref, ctx_ref, sems = refs
    blocks, three, half = x_ref.shape
    rows = three // 3

    @pl.when(place_ref[INNER] == 1)
    def _():
        copies = [
            pltpu.make_async_copy(ref, x_ref.at[place_ref[ATTEND + i]], sems.at[i])
            for i, ref in enumerate((own_in, near_in, mid_in, far_in))
        ]
        for copy in copies:
            copy.start()
        for copy in copies:
            copy.wait()

        def step(i, carry):
            for j in range(2):
                cols = pl.ds(pl.multiple_of((2 * i + j) * HD, HD), HD)

                def store(b, ctx, cols=cols):
                    ctx_ref[b, :, cols] = ctx

                attend_head(
                    blocks,
                    lambda b, cols=cols: x_ref[b, 0:rows, cols],
                    x_ref[:, rows : 2 * rows, cols].reshape(blocks * rows, HD),
                    x_ref[:, 2 * rows : 3 * rows, cols].reshape(blocks * rows, HD),
                    store,
                )
            return carry

        lax.fori_loop(0, half // HD // 2, step, 0)
        for i, out in enumerate(outs):
            out[...] = ctx_ref[place_ref[ATTEND + i]]


def line_of_four(place, queries, keys, values, gate, up, down, send_cot):
    rows, width = queries.shape
    half = width // 2
    block = sds((3 * rows, half))
    first, second = call(
        halves_kernel,
        (block, block),
        (place, queries, keys, values),
        [SMEM, VMEM, VMEM, VMEM],
        moved=12 * rows * width,
    )
    gate_end = send(gate, OUTWARD)
    up_end = send(up, OUTWARD)
    near = send(first, INWARD)
    mid = send(second, MIDDLE)
    far = send(second, [(0, 2), (3, 1)])
    piece = sds((rows, half))
    pieces = call(
        middle_kernel,
        (piece,) * 4,
        (place, first, near, mid, far),
        [SMEM] + [HBM] * 4,
        [
            pltpu.VMEM((4, 3 * rows, half), BF),
            pltpu.VMEM((4, rows, half), BF),
            pltpu.SemaphoreType.DMA((4,)),
        ],
        flops=64 * rows * rows * half,
        moved=32 * rows * half,
        after=(gate_end, up_end, send_cot),
    )
    gate_inner = send(gate, INWARD, near, far)
    gate_mid = send(gate, MIDDLE, near, mid, far)
    down_end = send(down, OUTWARD)
    own, near, mid, far = lax.optimization_barrier((*pieces, gate_mid, gate_inner, down_end))[:4]
    near = send(near, OUTWARD)
    mid = send(mid, MIDDLE)
    far = send(far, [(2, 0), (1, 3)])
    gate_mid_near = send(gate_inner, MIDDLE, mid, far)
    gate_far = send(gate_mid, OUTWARD, down_end)
    up_mid = send(up, MIDDLE, gate_mid)
    up_inner = send(up, INWARD, gate_inner)
    norm_after = (gate_far, up_mid)
    gate_far_near = send(gate_mid_near, OUTWARD)
    up_far = send(up_mid, OUTWARD)
    up_mid_near = send(up_inner, MIDDLE, up_mid)
    down_mid = send(down, MIDDLE, gate_mid_near)
    down_inner = send(down, INWARD, up_inner)
    up_far_near = send(up_mid_near, OUTWARD, up_far)
    down_far = send(down_mid, OUTWARD, gate_far_near)
    down_mid_near = send(down_inner, MIDDLE, up_mid_near)
    up_after = (down_mid_near,)
    down_far_near = send(down_mid_near, OUTWARD, up_far_near)
    gate_in = [
        [gate],
        [gate_inner, gate_end],
        [gate_mid, gate_far],
        [gate_mid_near, gate_far_near],
    ]
    up_in = [[up], [up_inner, up_end], [up_mid, up_far], [up_mid_near, up_far_near]]
    down_in = [
        [down],
        [down_inner, down_end],
        [down_mid, down_far],
        [down_mid_near, down_far_near],
    ]
    return (own, near, mid, far), gate_in, up_in, down_in, norm_after, up_after


def join_middle(place_ref, pieces, ctx_ref):
    own, near, mid, far = pieces
    half = own.shape[1]
    for plane, (lower, upper) in enumerate(((near, far), (own, mid), (mid, own), (far, near))):

        @pl.when(place_ref[PLANE] == plane)
        def _(lower=lower, upper=upper):
            ctx_ref[:, :half] = lower[...]
            ctx_ref[:, half:] = upper[...]


def join_groups(place_ref, pieces, ctx_ref):
    (ctx,) = pieces
    groups, _, part = ctx.shape
    for g in range(groups):
        ctx_ref[:, g * part : (g + 1) * part] = ctx[g]


def slot_rows(ids_t, owners, cap):
    tokens = ids_t.shape[1]
    experts = lax.broadcasted_iota(jnp.int32, (owners, tokens), 0)
    first = (experts == ids_t[0:1]).astype(F32)
    second = (experts == ids_t[1:2]).astype(F32)
    src = lax.broadcasted_iota(jnp.int32, (tokens, tokens), 0)
    dst = lax.broadcasted_iota(jnp.int32, (tokens, tokens), 1)
    earlier = (src < dst).astype(F32).astype(BF)
    count = mm((first + second).astype(BF), earlier, NN)
    slot0 = jnp.sum(first * count, axis=0, keepdims=True).astype(jnp.int32)
    slot1 = jnp.sum(second * count, axis=0, keepdims=True).astype(jnp.int32)
    return ids_t[0:1] * cap + slot0, ids_t[1:2] * cap + slot1


def slot_cols(ids, owners, cap):
    tokens = ids.shape[0]
    experts = lax.broadcasted_iota(jnp.int32, (tokens, owners), 1)
    first = (experts == ids[:, 0:1]).astype(F32)
    second = (experts == ids[:, 1:2]).astype(F32)
    dst = lax.broadcasted_iota(jnp.int32, (tokens, tokens), 0)
    src = lax.broadcasted_iota(jnp.int32, (tokens, tokens), 1)
    earlier = (src < dst).astype(F32).astype(BF)
    count = mm(earlier, (first + second).astype(BF), NN)
    slot0 = jnp.sum(first * count, axis=1, keepdims=True).astype(jnp.int32)
    slot1 = jnp.sum(second * count, axis=1, keepdims=True).astype(jnp.int32)
    return ids[:, 0:1] * cap + slot0, ids[:, 1:2] * cap + slot1


def one_hot(hit):
    return jnp.where(hit, 1.0, 0.0).astype(BF)


def send_cot_kernel(owners, cap, ids_ref, w_ref, cot_ref, o_ref):
    tokens = cot_ref.shape[0]
    at0, at1 = slot_rows(ids_ref[...], owners, cap)
    rows = lax.broadcasted_iota(jnp.int32, (owners * cap, tokens), 0)
    cot = cot_ref[...].astype(F32)
    o_ref[...] = (
        mm(one_hot(rows == at0), (w_ref[:, 0:1] * cot).astype(BF), NN)
        + mm(one_hot(rows == at1), (w_ref[:, 1:2] * cot).astype(BF), NN)
    ).astype(BF)


def norm_kernel(owners, cap, join, place_ref, ids_ref, resid_ref, gain_ref, *refs):
    *pieces, stream_ref, o_ref, ctx_ref = refs
    tokens, width = resid_ref.shape
    join(place_ref, pieces, ctx_ref)
    stream = (resid_ref[...].astype(F32) + ctx_ref[...].astype(F32)).astype(BF)
    stream_ref[...] = stream
    stream = stream.astype(F32)
    square = jnp.sum(stream * stream, axis=-1, keepdims=True)
    inv_rms = lax.rsqrt(square / width + 1e-05)
    at0, at1 = slot_rows(ids_ref[...], owners, cap)
    rows = lax.broadcasted_iota(jnp.int32, (owners * cap, tokens), 0)
    pick = one_hot((rows == at0) | (rows == at1))
    normed = ((stream_ref[...].astype(F32) * inv_rms) * gain_ref[...]).astype(BF)
    o_ref[...] = mm(pick, normed, NN).astype(BF)


def fetch(inner, choices, dst, sem):
    if len(choices) == 1:
        pltpu.make_async_copy(choices[0], dst, sem).start()
        return

    @pl.when(inner == 1)
    def _():
        pltpu.make_async_copy(choices[0], dst, sem).start()

    @pl.when(inner == 0)
    def _():
        pltpu.make_async_copy(choices[1], dst, sem).start()


def arrived(choices, dst, sem):
    pltpu.make_async_copy(choices[0], dst, sem).wait()


def regroup(refs, shape):
    refs = list(refs)
    return [[refs.pop(0) for _ in range(size)] for size in shape], refs


def cols_of(place_ref, slot, part):
    return pl.ds(pl.multiple_of(place_ref[COLS + slot] * part, part), part)


def up_kernel(shape, place_ref, x_ref, *refs):
    slots = len(shape)
    gate_in, refs = regroup(refs, shape)
    up_in, refs = regroup(refs, shape)
    hidden_ref, to_gate_ref, to_up_ref, gate_w, up_w, sems = refs
    part = gate_w.shape[2]
    inner = place_ref[INNER]
    for j in range(slots):
        fetch(inner, gate_in[j], gate_w.at[j], sems.at[0, j])
        fetch(inner, up_in[j], up_w.at[j], sems.at[1, j])
    gate = up = None
    for j in range(slots):
        rows = x_ref[:, cols_of(place_ref, j, part)]
        arrived(gate_in[j], gate_w.at[j], sems.at[0, j])
        term = mm(rows, gate_w[j], NT)
        gate = term if gate is None else gate + term
        arrived(up_in[j], up_w.at[j], sems.at[1, j])
        term = mm(rows, up_w[j], NT)
        up = term if up is None else up + term
    sigma = 1.0 / (1.0 + jnp.exp(-gate))
    silu = gate * sigma
    hidden_ref[...] = (silu * up).astype(BF)
    to_gate_ref[...] = up * sigma * (1.0 + gate * (1.0 - sigma))
    to_up_ref[...] = silu


def down_kernel(shape, place_ref, hidden_ref, cot_ref, *refs):
    slots = len(shape)
    down_in, refs = regroup(refs, shape)
    out_ref, d_hidden_ref, down_w, sems = refs
    part = down_w.shape[2]
    inner = place_ref[INNER]
    for j in range(slots):
        fetch(inner, down_in[j], down_w.at[j], sems.at[j])
    total = None
    for j in range(slots):
        rows = cot_ref[:, cols_of(place_ref, j, part)]
        arrived(down_in[j], down_w.at[j], sems.at[j])
        term = mm(rows, down_w[j], NT)
        total = term if total is None else total + term
        out_ref[:, j * part : (j + 1) * part] = mm(hidden_ref[...], down_w[j], NN).astype(BF)
    d_hidden_ref[...] = total


def grad_kernel(
    shape, place_ref, hidden_in, cot_in, d_hidden_in, to_gate_in, to_up_in, *refs
):
    slots = len(shape) - 1
    down_in, refs = regroup(refs, shape[-1:])
    gate_in, refs = regroup(refs, shape[:-1])
    up_in, refs = regroup(refs, shape[:-1])
    (o_ref, d_gate_ref, d_up_ref, down_w, gate_w, up_w, sems) = refs[:7]
    hidden_ref, cot_ref, d_hidden_ref, to_gate_ref, to_up_ref = refs[7:]
    part = down_w.shape[1]
    inner = place_ref[INNER]
    last = place_ref[COLS + cot_in.shape[1] // part - 1]
    pairs = [
        (cot_in.at[:, pl.ds(pl.multiple_of(last * part, part), part)], cot_ref),
        (d_hidden_in, d_hidden_ref),
        (to_gate_in, to_gate_ref),
        (to_up_in, to_up_ref),
        (hidden_in, hidden_ref),
    ]
    fetch(inner, down_in[0], down_w, sems.at[2, 0])
    copies = [
        pltpu.make_async_copy(src, dst, sems.at[3 + i, 0]) for i, (src, dst) in enumerate(pairs)
    ]
    for copy in copies:
        copy.start()
    for j in range(slots):
        fetch(inner, gate_in[j], gate_w.at[j], sems.at[0, j])
        fetch(inner, up_in[j], up_w.at[j], sems.at[1, j])
    arrived(down_in[0], down_w, sems.at[2, 0])
    for copy in copies:
        copy.wait()
    d_hidden = d_hidden_ref[...] + mm(cot_ref[...], down_w[...], NT)
    d_gate = (d_hidden * to_gate_ref[...]).astype(BF)
    d_up = (d_hidden * to_up_ref[...]).astype(BF)
    d_gate_ref[...] = d_gate
    d_up_ref[...] = d_up
    o_ref[:, slots * part :] = mm(hidden_ref[...], down_w[...], NN).astype(BF)
    for j in range(slots):
        arrived(gate_in[j], gate_w.at[j], sems.at[0, j])
        arrived(up_in[j], up_w.at[j], sems.at[1, j])
        o_ref[:, j * part : (j + 1) * part] = (
            mm(d_gate, gate_w[j], NN) + mm(d_up, up_w[j], NN)
        ).astype(BF)


def rest_kernel(shape, place_ref, d_gate_ref, d_up_ref, *refs):
    slots = len(shape)
    gate_in, refs = regroup(refs, shape)
    up_in, refs = regroup(refs, shape)
    o_ref, gate_w, up_w, sems = refs
    part = gate_w.shape[2]
    inner = place_ref[INNER]
    for j in range(slots):
        fetch(inner, gate_in[j], gate_w.at[j], sems.at[0, j])
        fetch(inner, up_in[j], up_w.at[j], sems.at[1, j])
    for j in range(slots):
        arrived(gate_in[j], gate_w.at[j], sems.at[0, j])
        arrived(up_in[j], up_w.at[j], sems.at[1, j])
        o_ref[:, j * part : (j + 1) * part] = (
            mm(d_gate_ref[...], gate_w[j], NN) + mm(d_up_ref[...], up_w[j], NN)
        ).astype(BF)


def final_kernel(
    owners,
    cap,
    place_ref,
    ids_ref,
    w_ref,
    gain_ref,
    stream_ref,
    cot_ref,
    first_ref,
    early_ref,
    late_ref,
    output_ref,
    grad_ref,
    d_normed_ref,
):
    tokens, width = stream_ref.shape
    done = first_ref.shape[1]
    part = width - done
    slots = width // part
    at0, at1 = slot_cols(ids_ref[...], owners, cap)
    rows = lax.broadcasted_iota(jnp.int32, (tokens, owners * cap), 1)
    pick0, pick1 = one_hot(rows == at0), one_hot(rows == at1)
    both = pick0 + pick1
    w0, w1 = w_ref[:, 0:1], w_ref[:, 1:2]
    square = jnp.zeros((tokens, 1), F32)
    dot = jnp.zeros((tokens, 1), F32)
    for j in range(slots):
        cols = cols_of(place_ref, j, part)
        if j < slots - 1:
            pairs = first_ref[:, j * part : (j + 1) * part]
        else:
            pairs = early_ref[:, slots // 2 * part :]
        stream = stream_ref[:, cols].astype(F32)
        mixed = w0 * mm(pick0, pairs, NN) + w1 * mm(pick1, pairs, NN)
        output_ref[:, cols] = (stream + mixed).astype(BF)
        if j < slots // 2:
            grads = early_ref[:, j * part : (j + 1) * part]
        else:
            grads = late_ref[:, (j - slots // 2) * part : (j - slots // 2 + 1) * part]
        gained = mm(both, grads, NN) * gain_ref[:, cols]
        d_normed_ref[:, cols] = gained
        square = square + jnp.sum(stream * stream, axis=-1, keepdims=True)
        dot = dot + jnp.sum(gained * stream, axis=-1, keepdims=True)
    inv_rms = lax.rsqrt(square / width + 1e-05)
    mean = dot * inv_rms / width
    unit_rows = stream_ref[...].astype(F32) * inv_rms
    d_stream = inv_rms * (d_normed_ref[...] - unit_rows * mean)
    grad_ref[...] = (cot_ref[...].astype(F32) + d_stream).astype(BF)


MIDDLE = [(1, 2), (2, 1)]
OUTWARD = [(1, 0), (2, 3)]
INWARD = [(0, 1), (3, 2)]


def gather_all(shard, groups):
    whole_weight = lax.all_gather(shard, "seq", axis=0)
    return [[whole_weight[j]] for j in range(groups)]


def send(array, pairs, *first):
    return lax.ppermute(gated(array, *first), "seq", pairs)


def places(groups):
    if groups == 4:
        own = lax.axis_index("seq")
        table = jnp.array(
            [
                [0, 0, 1, 2, 3, 0, 0, 0, 0, 0],
                [1, 1, 0, 2, 3, 1, 1, 0, 2, 3],
                [1, 2, 3, 1, 0, 2, 2, 3, 1, 0],
                [0, 3, 2, 1, 0, 3, 0, 0, 0, 0],
            ],
            jnp.int32,
        )
        return table[own]
    return jnp.arange(-1, groups, dtype=jnp.int32)


def exchange(rows, owners, axis):
    total, width = rows.shape
    rows = rows.reshape(owners, total // owners, width)
    rows = lax.all_to_all(rows, axis, split_axis=0, concat_axis=0, tiled=True)
    return rows.reshape(total, width)


def flat(slots):
    return [ref for choices in slots for ref in choices]


def per_device(
    queries,
    keys,
    values,
    resid,
    norm_gain,
    w_gate,
    w_up,
    w_down,
    expert_ids,
    route_weights,
    cotangent,
):
    groups = lax.axis_size("seq")
    owners = lax.axis_size("exp")
    tokens, width = queries.shape[1:]
    ffw = w_gate.shape[2]
    part = width // groups
    cap = max(2, tokens * 10 // (4 * owners))
    total = owners * cap
    ids = expert_ids[0]
    ids_t = ids.T
    weights = route_weights[0]
    gain = norm_gain[None]
    cot = cotangent[0]
    place = places(groups)

    one = 2 * total * width * ffw
    send_cot = call(
        functools.partial(send_cot_kernel, owners, cap),
        sds((total, width)),
        (ids_t, weights, cot),
        [VMEM] * 3,
        flops=4 * total * tokens * width,
        moved=2 * (total + tokens) * width,
    )
    cot_rows = exchange(send_cot, owners, "exp")
    shards = (w_gate[0].T, w_up[0].T, w_down[0])
    if groups == 4:
        join = join_middle
        pieces, gate_in, up_in, down_in, norm_after, up_after = line_of_four(
            place, queries[0], keys[0], values[0], *shards, send_cot
        )
    else:
        join = join_groups
        gate_in, up_in, down_in = [gather_all(shard, groups) for shard in shards]
        packed = pack(queries[0], keys[0], values[0], groups)
        heads = lax.all_to_all(packed, "seq", split_axis=0, concat_axis=0, tiled=True)
        ctx = attend(heads)
        pieces = (lax.all_to_all(ctx, "seq", split_axis=0, concat_axis=0, tiled=True),)
        norm_after = up_after = ()
    shape = [len(choices) for choices in gate_in]

    stream, send_rows = call(
        functools.partial(norm_kernel, owners, cap, join),
        (sds((tokens, width)), sds((total, width))),
        (place, ids_t, resid[0], gain, *pieces),
        [SMEM] + [VMEM] * (3 + len(pieces)),
        [pltpu.VMEM((tokens, width), BF)],
        flops=2 * total * tokens * width,
        moved=2 * (total + 3 * tokens) * width,
        after=(*norm_after, cot_rows),
    )
    rows = exchange(send_rows, owners, "exp")

    full_w = pltpu.VMEM((groups, ffw, part), BF)
    hidden, to_gate, to_up = call(
        functools.partial(up_kernel, shape),
        (sds((total, ffw)), sds((total, ffw), F32), sds((total, ffw), F32)),
        (place, rows, *flat(gate_in), *flat(up_in)),
        [SMEM, VMEM] + [HBM] * (2 * sum(shape)),
        [full_w, full_w, pltpu.SemaphoreType.DMA((2, groups))],
        flops=2 * one,
        moved=4 * width * ffw + 2 * total * width + 10 * total * ffw,
        after=up_after,

    )
    out_first, d_hidden = call(
        functools.partial(down_kernel, shape[:-1]),
        (sds((total, width - part)), sds((total, ffw), F32)),
        (place, hidden, cot_rows, *flat(down_in[:-1])),
        [SMEM, VMEM, VMEM] + [HBM] * sum(shape[:-1]),
        [
            pltpu.VMEM((groups - 1, ffw, part), BF),
            pltpu.SemaphoreType.DMA((groups - 1,)),
        ],
        flops=2 * one * (groups - 1) // groups,
        moved=2 * width * ffw + 4 * total * width + 6 * total * ffw,
    )
    back_first = exchange(out_first, owners, "exp")
    early = groups // 2
    shape_early = [*shape[:early], shape[-1]]
    half_w = pltpu.VMEM((early, ffw, part), BF)
    late_w = pltpu.VMEM((groups - early, ffw, part), BF)
    back, d_gate, d_up = call(
        functools.partial(grad_kernel, shape_early),
        (sds((total, (early + 1) * part)), sds((total, ffw)), sds((total, ffw))),
        (
            place,
            hidden,
            cot_rows,
            d_hidden,
            to_gate,
            to_up,
            *flat(down_in[-1:]),
            *flat(gate_in[:early]),
            *flat(up_in[:early]),
        ),
        [SMEM] + [HBM] * (5 + shape[-1] + 2 * sum(shape[:early])),
        [
            pltpu.VMEM((ffw, part), BF),
            half_w,
            half_w,
            pltpu.SemaphoreType.DMA((8, groups)),
            pltpu.VMEM((total, ffw), BF),
            pltpu.VMEM((total, part), BF),
            pltpu.VMEM((total, ffw), F32),
            pltpu.VMEM((total, ffw), F32),
            pltpu.VMEM((total, ffw), F32),
        ],
        flops=one + 2 * one // groups,
        moved=2 * width * ffw + 2 * total * width + 18 * total * ffw,
    )
    back_early = exchange(back, owners, "exp")
    rest = call(
        functools.partial(rest_kernel, shape[early:]),
        sds((total, width - early * part)),
        (place, d_gate, d_up, *flat(gate_in[early:]), *flat(up_in[early:])),
        [SMEM, VMEM, VMEM] + [HBM] * (2 * sum(shape[early:])),
        [late_w, late_w, pltpu.SemaphoreType.DMA((2, groups))],
        flops=one,
        moved=2 * width * ffw + 2 * total * width + 4 * total * ffw,
    )
    back_late = exchange(rest, owners, "exp")
    output, stream_grad = call(
        functools.partial(final_kernel, owners, cap),
        (sds((tokens, width)), sds((tokens, width))),
        (place, ids, weights, gain, stream, cot, back_first, back_early, back_late),
        [SMEM] + [VMEM] * 8,
        [pltpu.VMEM((tokens, width), F32)],
        flops=6 * total * tokens * width,
        moved=4 * total * width + 8 * tokens * width,
        vmem=16,
        held=True,
    )
    return (output[None], stream_grad[None])


def solution(mesh):
    placed = (
        P("exp", "seq", None),
        P("exp", "seq", None),
        P("exp", "seq", None),
        P("exp", "seq", None),
        P(),
        P("exp", "seq", None),
        P("exp", "seq", None),
        P("exp", None, "seq"),
        P("exp", "seq", None),
        P("exp", "seq", None),
        P("exp", "seq", None),
    )
    return jax.shard_map(
        per_device,
        mesh=mesh,
        in_specs=placed,
        out_specs=(P("exp", "seq", None), P("exp", "seq", None)),
        check_vma=False,
    )
```

```python
import functools

import jax
import jax.numpy as jnp
from jax import lax
from jax.experimental import pallas as pl
from jax.experimental.pallas import tpu as pltpu
from jax.sharding import PartitionSpec as P

HD = 128
BF = jnp.bfloat16
F32 = jnp.float32
MIB = 1 << 20
HBM = pl.BlockSpec(memory_space=pltpu.HBM)
VMEM = pl.BlockSpec(memory_space=pltpu.VMEM)
SMEM = pl.BlockSpec(memory_space=pltpu.SMEM)
NT = (((1,), (1,)), ((), ()))
NN = (((1,), (0,)), ((), ()))


def mm(a, b, dims):
    return lax.dot_general(a, b, dims, preferred_element_type=F32)


def whole(array):
    return pl.BlockSpec(array.shape, lambda i: (0,) * len(array.shape))


def call(kernel, outs, args, in_specs, scratch=(), flops=0, moved=0, vmem=56, after=(), held=False):
    count, extra = len(args), len(after)

    def body(*refs):
        kernel(*refs[:count], *refs[count + extra :])

    return pl.pallas_call(
        body,
        grid=() if held else (1,),
        out_shape=outs,
        in_specs=[
            *[
                whole(arg) if spec is VMEM and not held else spec
                for arg, spec in zip(args, in_specs)
            ],
            *[HBM] * extra,
        ],
        out_specs=jax.tree.map(lambda out: VMEM if held else whole(out), outs),
        scratch_shapes=list(scratch),
        compiler_params=pltpu.CompilerParams(vmem_limit_bytes=vmem * MIB),
        cost_estimate=pl.CostEstimate(flops=flops, bytes_accessed=moved, transcendentals=0),
    )(*args, *after)


def gated(array, *first):
    return lax.optimization_barrier((array, *first))[0] if first else array


def sds(shape, dtype=BF):
    return jax.ShapeDtypeStruct(shape, dtype)


def pack_kernel(q_ref, k_ref, v_ref, o_ref):
    rows = q_ref.shape[0]
    o_ref[0, 0:rows] = q_ref[...]
    o_ref[0, rows : 2 * rows] = k_ref[...]
    o_ref[0, 2 * rows : 3 * rows] = v_ref[...]


def pack(q, k, v, groups):
    rows, width = q.shape
    part = width // groups
    spec = pl.BlockSpec((rows, part), lambda g: (0, g))
    return pl.pallas_call(
        pack_kernel,
        grid=(groups,),
        out_shape=sds((groups, 3 * rows, part)),
        in_specs=[spec] * 3,
        out_specs=pl.BlockSpec((1, 3 * rows, part), lambda g: (g, 0, 0)),
        cost_estimate=pl.CostEstimate(
            flops=0, bytes_accessed=12 * rows * width, transcendentals=0
        ),
    )(q, k, v)


def attend_head(blocks, query_of, keys, vals, store):
    rows = keys.shape[0] // blocks
    scale = HD ** (-0.5)
    row_ids = lax.broadcasted_iota(jnp.int32, (rows, rows), 0)
    col_ids = lax.broadcasted_iota(jnp.int32, (rows, rows), 1)
    keep = col_ids <= row_ids
    for b in range(blocks):
        query = query_of(b)
        end = b * rows
        diag = mm(query, keys[end : end + rows], NT) * scale
        diag = jnp.where(keep, diag, -jnp.inf)
        top = jnp.max(diag, axis=-1, keepdims=True)
        if b:
            early = mm(query, keys[:end], NT) * scale
            top = jnp.maximum(top, jnp.max(early, axis=-1, keepdims=True))
        diag = jnp.exp(diag - top)
        total = jnp.sum(diag, axis=-1, keepdims=True)
        if b:
            early = jnp.exp(early - top)
            total = total + jnp.sum(early, axis=-1, keepdims=True)
        inverse = 1.0 / total
        ctx = mm((diag * inverse).astype(BF), vals[end : end + rows], NN)
        if b:
            ctx = ctx + mm((early * inverse).astype(BF), vals[:end], NN)
        store(b, ctx.astype(BF))


def attend_kernel(x_ref, o_ref):
    blocks, three, hd = x_ref.shape
    rows = three // 3

    def store(b, ctx):
        o_ref[b] = ctx

    attend_head(
        blocks,
        lambda b: x_ref[b, 0:rows, :],
        x_ref[:, rows : 2 * rows, :].reshape(blocks * rows, hd),
        x_ref[:, 2 * rows : 3 * rows, :].reshape(blocks * rows, hd),
        store,
    )


def attend(x):
    blocks, three, part = x.shape
    rows = three // 3
    length = blocks * rows
    return pl.pallas_call(
        attend_kernel,
        grid=(part // HD,),
        out_shape=sds((blocks, rows, part)),
        in_specs=[pl.BlockSpec((blocks, three, HD), lambda h: (0, 0, h))],
        out_specs=pl.BlockSpec((blocks, rows, HD), lambda h: (0, 0, h)),
        compiler_params=pltpu.CompilerParams(vmem_limit_bytes=40 * MIB),
        cost_estimate=pl.CostEstimate(
            flops=4 * length * length * part,
            bytes_accessed=8 * length * part,
            transcendentals=length * length * part // HD,
        ),
    )(x)


INNER, COLS, PLANE, ATTEND = 0, 1, 5, 6


def halves_kernel(place_ref, q_ref, k_ref, v_ref, first_ref, second_ref):
    rows, width = q_ref.shape
    half = width // 2

    def copy(lower, upper):
        for i, ref in enumerate((q_ref, k_ref, v_ref)):
            lower[i * rows : (i + 1) * rows] = ref[:, :half]
            upper[i * rows : (i + 1) * rows] = ref[:, half:]

    @pl.when(place_ref[PLANE] < 2)
    def _():
        copy(first_ref, second_ref)

    @pl.when(place_ref[PLANE] >= 2)
    def _():
        copy(second_ref, first_ref)


def middle_kernel(place_ref, own_in, near_in, mid_in, far_in, *refs):
    *outs, x_ref, ctx_ref, sems = refs
    blocks, three, half = x_ref.shape
    rows = three // 3

    @pl.when(place_ref[INNER] == 1)
    def _():
        copies = [
            pltpu.make_async_copy(ref, x_ref.at[place_ref[ATTEND + i]], sems.at[i])
            for i, ref in enumerate((own_in, near_in, mid_in, far_in))
        ]
        for copy in copies:
            copy.start()
        for copy in copies:
            copy.wait()

        def step(i, carry):
            for j in range(2):
                cols = pl.ds(pl.multiple_of((2 * i + j) * HD, HD), HD)

                def store(b, ctx, cols=cols):
                    ctx_ref[b, :, cols] = ctx

                attend_head(
                    blocks,
                    lambda b, cols=cols: x_ref[b, 0:rows, cols],
                    x_ref[:, rows : 2 * rows, cols].reshape(blocks * rows, HD),
                    x_ref[:, 2 * rows : 3 * rows, cols].reshape(blocks * rows, HD),
                    store,
                )
            return carry

        lax.fori_loop(0, half // HD // 2, step, 0)
        for i, out in enumerate(outs):
            out[...] = ctx_ref[place_ref[ATTEND + i]]


def line_of_four(place, queries, keys, values, gate, up, down, cot_rows):
    rows, width = queries.shape
    half = width // 2
    block = sds((3 * rows, half))
    first, second = call(
        halves_kernel,
        (block, block),
        (place, queries, keys, values),
        [SMEM, VMEM, VMEM, VMEM],
        moved=12 * rows * width,
    )
    gate_end = send(gate, OUTWARD)
    up_end = send(up, OUTWARD)
    near = send(first, INWARD)
    mid = send(second, MIDDLE)
    far = send(second, [(0, 2), (3, 1)])
    piece = sds((rows, half))
    pieces = call(
        middle_kernel,
        (piece,) * 4,
        (place, first, near, mid, far),
        [SMEM] + [HBM] * 4,
        [
            pltpu.VMEM((4, 3 * rows, half), BF),
            pltpu.VMEM((4, rows, half), BF),
            pltpu.SemaphoreType.DMA((4,)),
        ],
        flops=64 * rows * rows * half,
        moved=32 * rows * half,
        after=(gate_end, up_end, cot_rows),
    )
    gate_mid = send(gate, MIDDLE, near, mid, far)
    gate_inner = send(gate, INWARD, near, far)
    down_end = send(down, OUTWARD)
    gate_far = send(gate_mid, OUTWARD, down_end, *pieces)
    up_mid = send(up, MIDDLE, gate_mid)
    up_inner = send(up, INWARD, gate_inner)
    own, near, mid, far = lax.optimization_barrier((*pieces, gate_far, up_mid))[:4]
    near = send(near, OUTWARD)
    mid = send(mid, MIDDLE)
    far = send(far, [(2, 0), (1, 3)])
    gate_mid_near = send(gate_inner, MIDDLE, up_mid, gate_far)
    up_far = send(up_mid, OUTWARD, gate_far)
    up_mid_near = send(up_inner, MIDDLE, mid, far)
    down_inner = send(down, INWARD, up_inner, up_mid)
    gate_far_near = send(gate_mid_near, OUTWARD, up_far)
    down_mid = send(down, MIDDLE, gate_mid_near)
    up_far_near = send(up_mid_near, OUTWARD, up_far)
    down_mid_near = send(down_inner, MIDDLE, up_mid_near)
    down_far = send(down_mid, OUTWARD, gate_far_near)
    down_far_near = send(down_mid_near, OUTWARD, up_far_near)
    norm_after = ()
    up_after = (down_mid_near,)
    gate_in = [
        [gate],
        [gate_inner, gate_end],
        [gate_mid, gate_far],
        [gate_mid_near, gate_far_near],
    ]
    up_in = [[up], [up_inner, up_end], [up_mid, up_far], [up_mid_near, up_far_near]]
    down_in = [
        [down],
        [down_inner, down_end],
        [down_mid, down_far],
        [down_mid_near, down_far_near],
    ]
    return (own, near, mid, far), gate_in, up_in, down_in, norm_after, up_after


def join_middle(place_ref, pieces, ctx_ref):
    own, near, mid, far = pieces
    half = own.shape[1]
    for plane, (lower, upper) in enumerate(((near, far), (own, mid), (mid, own), (far, near))):

        @pl.when(place_ref[PLANE] == plane)
        def _(lower=lower, upper=upper):
            ctx_ref[:, :half] = lower[...]
            ctx_ref[:, half:] = upper[...]


def join_groups(place_ref, pieces, ctx_ref):
    (ctx,) = pieces
    groups, _, part = ctx.shape
    for g in range(groups):
        ctx_ref[:, g * part : (g + 1) * part] = ctx[g]


def slot_rows(ids_t, owners, cap):
    tokens = ids_t.shape[1]
    experts = lax.broadcasted_iota(jnp.int32, (owners, tokens), 0)
    first = (experts == ids_t[0:1]).astype(F32)
    second = (experts == ids_t[1:2]).astype(F32)
    src = lax.broadcasted_iota(jnp.int32, (tokens, tokens), 0)
    dst = lax.broadcasted_iota(jnp.int32, (tokens, tokens), 1)
    earlier = (src < dst).astype(F32).astype(BF)
    count = mm((first + second).astype(BF), earlier, NN)
    slot0 = jnp.sum(first * count, axis=0, keepdims=True).astype(jnp.int32)
    slot1 = jnp.sum(second * count, axis=0, keepdims=True).astype(jnp.int32)
    return ids_t[0:1] * cap + slot0, ids_t[1:2] * cap + slot1


def slot_cols(ids, owners, cap):
    tokens = ids.shape[0]
    experts = lax.broadcasted_iota(jnp.int32, (tokens, owners), 1)
    first = (experts == ids[:, 0:1]).astype(F32)
    second = (experts == ids[:, 1:2]).astype(F32)
    dst = lax.broadcasted_iota(jnp.int32, (tokens, tokens), 0)
    src = lax.broadcasted_iota(jnp.int32, (tokens, tokens), 1)
    earlier = (src < dst).astype(F32).astype(BF)
    count = mm(earlier, (first + second).astype(BF), NN)
    slot0 = jnp.sum(first * count, axis=1, keepdims=True).astype(jnp.int32)
    slot1 = jnp.sum(second * count, axis=1, keepdims=True).astype(jnp.int32)
    return ids[:, 0:1] * cap + slot0, ids[:, 1:2] * cap + slot1


def one_hot(hit):
    return jnp.where(hit, 1.0, 0.0).astype(BF)


def send_cot_kernel(owners, cap, ids_ref, w_ref, cot_ref, o_ref):
    tokens = cot_ref.shape[0]
    at0, at1 = slot_rows(ids_ref[...], owners, cap)
    rows = lax.broadcasted_iota(jnp.int32, (owners * cap, tokens), 0)
    cot = cot_ref[...].astype(F32)
    o_ref[...] = (
        mm(one_hot(rows == at0), (w_ref[:, 0:1] * cot).astype(BF), NN)
        + mm(one_hot(rows == at1), (w_ref[:, 1:2] * cot).astype(BF), NN)
    ).astype(BF)


def norm_kernel(owners, cap, join, place_ref, ids_ref, resid_ref, gain_ref, *refs):
    *pieces, stream_ref, o_ref, ctx_ref = refs
    tokens, width = resid_ref.shape
    join(place_ref, pieces, ctx_ref)
    stream = (resid_ref[...].astype(F32) + ctx_ref[...].astype(F32)).astype(BF)
    stream_ref[...] = stream
    stream = stream.astype(F32)
    square = jnp.sum(stream * stream, axis=-1, keepdims=True)
    inv_rms = lax.rsqrt(square / width + 1e-05)
    at0, at1 = slot_rows(ids_ref[...], owners, cap)
    rows = lax.broadcasted_iota(jnp.int32, (owners * cap, tokens), 0)
    pick = one_hot((rows == at0) | (rows == at1))
    normed = ((stream_ref[...].astype(F32) * inv_rms) * gain_ref[...]).astype(BF)
    o_ref[...] = mm(pick, normed, NN).astype(BF)


def fetch(inner, choices, dst, sem):
    if len(choices) == 1:
        pltpu.make_async_copy(choices[0], dst, sem).start()
        return

    @pl.when(inner == 1)
    def _():
        pltpu.make_async_copy(choices[0], dst, sem).start()

    @pl.when(inner == 0)
    def _():
        pltpu.make_async_copy(choices[1], dst, sem).start()


def arrived(choices, dst, sem):
    pltpu.make_async_copy(choices[0], dst, sem).wait()


def regroup(refs, shape):
    refs = list(refs)
    return [[refs.pop(0) for _ in range(size)] for size in shape], refs


def cols_of(place_ref, slot, part):
    return pl.ds(pl.multiple_of(place_ref[COLS + slot] * part, part), part)


def up_kernel(shape, place_ref, x_ref, *refs):
    slots = len(shape)
    gate_in, refs = regroup(refs, shape)
    up_in, refs = regroup(refs, shape)
    hidden_ref, to_gate_ref, to_up_ref, gate_w, up_w, sems = refs
    part = gate_w.shape[2]
    inner = place_ref[INNER]
    for j in range(slots):
        fetch(inner, gate_in[j], gate_w.at[j], sems.at[0, j])
        fetch(inner, up_in[j], up_w.at[j], sems.at[1, j])
    gate = up = None
    for j in range(slots):
        rows = x_ref[:, cols_of(place_ref, j, part)]
        arrived(gate_in[j], gate_w.at[j], sems.at[0, j])
        term = mm(rows, gate_w[j], NT)
        gate = term if gate is None else gate + term
        arrived(up_in[j], up_w.at[j], sems.at[1, j])
        term = mm(rows, up_w[j], NT)
        up = term if up is None else up + term
    sigma = 1.0 / (1.0 + jnp.exp(-gate))
    silu = gate * sigma
    hidden_ref[...] = (silu * up).astype(BF)
    to_gate_ref[...] = up * sigma * (1.0 + gate * (1.0 - sigma))
    to_up_ref[...] = silu


def down_kernel(shape, place_ref, hidden_ref, cot_ref, *refs):
    slots = len(shape)
    down_in, refs = regroup(refs, shape)
    out_ref, d_hidden_ref, down_w, sems = refs
    part = down_w.shape[2]
    inner = place_ref[INNER]
    for j in range(slots):
        fetch(inner, down_in[j], down_w.at[j], sems.at[j])
    total = None
    for j in range(slots):
        rows = cot_ref[:, cols_of(place_ref, j, part)]
        arrived(down_in[j], down_w.at[j], sems.at[j])
        term = mm(rows, down_w[j], NT)
        total = term if total is None else total + term
        out_ref[:, j * part : (j + 1) * part] = mm(hidden_ref[...], down_w[j], NN).astype(BF)
    d_hidden_ref[...] = total


def grad_kernel(
    shape, place_ref, hidden_in, cot_in, d_hidden_in, to_gate_in, to_up_in, *refs
):
    slots = len(shape) - 1
    down_in, refs = regroup(refs, shape[-1:])
    gate_in, refs = regroup(refs, shape[:-1])
    up_in, refs = regroup(refs, shape[:-1])
    o_ref, down_w, gate_w, up_w, sems = refs[:5]
    hidden_ref, cot_ref, d_hidden_ref, to_gate_ref, to_up_ref = refs[5:]
    part = down_w.shape[1]
    inner = place_ref[INNER]
    last = place_ref[COLS + cot_in.shape[1] // part - 1]
    pairs = [
        (cot_in.at[:, pl.ds(pl.multiple_of(last * part, part), part)], cot_ref),
        (d_hidden_in, d_hidden_ref),
        (to_gate_in, to_gate_ref),
        (to_up_in, to_up_ref),
        (hidden_in, hidden_ref),
    ]
    fetch(inner, down_in[0], down_w, sems.at[2, 0])
    copies = [
        pltpu.make_async_copy(src, dst, sems.at[3 + i, 0]) for i, (src, dst) in enumerate(pairs)
    ]
    for copy in copies:
        copy.start()
    for j in range(slots):
        fetch(inner, gate_in[j], gate_w.at[j], sems.at[0, j])
        fetch(inner, up_in[j], up_w.at[j], sems.at[1, j])
    arrived(down_in[0], down_w, sems.at[2, 0])
    for copy in copies:
        copy.wait()
    d_hidden = d_hidden_ref[...] + mm(cot_ref[...], down_w[...], NT)
    d_gate = (d_hidden * to_gate_ref[...]).astype(BF)
    d_up = (d_hidden * to_up_ref[...]).astype(BF)
    o_ref[:, slots * part :] = mm(hidden_ref[...], down_w[...], NN).astype(BF)
    for j in range(slots):
        arrived(gate_in[j], gate_w.at[j], sems.at[0, j])
        arrived(up_in[j], up_w.at[j], sems.at[1, j])
        o_ref[:, j * part : (j + 1) * part] = (
            mm(d_gate, gate_w[j], NN) + mm(d_up, up_w[j], NN)
        ).astype(BF)


def final_kernel(
    owners,
    cap,
    place_ref,
    ids_ref,
    w_ref,
    gain_ref,
    stream_ref,
    cot_ref,
    first_ref,
    last_ref,
    output_ref,
    grad_ref,
    d_normed_ref,
):
    tokens, width = stream_ref.shape
    done = first_ref.shape[1]
    part = width - done
    slots = width // part
    at0, at1 = slot_cols(ids_ref[...], owners, cap)
    rows = lax.broadcasted_iota(jnp.int32, (tokens, owners * cap), 1)
    pick0, pick1 = one_hot(rows == at0), one_hot(rows == at1)
    both = pick0 + pick1
    w0, w1 = w_ref[:, 0:1], w_ref[:, 1:2]
    square = jnp.zeros((tokens, 1), F32)
    dot = jnp.zeros((tokens, 1), F32)
    for j in range(slots):
        cols = cols_of(place_ref, j, part)
        if j < slots - 1:
            pairs = first_ref[:, j * part : (j + 1) * part]
        else:
            pairs = last_ref[:, width:]
        stream = stream_ref[:, cols].astype(F32)
        mixed = w0 * mm(pick0, pairs, NN) + w1 * mm(pick1, pairs, NN)
        output_ref[:, cols] = (stream + mixed).astype(BF)
        grads = last_ref[:, j * part : (j + 1) * part]
        gained = mm(both, grads, NN) * gain_ref[:, cols]
        d_normed_ref[:, cols] = gained
        square = square + jnp.sum(stream * stream, axis=-1, keepdims=True)
        dot = dot + jnp.sum(gained * stream, axis=-1, keepdims=True)
    inv_rms = lax.rsqrt(square / width + 1e-05)
    mean = dot * inv_rms / width
    unit_rows = stream_ref[...].astype(F32) * inv_rms
    d_stream = inv_rms * (d_normed_ref[...] - unit_rows * mean)
    grad_ref[...] = (cot_ref[...].astype(F32) + d_stream).astype(BF)


MIDDLE = [(1, 2), (2, 1)]
OUTWARD = [(1, 0), (2, 3)]
INWARD = [(0, 1), (3, 2)]


def gather_all(shard, groups):
    whole_weight = lax.all_gather(shard, "seq", axis=0)
    return [[whole_weight[j]] for j in range(groups)]


def send(array, pairs, *first):
    return lax.ppermute(gated(array, *first), "seq", pairs)


def places(groups):
    if groups == 4:
        own = lax.axis_index("seq")
        table = jnp.array(
            [
                [0, 0, 1, 2, 3, 0, 0, 0, 0, 0],
                [1, 1, 0, 2, 3, 1, 1, 0, 2, 3],
                [1, 2, 3, 1, 0, 2, 2, 3, 1, 0],
                [0, 3, 2, 1, 0, 3, 0, 0, 0, 0],
            ],
            jnp.int32,
        )
        return table[own]
    return jnp.arange(-1, groups, dtype=jnp.int32)


def exchange(rows, owners, axis):
    total, width = rows.shape
    rows = rows.reshape(owners, total // owners, width)
    rows = lax.all_to_all(rows, axis, split_axis=0, concat_axis=0, tiled=True)
    return rows.reshape(total, width)


def flat(slots):
    return [ref for choices in slots for ref in choices]


def per_device(
    queries,
    keys,
    values,
    resid,
    norm_gain,
    w_gate,
    w_up,
    w_down,
    expert_ids,
    route_weights,
    cotangent,
):
    groups = lax.axis_size("seq")
    owners = lax.axis_size("exp")
    tokens, width = queries.shape[1:]
    ffw = w_gate.shape[2]
    part = width // groups
    cap = max(2, tokens * 10 // (4 * owners))
    total = owners * cap
    ids = expert_ids[0]
    ids_t = ids.T
    weights = route_weights[0]
    gain = norm_gain[None]
    cot = cotangent[0]
    place = places(groups)

    one = 2 * total * width * ffw
    send_cot = call(
        functools.partial(send_cot_kernel, owners, cap),
        sds((total, width)),
        (ids_t, weights, cot),
        [VMEM] * 3,
        flops=4 * total * tokens * width,
        moved=2 * (total + tokens) * width,
    )
    cot_rows = exchange(send_cot, owners, "exp")
    shards = (w_gate[0].T, w_up[0].T, w_down[0])
    if groups == 4:
        join = join_middle
        pieces, gate_in, up_in, down_in, norm_after, up_after = line_of_four(
            place, queries[0], keys[0], values[0], *shards, cot_rows
        )
    else:
        join = join_groups
        gate_in, up_in, down_in = [gather_all(shard, groups) for shard in shards]
        packed = pack(queries[0], keys[0], values[0], groups)
        heads = lax.all_to_all(packed, "seq", split_axis=0, concat_axis=0, tiled=True)
        ctx = attend(heads)
        pieces = (lax.all_to_all(ctx, "seq", split_axis=0, concat_axis=0, tiled=True),)
        norm_after = up_after = ()
    shape = [len(choices) for choices in gate_in]

    stream, send_rows = call(
        functools.partial(norm_kernel, owners, cap, join),
        (sds((tokens, width)), sds((total, width))),
        (place, ids_t, resid[0], gain, *pieces),
        [SMEM] + [VMEM] * (3 + len(pieces)),
        [pltpu.VMEM((tokens, width), BF)],
        flops=2 * total * tokens * width,
        moved=2 * (total + 3 * tokens) * width,
        after=norm_after,
    )
    rows = exchange(send_rows, owners, "exp")

    full_w = pltpu.VMEM((groups, ffw, part), BF)
    hidden, to_gate, to_up = call(
        functools.partial(up_kernel, shape),
        (sds((total, ffw)), sds((total, ffw), F32), sds((total, ffw), F32)),
        (place, rows, *flat(gate_in), *flat(up_in)),
        [SMEM, VMEM] + [HBM] * (2 * sum(shape)),
        [full_w, full_w, pltpu.SemaphoreType.DMA((2, groups))],
        flops=2 * one,
        moved=4 * width * ffw + 2 * total * width + 10 * total * ffw,
        after=up_after,

    )
    out_first, d_hidden = call(
        functools.partial(down_kernel, shape[:-1]),
        (sds((total, width - part)), sds((total, ffw), F32)),
        (place, hidden, cot_rows, *flat(down_in[:-1])),
        [SMEM, VMEM, VMEM] + [HBM] * sum(shape[:-1]),
        [
            pltpu.VMEM((groups - 1, ffw, part), BF),
            pltpu.SemaphoreType.DMA((groups - 1,)),
        ],
        flops=2 * one * (groups - 1) // groups,
        moved=2 * width * ffw + 4 * total * width + 6 * total * ffw,
    )
    back_first = exchange(out_first, owners, "exp")
    back = call(
        functools.partial(grad_kernel, [*shape, shape[-1]]),
        sds((total, width + part)),
        (
            place,
            hidden,
            cot_rows,
            d_hidden,
            to_gate,
            to_up,
            *flat(down_in[-1:]),
            *flat(gate_in),
            *flat(up_in),
        ),
        [SMEM] + [HBM] * (5 + shape[-1] + 2 * sum(shape)),
        [
            pltpu.VMEM((ffw, part), BF),
            full_w,
            full_w,
            pltpu.SemaphoreType.DMA((8, groups)),
            pltpu.VMEM((total, ffw), BF),
            pltpu.VMEM((total, part), BF),
            pltpu.VMEM((total, ffw), F32),
            pltpu.VMEM((total, ffw), F32),
            pltpu.VMEM((total, ffw), F32),
        ],
        flops=2 * one + 2 * one // groups,
        moved=4 * width * ffw + 4 * total * width + 14 * total * ffw,
    )
    back_last = exchange(back, owners, "exp")
    output, stream_grad = call(
        functools.partial(final_kernel, owners, cap),
        (sds((tokens, width)), sds((tokens, width))),
        (place, ids, weights, gain, stream, cot, back_first, back_last),
        [SMEM] + [VMEM] * 7,
        [pltpu.VMEM((tokens, width), F32)],
        flops=6 * total * tokens * width,
        moved=4 * total * width + 8 * tokens * width,
        vmem=16,
        held=True,
    )
    return (output[None], stream_grad[None])


def solution(mesh):
    placed = (
        P("exp", "seq", None),
        P("exp", "seq", None),
        P("exp", "seq", None),
        P("exp", "seq", None),
        P(),
        P("exp", "seq", None),
        P("exp", "seq", None),
        P("exp", None, "seq"),
        P("exp", "seq", None),
        P("exp", "seq", None),
        P("exp", "seq", None),
    )
    return jax.shard_map(
        per_device,
        mesh=mesh,
        in_specs=placed,
        out_specs=(P("exp", "seq", None), P("exp", "seq", None)),
        check_vma=False,
    )
```

```python
import functools

import jax
import jax.numpy as jnp
from jax import lax
from jax.experimental import pallas as pl
from jax.experimental.pallas import tpu as pltpu
from jax.sharding import PartitionSpec as P

HD = 128
BF = jnp.bfloat16
F32 = jnp.float32
MIB = 1 << 20
HBM = pl.BlockSpec(memory_space=pltpu.HBM)
VMEM = pl.BlockSpec(memory_space=pltpu.VMEM)
SMEM = pl.BlockSpec(memory_space=pltpu.SMEM)
NT = (((1,), (1,)), ((), ()))
NN = (((1,), (0,)), ((), ()))


def mm(a, b, dims):
    return lax.dot_general(a, b, dims, preferred_element_type=F32)


def whole(array):
    return pl.BlockSpec(array.shape, lambda i: (0,) * len(array.shape))


def call(kernel, outs, args, in_specs, scratch=(), flops=0, moved=0, vmem=56, after=(), held=False):
    count, extra = len(args), len(after)

    def body(*refs):
        kernel(*refs[:count], *refs[count + extra :])

    return pl.pallas_call(
        body,
        grid=() if held else (1,),
        out_shape=outs,
        in_specs=[
            *[
                whole(arg) if spec is VMEM and not held else spec
                for arg, spec in zip(args, in_specs)
            ],
            *[HBM] * extra,
        ],
        out_specs=jax.tree.map(lambda out: VMEM if held else whole(out), outs),
        scratch_shapes=list(scratch),
        compiler_params=pltpu.CompilerParams(vmem_limit_bytes=vmem * MIB),
        cost_estimate=pl.CostEstimate(flops=flops, bytes_accessed=moved, transcendentals=0),
    )(*args, *after)


def gated(array, *first):
    return lax.optimization_barrier((array, *first))[0] if first else array


def sds(shape, dtype=BF):
    return jax.ShapeDtypeStruct(shape, dtype)


def pack_kernel(q_ref, k_ref, v_ref, o_ref):
    rows = q_ref.shape[0]
    o_ref[0, 0:rows] = q_ref[...]
    o_ref[0, rows : 2 * rows] = k_ref[...]
    o_ref[0, 2 * rows : 3 * rows] = v_ref[...]


def pack(q, k, v, groups):
    rows, width = q.shape
    part = width // groups
    spec = pl.BlockSpec((rows, part), lambda g: (0, g))
    return pl.pallas_call(
        pack_kernel,
        grid=(groups,),
        out_shape=sds((groups, 3 * rows, part)),
        in_specs=[spec] * 3,
        out_specs=pl.BlockSpec((1, 3 * rows, part), lambda g: (g, 0, 0)),
        cost_estimate=pl.CostEstimate(
            flops=0, bytes_accessed=12 * rows * width, transcendentals=0
        ),
    )(q, k, v)


def attend_head(blocks, query_of, keys, vals, store):
    rows = keys.shape[0] // blocks
    scale = HD ** (-0.5)
    row_ids = lax.broadcasted_iota(jnp.int32, (rows, rows), 0)
    col_ids = lax.broadcasted_iota(jnp.int32, (rows, rows), 1)
    keep = col_ids <= row_ids
    for b in range(blocks):
        query = query_of(b)
        end = b * rows
        diag = mm(query, keys[end : end + rows], NT) * scale
        diag = jnp.where(keep, diag, -jnp.inf)
        top = jnp.max(diag, axis=-1, keepdims=True)
        if b:
            early = mm(query, keys[:end], NT) * scale
            top = jnp.maximum(top, jnp.max(early, axis=-1, keepdims=True))
        diag = jnp.exp(diag - top)
        total = jnp.sum(diag, axis=-1, keepdims=True)
        if b:
            early = jnp.exp(early - top)
            total = total + jnp.sum(early, axis=-1, keepdims=True)
        inverse = 1.0 / total
        ctx = mm((diag * inverse).astype(BF), vals[end : end + rows], NN)
        if b:
            ctx = ctx + mm((early * inverse).astype(BF), vals[:end], NN)
        store(b, ctx.astype(BF))


def attend_kernel(x_ref, o_ref):
    blocks, three, hd = x_ref.shape
    rows = three // 3

    def store(b, ctx):
        o_ref[b] = ctx

    attend_head(
        blocks,
        lambda b: x_ref[b, 0:rows, :],
        x_ref[:, rows : 2 * rows, :].reshape(blocks * rows, hd),
        x_ref[:, 2 * rows : 3 * rows, :].reshape(blocks * rows, hd),
        store,
    )


def attend(x):
    blocks, three, part = x.shape
    rows = three // 3
    length = blocks * rows
    return pl.pallas_call(
        attend_kernel,
        grid=(part // HD,),
        out_shape=sds((blocks, rows, part)),
        in_specs=[pl.BlockSpec((blocks, three, HD), lambda h: (0, 0, h))],
        out_specs=pl.BlockSpec((blocks, rows, HD), lambda h: (0, 0, h)),
        compiler_params=pltpu.CompilerParams(vmem_limit_bytes=40 * MIB),
        cost_estimate=pl.CostEstimate(
            flops=4 * length * length * part,
            bytes_accessed=8 * length * part,
            transcendentals=length * length * part // HD,
        ),
    )(x)


INNER, COLS, PLANE, ATTEND = 0, 1, 5, 6


def halves_kernel(place_ref, q_ref, k_ref, v_ref, first_ref, second_ref):
    rows, width = q_ref.shape
    half = width // 2

    def copy(lower, upper):
        for i, ref in enumerate((q_ref, k_ref, v_ref)):
            lower[i * rows : (i + 1) * rows] = ref[:, :half]
            upper[i * rows : (i + 1) * rows] = ref[:, half:]

    @pl.when(place_ref[PLANE] < 2)
    def _():
        copy(first_ref, second_ref)

    @pl.when(place_ref[PLANE] >= 2)
    def _():
        copy(second_ref, first_ref)


def middle_kernel(place_ref, own_in, near_in, mid_in, far_in, *refs):
    *outs, x_ref, ctx_ref, sems = refs
    blocks, three, half = x_ref.shape
    rows = three // 3

    @pl.when(place_ref[INNER] == 1)
    def _():
        copies = [
            pltpu.make_async_copy(ref, x_ref.at[place_ref[ATTEND + i]], sems.at[i])
            for i, ref in enumerate((own_in, near_in, mid_in, far_in))
        ]
        for copy in copies:
            copy.start()
        for copy in copies:
            copy.wait()

        def step(i, carry):
            for j in range(2):
                cols = pl.ds(pl.multiple_of((2 * i + j) * HD, HD), HD)

                def store(b, ctx, cols=cols):
                    ctx_ref[b, :, cols] = ctx

                attend_head(
                    blocks,
                    lambda b, cols=cols: x_ref[b, 0:rows, cols],
                    x_ref[:, rows : 2 * rows, cols].reshape(blocks * rows, HD),
                    x_ref[:, 2 * rows : 3 * rows, cols].reshape(blocks * rows, HD),
                    store,
                )
            return carry

        lax.fori_loop(0, half // HD // 2, step, 0)
        for i, out in enumerate(outs):
            out[...] = ctx_ref[place_ref[ATTEND + i]]


def line_of_four(place, queries, keys, values, gate, up, down, cot_rows):
    rows, width = queries.shape
    half = width // 2
    block = sds((3 * rows, half))
    first, second = call(
        halves_kernel,
        (block, block),
        (place, queries, keys, values),
        [SMEM, VMEM, VMEM, VMEM],
        moved=12 * rows * width,
    )
    gate_end = send(gate, OUTWARD)
    up_end = send(up, OUTWARD)
    down_end = send(down, OUTWARD, gate_end)
    near = send(first, INWARD)
    mid = send(second, MIDDLE)
    far = send(second, [(0, 2), (3, 1)])
    piece = sds((rows, half))
    pieces = call(
        middle_kernel,
        (piece,) * 4,
        (place, first, near, mid, far),
        [SMEM] + [HBM] * 4,
        [
            pltpu.VMEM((4, 3 * rows, half), BF),
            pltpu.VMEM((4, rows, half), BF),
            pltpu.SemaphoreType.DMA((4,)),
        ],
        flops=64 * rows * rows * half,
        moved=32 * rows * half,
        after=(gate_end, up_end, cot_rows),
    )
    gate_mid = send(gate, MIDDLE, near, mid, far)
    up_mid = send(up, MIDDLE, near, mid, far)
    down_mid = send(down, MIDDLE, gate_mid)
    gate_inner = send(gate, INWARD, near, far)
    up_inner = send(up, INWARD, gate_inner)
    down_inner = send(down, INWARD, up_inner)
    own, near, mid, far = lax.optimization_barrier((*pieces, gate_mid, gate_inner, down_end))[:4]
    near = send(near, OUTWARD)
    mid = send(mid, MIDDLE)
    far = send(far, [(2, 0), (1, 3)])
    gate_mid_near = send(gate_inner, MIDDLE)
    gate_far = send(gate_mid, OUTWARD)
    up_far = send(up_mid, OUTWARD)
    up_mid_near = send(up_inner, MIDDLE, gate_far)
    down_mid_near = send(down_inner, MIDDLE, up_far)
    gate_far_near = send(gate_mid_near, OUTWARD)
    up_far_near = send(up_mid_near, OUTWARD, gate_far_near)
    down_far = send(down_mid, OUTWARD, gate_far_near)
    down_far_near = send(down_mid_near, OUTWARD, up_far_near)
    norm_after = (down_mid, gate_mid_near, gate_far, up_far)
    up_after = (down_mid_near,)
    gate_in = [
        [gate],
        [gate_inner, gate_end],
        [gate_mid, gate_far],
        [gate_mid_near, gate_far_near],
    ]
    up_in = [[up], [up_inner, up_end], [up_mid, up_far], [up_mid_near, up_far_near]]
    down_in = [
        [down],
        [down_inner, down_end],
        [down_mid, down_far],
        [down_mid_near, down_far_near],
    ]
    return (own, near, mid, far), gate_in, up_in, down_in, norm_after, up_after


def join_middle(place_ref, pieces, ctx_ref):
    own, near, mid, far = pieces
    half = own.shape[1]
    for plane, (lower, upper) in enumerate(((near, far), (own, mid), (mid, own), (far, near))):

        @pl.when(place_ref[PLANE] == plane)
        def _(lower=lower, upper=upper):
            ctx_ref[:, :half] = lower[...]
            ctx_ref[:, half:] = upper[...]


def join_groups(place_ref, pieces, ctx_ref):
    (ctx,) = pieces
    groups, _, part = ctx.shape
    for g in range(groups):
        ctx_ref[:, g * part : (g + 1) * part] = ctx[g]


def slot_rows(ids_t, owners, cap):
    tokens = ids_t.shape[1]
    experts = lax.broadcasted_iota(jnp.int32, (owners, tokens), 0)
    first = (experts == ids_t[0:1]).astype(F32)
    second = (experts == ids_t[1:2]).astype(F32)
    src = lax.broadcasted_iota(jnp.int32, (tokens, tokens), 0)
    dst = lax.broadcasted_iota(jnp.int32, (tokens, tokens), 1)
    earlier = (src < dst).astype(F32).astype(BF)
    count = mm((first + second).astype(BF), earlier, NN)
    slot0 = jnp.sum(first * count, axis=0, keepdims=True).astype(jnp.int32)
    slot1 = jnp.sum(second * count, axis=0, keepdims=True).astype(jnp.int32)
    return ids_t[0:1] * cap + slot0, ids_t[1:2] * cap + slot1


def slot_cols(ids, owners, cap):
    tokens = ids.shape[0]
    experts = lax.broadcasted_iota(jnp.int32, (tokens, owners), 1)
    first = (experts == ids[:, 0:1]).astype(F32)
    second = (experts == ids[:, 1:2]).astype(F32)
    dst = lax.broadcasted_iota(jnp.int32, (tokens, tokens), 0)
    src = lax.broadcasted_iota(jnp.int32, (tokens, tokens), 1)
    earlier = (src < dst).astype(F32).astype(BF)
    count = mm(earlier, (first + second).astype(BF), NN)
    slot0 = jnp.sum(first * count, axis=1, keepdims=True).astype(jnp.int32)
    slot1 = jnp.sum(second * count, axis=1, keepdims=True).astype(jnp.int32)
    return ids[:, 0:1] * cap + slot0, ids[:, 1:2] * cap + slot1


def one_hot(hit):
    return jnp.where(hit, 1.0, 0.0).astype(BF)


def send_cot_kernel(owners, cap, ids_ref, w_ref, cot_ref, o_ref):
    tokens = cot_ref.shape[0]
    at0, at1 = slot_rows(ids_ref[...], owners, cap)
    rows = lax.broadcasted_iota(jnp.int32, (owners * cap, tokens), 0)
    cot = cot_ref[...].astype(F32)
    o_ref[...] = (
        mm(one_hot(rows == at0), (w_ref[:, 0:1] * cot).astype(BF), NN)
        + mm(one_hot(rows == at1), (w_ref[:, 1:2] * cot).astype(BF), NN)
    ).astype(BF)


def norm_kernel(owners, cap, join, place_ref, ids_ref, resid_ref, gain_ref, *refs):
    *pieces, stream_ref, o_ref, ctx_ref = refs
    tokens, width = resid_ref.shape
    join(place_ref, pieces, ctx_ref)
    stream = (resid_ref[...].astype(F32) + ctx_ref[...].astype(F32)).astype(BF)
    stream_ref[...] = stream
    stream = stream.astype(F32)
    square = jnp.sum(stream * stream, axis=-1, keepdims=True)
    inv_rms = lax.rsqrt(square / width + 1e-05)
    at0, at1 = slot_rows(ids_ref[...], owners, cap)
    rows = lax.broadcasted_iota(jnp.int32, (owners * cap, tokens), 0)
    pick = one_hot((rows == at0) | (rows == at1))
    normed = ((stream_ref[...].astype(F32) * inv_rms) * gain_ref[...]).astype(BF)
    o_ref[...] = mm(pick, normed, NN).astype(BF)


def fetch(inner, choices, dst, sem):
    if len(choices) == 1:
        pltpu.make_async_copy(choices[0], dst, sem).start()
        return

    @pl.when(inner == 1)
    def _():
        pltpu.make_async_copy(choices[0], dst, sem).start()

    @pl.when(inner == 0)
    def _():
        pltpu.make_async_copy(choices[1], dst, sem).start()


def arrived(choices, dst, sem):
    pltpu.make_async_copy(choices[0], dst, sem).wait()


def regroup(refs, shape):
    refs = list(refs)
    return [[refs.pop(0) for _ in range(size)] for size in shape], refs


def cols_of(place_ref, slot, part):
    return pl.ds(pl.multiple_of(place_ref[COLS + slot] * part, part), part)


def up_kernel(shape, place_ref, x_ref, *refs):
    slots = len(shape)
    gate_in, refs = regroup(refs, shape)
    up_in, refs = regroup(refs, shape)
    hidden_ref, to_gate_ref, to_up_ref, gate_w, up_w, sems = refs
    part = gate_w.shape[2]
    inner = place_ref[INNER]
    for j in range(slots):
        fetch(inner, gate_in[j], gate_w.at[j], sems.at[0, j])
        fetch(inner, up_in[j], up_w.at[j], sems.at[1, j])
    gate = up = None
    for j in range(slots):
        rows = x_ref[:, cols_of(place_ref, j, part)]
        arrived(gate_in[j], gate_w.at[j], sems.at[0, j])
        term = mm(rows, gate_w[j], NT)
        gate = term if gate is None else gate + term
        arrived(up_in[j], up_w.at[j], sems.at[1, j])
        term = mm(rows, up_w[j], NT)
        up = term if up is None else up + term
    sigma = 1.0 / (1.0 + jnp.exp(-gate))
    silu = gate * sigma
    hidden_ref[...] = (silu * up).astype(BF)
    to_gate_ref[...] = up * sigma * (1.0 + gate * (1.0 - sigma))
    to_up_ref[...] = silu


def down_kernel(shape, place_ref, hidden_ref, cot_ref, *refs):
    slots = len(shape)
    down_in, refs = regroup(refs, shape)
    out_ref, d_hidden_ref, down_w, sems = refs
    part = down_w.shape[2]
    inner = place_ref[INNER]
    for j in range(slots):
        fetch(inner, down_in[j], down_w.at[j], sems.at[j])
    total = None
    for j in range(slots):
        rows = cot_ref[:, cols_of(place_ref, j, part)]
        arrived(down_in[j], down_w.at[j], sems.at[j])
        term = mm(rows, down_w[j], NT)
        total = term if total is None else total + term
        out_ref[:, j * part : (j + 1) * part] = mm(hidden_ref[...], down_w[j], NN).astype(BF)
    d_hidden_ref[...] = total


def grad_kernel(
    shape, place_ref, hidden_in, cot_in, d_hidden_in, to_gate_in, to_up_in, *refs
):
    slots = len(shape) - 1
    down_in, refs = regroup(refs, shape[-1:])
    gate_in, refs = regroup(refs, shape[:-1])
    up_in, refs = regroup(refs, shape[:-1])
    o_ref, down_w, gate_w, up_w, sems = refs[:5]
    hidden_ref, cot_ref, d_hidden_ref, to_gate_ref, to_up_ref = refs[5:]
    part = down_w.shape[1]
    inner = place_ref[INNER]
    last = place_ref[COLS + cot_in.shape[1] // part - 1]
    pairs = [
        (cot_in.at[:, pl.ds(pl.multiple_of(last * part, part), part)], cot_ref),
        (d_hidden_in, d_hidden_ref),
        (to_gate_in, to_gate_ref),
        (to_up_in, to_up_ref),
        (hidden_in, hidden_ref),
    ]
    fetch(inner, down_in[0], down_w, sems.at[2, 0])
    copies = [
        pltpu.make_async_copy(src, dst, sems.at[3 + i, 0]) for i, (src, dst) in enumerate(pairs)
    ]
    for copy in copies:
        copy.start()
    for j in range(slots):
        fetch(inner, gate_in[j], gate_w.at[j], sems.at[0, j])
        fetch(inner, up_in[j], up_w.at[j], sems.at[1, j])
    arrived(down_in[0], down_w, sems.at[2, 0])
    for copy in copies:
        copy.wait()
    d_hidden = d_hidden_ref[...] + mm(cot_ref[...], down_w[...], NT)
    d_gate = (d_hidden * to_gate_ref[...]).astype(BF)
    d_up = (d_hidden * to_up_ref[...]).astype(BF)
    o_ref[:, slots * part :] = mm(hidden_ref[...], down_w[...], NN).astype(BF)
    for j in range(slots):
        arrived(gate_in[j], gate_w.at[j], sems.at[0, j])
        arrived(up_in[j], up_w.at[j], sems.at[1, j])
        o_ref[:, j * part : (j + 1) * part] = (
            mm(d_gate, gate_w[j], NN) + mm(d_up, up_w[j], NN)
        ).astype(BF)


def final_kernel(
    owners,
    cap,
    place_ref,
    ids_ref,
    w_ref,
    gain_ref,
    stream_ref,
    cot_ref,
    first_ref,
    last_ref,
    output_ref,
    grad_ref,
    d_normed_ref,
):
    tokens, width = stream_ref.shape
    done = first_ref.shape[1]
    part = width - done
    slots = width // part
    at0, at1 = slot_cols(ids_ref[...], owners, cap)
    rows = lax.broadcasted_iota(jnp.int32, (tokens, owners * cap), 1)
    pick0, pick1 = one_hot(rows == at0), one_hot(rows == at1)
    both = pick0 + pick1
    w0, w1 = w_ref[:, 0:1], w_ref[:, 1:2]
    square = jnp.zeros((tokens, 1), F32)
    dot = jnp.zeros((tokens, 1), F32)
    for j in range(slots):
        cols = cols_of(place_ref, j, part)
        if j < slots - 1:
            pairs = first_ref[:, j * part : (j + 1) * part]
        else:
            pairs = last_ref[:, width:]
        stream = stream_ref[:, cols].astype(F32)
        mixed = w0 * mm(pick0, pairs, NN) + w1 * mm(pick1, pairs, NN)
        output_ref[:, cols] = (stream + mixed).astype(BF)
        grads = last_ref[:, j * part : (j + 1) * part]
        gained = mm(both, grads, NN) * gain_ref[:, cols]
        d_normed_ref[:, cols] = gained
        square = square + jnp.sum(stream * stream, axis=-1, keepdims=True)
        dot = dot + jnp.sum(gained * stream, axis=-1, keepdims=True)
    inv_rms = lax.rsqrt(square / width + 1e-05)
    mean = dot * inv_rms / width
    unit_rows = stream_ref[...].astype(F32) * inv_rms
    d_stream = inv_rms * (d_normed_ref[...] - unit_rows * mean)
    grad_ref[...] = (cot_ref[...].astype(F32) + d_stream).astype(BF)


MIDDLE = [(1, 2), (2, 1)]
OUTWARD = [(1, 0), (2, 3)]
INWARD = [(0, 1), (3, 2)]


def gather_all(shard, groups):
    whole_weight = lax.all_gather(shard, "seq", axis=0)
    return [[whole_weight[j]] for j in range(groups)]


def send(array, pairs, *first):
    return lax.ppermute(gated(array, *first), "seq", pairs)


def places(groups):
    if groups == 4:
        own = lax.axis_index("seq")
        table = jnp.array(
            [
                [0, 0, 1, 2, 3, 0, 0, 0, 0, 0],
                [1, 1, 0, 2, 3, 1, 1, 0, 2, 3],
                [1, 2, 3, 1, 0, 2, 2, 3, 1, 0],
                [0, 3, 2, 1, 0, 3, 0, 0, 0, 0],
            ],
            jnp.int32,
        )
        return table[own]
    return jnp.arange(-1, groups, dtype=jnp.int32)


def exchange(rows, owners, axis):
    total, width = rows.shape
    rows = rows.reshape(owners, total // owners, width)
    rows = lax.all_to_all(rows, axis, split_axis=0, concat_axis=0, tiled=True)
    return rows.reshape(total, width)


def flat(slots):
    return [ref for choices in slots for ref in choices]


def per_device(
    queries,
    keys,
    values,
    resid,
    norm_gain,
    w_gate,
    w_up,
    w_down,
    expert_ids,
    route_weights,
    cotangent,
):
    groups = lax.axis_size("seq")
    owners = lax.axis_size("exp")
    tokens, width = queries.shape[1:]
    ffw = w_gate.shape[2]
    part = width // groups
    cap = max(2, tokens * 10 // (4 * owners))
    total = owners * cap
    ids = expert_ids[0]
    ids_t = ids.T
    weights = route_weights[0]
    gain = norm_gain[None]
    cot = cotangent[0]
    place = places(groups)

    one = 2 * total * width * ffw
    send_cot = call(
        functools.partial(send_cot_kernel, owners, cap),
        sds((total, width)),
        (ids_t, weights, cot),
        [VMEM] * 3,
        flops=4 * total * tokens * width,
        moved=2 * (total + tokens) * width,
    )
    cot_rows = exchange(send_cot, owners, "exp")
    shards = (w_gate[0].T, w_up[0].T, w_down[0])
    if groups == 4:
        join = join_middle
        pieces, gate_in, up_in, down_in, norm_after, up_after = line_of_four(
            place, queries[0], keys[0], values[0], *shards, cot_rows
        )
    else:
        join = join_groups
        gate_in, up_in, down_in = [gather_all(shard, groups) for shard in shards]
        packed = pack(queries[0], keys[0], values[0], groups)
        heads = lax.all_to_all(packed, "seq", split_axis=0, concat_axis=0, tiled=True)
        ctx = attend(heads)
        pieces = (lax.all_to_all(ctx, "seq", split_axis=0, concat_axis=0, tiled=True),)
        norm_after = up_after = ()
    shape = [len(choices) for choices in gate_in]

    stream, send_rows = call(
        functools.partial(norm_kernel, owners, cap, join),
        (sds((tokens, width)), sds((total, width))),
        (place, ids_t, resid[0], gain, *pieces),
        [SMEM] + [VMEM] * (3 + len(pieces)),
        [pltpu.VMEM((tokens, width), BF)],
        flops=2 * total * tokens * width,
        moved=2 * (total + 3 * tokens) * width,
        after=norm_after,
    )
    rows = exchange(send_rows, owners, "exp")

    full_w = pltpu.VMEM((groups, ffw, part), BF)
    hidden, to_gate, to_up = call(
        functools.partial(up_kernel, shape),
        (sds((total, ffw)), sds((total, ffw), F32), sds((total, ffw), F32)),
        (place, rows, *flat(gate_in), *flat(up_in)),
        [SMEM, VMEM] + [HBM] * (2 * sum(shape)),
        [full_w, full_w, pltpu.SemaphoreType.DMA((2, groups))],
        flops=2 * one,
        moved=4 * width * ffw + 2 * total * width + 10 * total * ffw,
        after=up_after,

    )
    out_first, d_hidden = call(
        functools.partial(down_kernel, shape[:-1]),
        (sds((total, width - part)), sds((total, ffw), F32)),
        (place, hidden, cot_rows, *flat(down_in[:-1])),
        [SMEM, VMEM, VMEM] + [HBM] * sum(shape[:-1]),
        [
            pltpu.VMEM((groups - 1, ffw, part), BF),
            pltpu.SemaphoreType.DMA((groups - 1,)),
        ],
        flops=2 * one * (groups - 1) // groups,
        moved=2 * width * ffw + 4 * total * width + 6 * total * ffw,
    )
    back_first = exchange(out_first, owners, "exp")
    back = call(
        functools.partial(grad_kernel, [*shape, shape[-1]]),
        sds((total, width + part)),
        (
            place,
            hidden,
            cot_rows,
            d_hidden,
            to_gate,
            to_up,
            *flat(down_in[-1:]),
            *flat(gate_in),
            *flat(up_in),
        ),
        [SMEM] + [HBM] * (5 + shape[-1] + 2 * sum(shape)),
        [
            pltpu.VMEM((ffw, part), BF),
            full_w,
            full_w,
            pltpu.SemaphoreType.DMA((8, groups)),
            pltpu.VMEM((total, ffw), BF),
            pltpu.VMEM((total, part), BF),
            pltpu.VMEM((total, ffw), F32),
            pltpu.VMEM((total, ffw), F32),
            pltpu.VMEM((total, ffw), F32),
        ],
        flops=2 * one + 2 * one // groups,
        moved=4 * width * ffw + 4 * total * width + 14 * total * ffw,
    )
    back_last = exchange(back, owners, "exp")
    output, stream_grad = call(
        functools.partial(final_kernel, owners, cap),
        (sds((tokens, width)), sds((tokens, width))),
        (place, ids, weights, gain, stream, cot, back_first, back_last),
        [SMEM] + [VMEM] * 7,
        [pltpu.VMEM((tokens, width), F32)],
        flops=6 * total * tokens * width,
        moved=4 * total * width + 8 * tokens * width,
        vmem=16,
        held=True,
    )
    return (output[None], stream_grad[None])


def solution(mesh):
    placed = (
        P("exp", "seq", None),
        P("exp", "seq", None),
        P("exp", "seq", None),
        P("exp", "seq", None),
        P(),
        P("exp", "seq", None),
        P("exp", "seq", None),
        P("exp", None, "seq"),
        P("exp", "seq", None),
        P("exp", "seq", None),
        P("exp", "seq", None),
    )
    return jax.shard_map(
        per_device,
        mesh=mesh,
        in_specs=placed,
        out_specs=(P("exp", "seq", None), P("exp", "seq", None)),
        check_vma=False,
    )
```

```python
import functools

import jax
import jax.numpy as jnp
from jax import lax
from jax.experimental import pallas as pl
from jax.experimental.pallas import tpu as pltpu
from jax.sharding import PartitionSpec as P

HD = 128
BF = jnp.bfloat16
F32 = jnp.float32
MIB = 1 << 20
HBM = pl.BlockSpec(memory_space=pltpu.HBM)
VMEM = pl.BlockSpec(memory_space=pltpu.VMEM)
SMEM = pl.BlockSpec(memory_space=pltpu.SMEM)
NT = (((1,), (1,)), ((), ()))
NN = (((1,), (0,)), ((), ()))


def mm(a, b, dims):
    return lax.dot_general(a, b, dims, preferred_element_type=F32)


def whole(array):
    return pl.BlockSpec(array.shape, lambda i: (0,) * len(array.shape))


def call(kernel, outs, args, in_specs, scratch=(), flops=0, moved=0, vmem=56, after=(), held=False):
    count, extra = len(args), len(after)

    def body(*refs):
        kernel(*refs[:count], *refs[count + extra :])

    return pl.pallas_call(
        body,
        grid=() if held else (1,),
        out_shape=outs,
        in_specs=[
            *[
                whole(arg) if spec is VMEM and not held else spec
                for arg, spec in zip(args, in_specs)
            ],
            *[HBM] * extra,
        ],
        out_specs=jax.tree.map(lambda out: VMEM if held else whole(out), outs),
        scratch_shapes=list(scratch),
        compiler_params=pltpu.CompilerParams(vmem_limit_bytes=vmem * MIB),
        cost_estimate=pl.CostEstimate(flops=flops, bytes_accessed=moved, transcendentals=0),
    )(*args, *after)


def gated(array, *first):
    return lax.optimization_barrier((array, *first))[0] if first else array


def sds(shape, dtype=BF):
    return jax.ShapeDtypeStruct(shape, dtype)


def pack_kernel(q_ref, k_ref, v_ref, o_ref):
    rows = q_ref.shape[0]
    o_ref[0, 0:rows] = q_ref[...]
    o_ref[0, rows : 2 * rows] = k_ref[...]
    o_ref[0, 2 * rows : 3 * rows] = v_ref[...]


def pack(q, k, v, groups):
    rows, width = q.shape
    part = width // groups
    spec = pl.BlockSpec((rows, part), lambda g: (0, g))
    return pl.pallas_call(
        pack_kernel,
        grid=(groups,),
        out_shape=sds((groups, 3 * rows, part)),
        in_specs=[spec] * 3,
        out_specs=pl.BlockSpec((1, 3 * rows, part), lambda g: (g, 0, 0)),
        cost_estimate=pl.CostEstimate(
            flops=0, bytes_accessed=12 * rows * width, transcendentals=0
        ),
    )(q, k, v)


def attend_head(blocks, query_of, keys, vals, store):
    rows = keys.shape[0] // blocks
    scale = HD ** (-0.5)
    row_ids = lax.broadcasted_iota(jnp.int32, (rows, rows), 0)
    col_ids = lax.broadcasted_iota(jnp.int32, (rows, rows), 1)
    keep = col_ids <= row_ids
    for b in range(blocks):
        query = query_of(b)
        end = b * rows
        diag = mm(query, keys[end : end + rows], NT) * scale
        diag = jnp.where(keep, diag, -jnp.inf)
        top = jnp.max(diag, axis=-1, keepdims=True)
        if b:
            early = mm(query, keys[:end], NT) * scale
            top = jnp.maximum(top, jnp.max(early, axis=-1, keepdims=True))
        diag = jnp.exp(diag - top)
        total = jnp.sum(diag, axis=-1, keepdims=True)
        if b:
            early = jnp.exp(early - top)
            total = total + jnp.sum(early, axis=-1, keepdims=True)
        inverse = 1.0 / total
        ctx = mm((diag * inverse).astype(BF), vals[end : end + rows], NN)
        if b:
            ctx = ctx + mm((early * inverse).astype(BF), vals[:end], NN)
        store(b, ctx.astype(BF))


def attend_kernel(x_ref, o_ref):
    blocks, three, hd = x_ref.shape
    rows = three // 3

    def store(b, ctx):
        o_ref[b] = ctx

    attend_head(
        blocks,
        lambda b: x_ref[b, 0:rows, :],
        x_ref[:, rows : 2 * rows, :].reshape(blocks * rows, hd),
        x_ref[:, 2 * rows : 3 * rows, :].reshape(blocks * rows, hd),
        store,
    )


def attend(x):
    blocks, three, part = x.shape
    rows = three // 3
    length = blocks * rows
    return pl.pallas_call(
        attend_kernel,
        grid=(part // HD,),
        out_shape=sds((blocks, rows, part)),
        in_specs=[pl.BlockSpec((blocks, three, HD), lambda h: (0, 0, h))],
        out_specs=pl.BlockSpec((blocks, rows, HD), lambda h: (0, 0, h)),
        compiler_params=pltpu.CompilerParams(vmem_limit_bytes=40 * MIB),
        cost_estimate=pl.CostEstimate(
            flops=4 * length * length * part,
            bytes_accessed=8 * length * part,
            transcendentals=length * length * part // HD,
        ),
    )(x)


INNER, COLS, PLANE, ATTEND = 0, 1, 5, 6


def halves_kernel(place_ref, q_ref, k_ref, v_ref, first_ref, second_ref):
    rows, width = q_ref.shape
    half = width // 2

    def copy(lower, upper):
        for i, ref in enumerate((q_ref, k_ref, v_ref)):
            lower[i * rows : (i + 1) * rows] = ref[:, :half]
            upper[i * rows : (i + 1) * rows] = ref[:, half:]

    @pl.when(place_ref[PLANE] < 2)
    def _():
        copy(first_ref, second_ref)

    @pl.when(place_ref[PLANE] >= 2)
    def _():
        copy(second_ref, first_ref)


def middle_kernel(place_ref, own_in, near_in, mid_in, far_in, *refs):
    *outs, x_ref, ctx_ref, sems = refs
    blocks, three, half = x_ref.shape
    rows = three // 3

    @pl.when(place_ref[INNER] == 1)
    def _():
        copies = [
            pltpu.make_async_copy(ref, x_ref.at[place_ref[ATTEND + i]], sems.at[i])
            for i, ref in enumerate((own_in, near_in, mid_in, far_in))
        ]
        for copy in copies:
            copy.start()
        for copy in copies:
            copy.wait()

        def step(i, carry):
            for j in range(2):
                cols = pl.ds(pl.multiple_of((2 * i + j) * HD, HD), HD)

                def store(b, ctx, cols=cols):
                    ctx_ref[b, :, cols] = ctx

                attend_head(
                    blocks,
                    lambda b, cols=cols: x_ref[b, 0:rows, cols],
                    x_ref[:, rows : 2 * rows, cols].reshape(blocks * rows, HD),
                    x_ref[:, 2 * rows : 3 * rows, cols].reshape(blocks * rows, HD),
                    store,
                )
            return carry

        lax.fori_loop(0, half // HD // 2, step, 0)
        for i, out in enumerate(outs):
            out[...] = ctx_ref[place_ref[ATTEND + i]]


def line_of_four(place, queries, keys, values, gate, up, down, cot_rows):
    rows, width = queries.shape
    half = width // 2
    block = sds((3 * rows, half))
    first, second = call(
        halves_kernel,
        (block, block),
        (place, queries, keys, values),
        [SMEM, VMEM, VMEM, VMEM],
        moved=12 * rows * width,
    )
    gate_end = send(gate, OUTWARD)
    up_end = send(up, OUTWARD)
    down_end = send(down, OUTWARD, gate_end)
    near = send(first, INWARD)
    mid = send(second, MIDDLE)
    far = send(second, [(0, 2), (3, 1)])
    piece = sds((rows, half))
    pieces = call(
        middle_kernel,
        (piece,) * 4,
        (place, first, near, mid, far),
        [SMEM] + [HBM] * 4,
        [
            pltpu.VMEM((4, 3 * rows, half), BF),
            pltpu.VMEM((4, rows, half), BF),
            pltpu.SemaphoreType.DMA((4,)),
        ],
        flops=64 * rows * rows * half,
        moved=32 * rows * half,
        after=(gate_end, up_end, cot_rows),
    )
    gate_mid = send(gate, MIDDLE, near, mid, far)
    up_mid = send(up, MIDDLE, near, mid, far)
    down_mid = send(down, MIDDLE, gate_mid)
    gate_inner = send(gate, INWARD, near, far, gate_end, up_end)
    up_inner = send(up, INWARD, gate_inner, down_end)
    down_inner = send(down, INWARD, up_inner)
    own, near, mid, far = lax.optimization_barrier((*pieces, gate_inner))[:4]
    mid = send(mid, MIDDLE)
    far = send(far, [(2, 0), (1, 3)])
    up_far = send(up_mid, OUTWARD, own)
    near = send(near, OUTWARD, up_far)
    gate_mid_near = send(gate_inner, MIDDLE)
    gate_far = send(gate_mid, OUTWARD, own)
    up_mid_near = send(up_inner, MIDDLE, gate_far)
    down_mid_near = send(down_inner, MIDDLE, up_far)
    gate_far_near = send(gate_mid_near, OUTWARD)
    up_far_near = send(up_mid_near, OUTWARD, gate_far_near)
    down_far = send(down_mid, OUTWARD, gate_far_near)
    down_far_near = send(down_mid_near, OUTWARD, up_far_near)
    norm_after = (down_mid, gate_mid_near, gate_far)
    up_after = (down_mid_near,)
    gate_in = [
        [gate],
        [gate_inner, gate_end],
        [gate_mid, gate_far],
        [gate_mid_near, gate_far_near],
    ]
    up_in = [[up], [up_inner, up_end], [up_mid, up_far], [up_mid_near, up_far_near]]
    down_in = [
        [down],
        [down_inner, down_end],
        [down_mid, down_far],
        [down_mid_near, down_far_near],
    ]
    return (own, near, mid, far), gate_in, up_in, down_in, norm_after, up_after


def join_middle(place_ref, pieces, ctx_ref):
    own, near, mid, far = pieces
    half = own.shape[1]
    for plane, (lower, upper) in enumerate(((near, far), (own, mid), (mid, own), (far, near))):

        @pl.when(place_ref[PLANE] == plane)
        def _(lower=lower, upper=upper):
            ctx_ref[:, :half] = lower[...]
            ctx_ref[:, half:] = upper[...]


def join_groups(place_ref, pieces, ctx_ref):
    (ctx,) = pieces
    groups, _, part = ctx.shape
    for g in range(groups):
        ctx_ref[:, g * part : (g + 1) * part] = ctx[g]


def slot_rows(ids_t, owners, cap):
    tokens = ids_t.shape[1]
    experts = lax.broadcasted_iota(jnp.int32, (owners, tokens), 0)
    first = (experts == ids_t[0:1]).astype(F32)
    second = (experts == ids_t[1:2]).astype(F32)
    src = lax.broadcasted_iota(jnp.int32, (tokens, tokens), 0)
    dst = lax.broadcasted_iota(jnp.int32, (tokens, tokens), 1)
    earlier = (src < dst).astype(F32).astype(BF)
    count = mm((first + second).astype(BF), earlier, NN)
    slot0 = jnp.sum(first * count, axis=0, keepdims=True).astype(jnp.int32)
    slot1 = jnp.sum(second * count, axis=0, keepdims=True).astype(jnp.int32)
    return ids_t[0:1] * cap + slot0, ids_t[1:2] * cap + slot1


def slot_cols(ids, owners, cap):
    tokens = ids.shape[0]
    experts = lax.broadcasted_iota(jnp.int32, (tokens, owners), 1)
    first = (experts == ids[:, 0:1]).astype(F32)
    second = (experts == ids[:, 1:2]).astype(F32)
    dst = lax.broadcasted_iota(jnp.int32, (tokens, tokens), 0)
    src = lax.broadcasted_iota(jnp.int32, (tokens, tokens), 1)
    earlier = (src < dst).astype(F32).astype(BF)
    count = mm(earlier, (first + second).astype(BF), NN)
    slot0 = jnp.sum(first * count, axis=1, keepdims=True).astype(jnp.int32)
    slot1 = jnp.sum(second * count, axis=1, keepdims=True).astype(jnp.int32)
    return ids[:, 0:1] * cap + slot0, ids[:, 1:2] * cap + slot1


def one_hot(hit):
    return jnp.where(hit, 1.0, 0.0).astype(BF)


def send_cot_kernel(owners, cap, ids_ref, w_ref, cot_ref, o_ref):
    tokens = cot_ref.shape[0]
    at0, at1 = slot_rows(ids_ref[...], owners, cap)
    rows = lax.broadcasted_iota(jnp.int32, (owners * cap, tokens), 0)
    cot = cot_ref[...].astype(F32)
    o_ref[...] = (
        mm(one_hot(rows == at0), (w_ref[:, 0:1] * cot).astype(BF), NN)
        + mm(one_hot(rows == at1), (w_ref[:, 1:2] * cot).astype(BF), NN)
    ).astype(BF)


def norm_kernel(owners, cap, join, place_ref, ids_ref, resid_ref, gain_ref, *refs):
    *pieces, stream_ref, o_ref, ctx_ref = refs
    tokens, width = resid_ref.shape
    join(place_ref, pieces, ctx_ref)
    stream = (resid_ref[...].astype(F32) + ctx_ref[...].astype(F32)).astype(BF)
    stream_ref[...] = stream
    stream = stream.astype(F32)
    square = jnp.sum(stream * stream, axis=-1, keepdims=True)
    inv_rms = lax.rsqrt(square / width + 1e-05)
    at0, at1 = slot_rows(ids_ref[...], owners, cap)
    rows = lax.broadcasted_iota(jnp.int32, (owners * cap, tokens), 0)
    pick = one_hot((rows == at0) | (rows == at1))
    normed = ((stream_ref[...].astype(F32) * inv_rms) * gain_ref[...]).astype(BF)
    o_ref[...] = mm(pick, normed, NN).astype(BF)


def fetch(inner, choices, dst, sem):
    if len(choices) == 1:
        pltpu.make_async_copy(choices[0], dst, sem).start()
        return

    @pl.when(inner == 1)
    def _():
        pltpu.make_async_copy(choices[0], dst, sem).start()

    @pl.when(inner == 0)
    def _():
        pltpu.make_async_copy(choices[1], dst, sem).start()


def arrived(choices, dst, sem):
    pltpu.make_async_copy(choices[0], dst, sem).wait()


def regroup(refs, shape):
    refs = list(refs)
    return [[refs.pop(0) for _ in range(size)] for size in shape], refs


def cols_of(place_ref, slot, part):
    return pl.ds(pl.multiple_of(place_ref[COLS + slot] * part, part), part)


def gate_kernel(shape, place_ref, x_ref, *refs):
    slots = len(shape)
    gate_in, refs = regroup(refs, shape)
    o_ref, gate_w, sems = refs
    inner = place_ref[INNER]
    for j in range(slots):
        fetch(inner, gate_in[j], gate_w.at[j], sems.at[j])
    o_ref[...] = by_slots(place_ref, x_ref, gate_in, gate_w, sems)


def by_slots(place_ref, x_ref, weight_in, weight, sems):
    slots, _, part = weight.shape
    total = None
    for j in range(slots):
        rows = x_ref[:, cols_of(place_ref, j, part)]
        arrived(weight_in[j], weight.at[j], sems.at[j])
        term = mm(rows, weight[j], NT)
        total = term if total is None else total + term
    return total


def up_kernel(shape, place_ref, x_ref, gate_ref, *refs):
    slots = len(shape)
    up_in, refs = regroup(refs, shape)
    hidden_ref, to_gate_ref, to_up_ref, up_w, sems = refs
    inner = place_ref[INNER]
    for j in range(slots):
        fetch(inner, up_in[j], up_w.at[j], sems.at[j])
    gate = gate_ref[...]
    sigma = 1.0 / (1.0 + jnp.exp(-gate))
    silu = gate * sigma
    to_up_ref[...] = silu
    to_gate_ref[...] = sigma * (1.0 + gate * (1.0 - sigma))
    up = by_slots(place_ref, x_ref, up_in, up_w, sems)
    hidden_ref[...] = (to_up_ref[...] * up).astype(BF)
    to_gate_ref[...] = up * to_gate_ref[...]


def down_kernel(shape, place_ref, hidden_ref, cot_ref, *refs):
    slots = len(shape)
    down_in, refs = regroup(refs, shape)
    out_ref, d_hidden_ref, down_w, sems = refs
    part = down_w.shape[2]
    inner = place_ref[INNER]
    for j in range(slots):
        fetch(inner, down_in[j], down_w.at[j], sems.at[j])
    total = None
    for j in range(slots):
        rows = cot_ref[:, cols_of(place_ref, j, part)]
        arrived(down_in[j], down_w.at[j], sems.at[j])
        term = mm(rows, down_w[j], NT)
        total = term if total is None else total + term
        out_ref[:, j * part : (j + 1) * part] = mm(hidden_ref[...], down_w[j], NN).astype(BF)
    d_hidden_ref[...] = total


def grad_kernel(
    shape, place_ref, hidden_in, cot_in, d_hidden_in, to_gate_in, to_up_in, *refs
):
    slots = len(shape) - 1
    down_in, refs = regroup(refs, shape[-1:])
    gate_in, refs = regroup(refs, shape[:-1])
    up_in, refs = regroup(refs, shape[:-1])
    o_ref, down_w, gate_w, up_w, sems = refs[:5]
    hidden_ref, cot_ref, d_hidden_ref, to_gate_ref, to_up_ref = refs[5:]
    part = down_w.shape[1]
    inner = place_ref[INNER]
    last = place_ref[COLS + cot_in.shape[1] // part - 1]
    pairs = [
        (cot_in.at[:, pl.ds(pl.multiple_of(last * part, part), part)], cot_ref),
        (d_hidden_in, d_hidden_ref),
        (to_gate_in, to_gate_ref),
        (to_up_in, to_up_ref),
        (hidden_in, hidden_ref),
    ]
    fetch(inner, down_in[0], down_w, sems.at[2, 0])
    copies = [
        pltpu.make_async_copy(src, dst, sems.at[3 + i, 0]) for i, (src, dst) in enumerate(pairs)
    ]
    for copy in copies:
        copy.start()
    for j in range(slots):
        fetch(inner, gate_in[j], gate_w.at[j], sems.at[0, j])
        fetch(inner, up_in[j], up_w.at[j], sems.at[1, j])
    arrived(down_in[0], down_w, sems.at[2, 0])
    for copy in copies:
        copy.wait()
    d_hidden = d_hidden_ref[...] + mm(cot_ref[...], down_w[...], NT)
    d_gate = (d_hidden * to_gate_ref[...]).astype(BF)
    d_up = (d_hidden * to_up_ref[...]).astype(BF)
    o_ref[:, slots * part :] = mm(hidden_ref[...], down_w[...], NN).astype(BF)
    for j in range(slots):
        arrived(gate_in[j], gate_w.at[j], sems.at[0, j])
        arrived(up_in[j], up_w.at[j], sems.at[1, j])
        o_ref[:, j * part : (j + 1) * part] = (
            mm(d_gate, gate_w[j], NN) + mm(d_up, up_w[j], NN)
        ).astype(BF)


def final_kernel(
    owners,
    cap,
    place_ref,
    ids_ref,
    w_ref,
    gain_ref,
    stream_ref,
    cot_ref,
    first_ref,
    last_ref,
    output_ref,
    grad_ref,
    d_normed_ref,
):
    tokens, width = stream_ref.shape
    done = first_ref.shape[1]
    part = width - done
    slots = width // part
    at0, at1 = slot_cols(ids_ref[...], owners, cap)
    rows = lax.broadcasted_iota(jnp.int32, (tokens, owners * cap), 1)
    pick0, pick1 = one_hot(rows == at0), one_hot(rows == at1)
    both = pick0 + pick1
    w0, w1 = w_ref[:, 0:1], w_ref[:, 1:2]
    square = jnp.zeros((tokens, 1), F32)
    dot = jnp.zeros((tokens, 1), F32)
    for j in range(slots):
        cols = cols_of(place_ref, j, part)
        if j < slots - 1:
            pairs = first_ref[:, j * part : (j + 1) * part]
        else:
            pairs = last_ref[:, width:]
        stream = stream_ref[:, cols].astype(F32)
        mixed = w0 * mm(pick0, pairs, NN) + w1 * mm(pick1, pairs, NN)
        output_ref[:, cols] = (stream + mixed).astype(BF)
        grads = last_ref[:, j * part : (j + 1) * part]
        gained = mm(both, grads, NN) * gain_ref[:, cols]
        d_normed_ref[:, cols] = gained
        square = square + jnp.sum(stream * stream, axis=-1, keepdims=True)
        dot = dot + jnp.sum(gained * stream, axis=-1, keepdims=True)
    inv_rms = lax.rsqrt(square / width + 1e-05)
    mean = dot * inv_rms / width
    unit_rows = stream_ref[...].astype(F32) * inv_rms
    d_stream = inv_rms * (d_normed_ref[...] - unit_rows * mean)
    grad_ref[...] = (cot_ref[...].astype(F32) + d_stream).astype(BF)


MIDDLE = [(1, 2), (2, 1)]
OUTWARD = [(1, 0), (2, 3)]
INWARD = [(0, 1), (3, 2)]


def gather_all(shard, groups):
    whole_weight = lax.all_gather(shard, "seq", axis=0)
    return [[whole_weight[j]] for j in range(groups)]


def send(array, pairs, *first):
    return lax.ppermute(gated(array, *first), "seq", pairs)


def places(groups):
    if groups == 4:
        own = lax.axis_index("seq")
        table = jnp.array(
            [
                [0, 0, 1, 2, 3, 0, 0, 0, 0, 0],
                [1, 1, 0, 2, 3, 1, 1, 0, 2, 3],
                [1, 2, 3, 1, 0, 2, 2, 3, 1, 0],
                [0, 3, 2, 1, 0, 3, 0, 0, 0, 0],
            ],
            jnp.int32,
        )
        return table[own]
    return jnp.arange(-1, groups, dtype=jnp.int32)


def exchange(rows, owners, axis):
    total, width = rows.shape
    rows = rows.reshape(owners, total // owners, width)
    rows = lax.all_to_all(rows, axis, split_axis=0, concat_axis=0, tiled=True)
    return rows.reshape(total, width)


def flat(slots):
    return [ref for choices in slots for ref in choices]


def per_device(
    queries,
    keys,
    values,
    resid,
    norm_gain,
    w_gate,
    w_up,
    w_down,
    expert_ids,
    route_weights,
    cotangent,
):
    groups = lax.axis_size("seq")
    owners = lax.axis_size("exp")
    tokens, width = queries.shape[1:]
    ffw = w_gate.shape[2]
    part = width // groups
    cap = max(2, tokens * 10 // (4 * owners))
    total = owners * cap
    ids = expert_ids[0]
    ids_t = ids.T
    weights = route_weights[0]
    gain = norm_gain[None]
    cot = cotangent[0]
    place = places(groups)

    one = 2 * total * width * ffw
    send_cot = call(
        functools.partial(send_cot_kernel, owners, cap),
        sds((total, width)),
        (ids_t, weights, cot),
        [VMEM] * 3,
        flops=4 * total * tokens * width,
        moved=2 * (total + tokens) * width,
    )
    cot_rows = exchange(send_cot, owners, "exp")
    shards = (w_gate[0].T, w_up[0].T, w_down[0])
    if groups == 4:
        join = join_middle
        pieces, gate_in, up_in, down_in, norm_after, up_after = line_of_four(
            place, queries[0], keys[0], values[0], *shards, cot_rows
        )
    else:
        join = join_groups
        gate_in, up_in, down_in = [gather_all(shard, groups) for shard in shards]
        packed = pack(queries[0], keys[0], values[0], groups)
        heads = lax.all_to_all(packed, "seq", split_axis=0, concat_axis=0, tiled=True)
        ctx = attend(heads)
        pieces = (lax.all_to_all(ctx, "seq", split_axis=0, concat_axis=0, tiled=True),)
        norm_after = up_after = ()
    shape = [len(choices) for choices in gate_in]

    stream, send_rows = call(
        functools.partial(norm_kernel, owners, cap, join),
        (sds((tokens, width)), sds((total, width))),
        (place, ids_t, resid[0], gain, *pieces),
        [SMEM] + [VMEM] * (3 + len(pieces)),
        [pltpu.VMEM((tokens, width), BF)],
        flops=2 * total * tokens * width,
        moved=2 * (total + 3 * tokens) * width,
        after=norm_after,
    )
    rows = exchange(send_rows, owners, "exp")

    full_w = pltpu.VMEM((groups, ffw, part), BF)
    gate_pre = call(
        functools.partial(gate_kernel, shape),
        sds((total, ffw), F32),
        (place, rows, *flat(gate_in)),
        [SMEM, VMEM] + [HBM] * sum(shape),
        [full_w, pltpu.SemaphoreType.DMA((groups,))],
        flops=one,
        moved=2 * width * ffw + 2 * total * width + 4 * total * ffw,
    )
    hidden, to_gate, to_up = call(
        functools.partial(up_kernel, shape),
        (sds((total, ffw)), sds((total, ffw), F32), sds((total, ffw), F32)),
        (place, rows, gate_pre, *flat(up_in)),
        [SMEM, VMEM, VMEM] + [HBM] * sum(shape),
        [full_w, pltpu.SemaphoreType.DMA((groups,))],
        flops=one,
        moved=2 * width * ffw + 2 * total * width + 14 * total * ffw,
        after=up_after,
    )
    out_first, d_hidden = call(
        functools.partial(down_kernel, shape[:-1]),
        (sds((total, width - part)), sds((total, ffw), F32)),
        (place, hidden, cot_rows, *flat(down_in[:-1])),
        [SMEM, VMEM, VMEM] + [HBM] * sum(shape[:-1]),
        [
            pltpu.VMEM((groups - 1, ffw, part), BF),
            pltpu.SemaphoreType.DMA((groups - 1,)),
        ],
        flops=2 * one * (groups - 1) // groups,
        moved=2 * width * ffw + 4 * total * width + 6 * total * ffw,
    )
    back_first = exchange(out_first, owners, "exp")
    back = call(
        functools.partial(grad_kernel, [*shape, shape[-1]]),
        sds((total, width + part)),
        (
            place,
            hidden,
            cot_rows,
            d_hidden,
            to_gate,
            to_up,
            *flat(down_in[-1:]),
            *flat(gate_in),
            *flat(up_in),
        ),
        [SMEM] + [HBM] * (5 + shape[-1] + 2 * sum(shape)),
        [
            pltpu.VMEM((ffw, part), BF),
            full_w,
            full_w,
            pltpu.SemaphoreType.DMA((8, groups)),
            pltpu.VMEM((total, ffw), BF),
            pltpu.VMEM((total, part), BF),
            pltpu.VMEM((total, ffw), F32),
            pltpu.VMEM((total, ffw), F32),
            pltpu.VMEM((total, ffw), F32),
        ],
        flops=2 * one + 2 * one // groups,
        moved=4 * width * ffw + 4 * total * width + 14 * total * ffw,
    )
    back_last = exchange(back, owners, "exp")
    output, stream_grad = call(
        functools.partial(final_kernel, owners, cap),
        (sds((tokens, width)), sds((tokens, width))),
        (place, ids, weights, gain, stream, cot, back_first, back_last),
        [SMEM] + [VMEM] * 7,
        [pltpu.VMEM((tokens, width), F32)],
        flops=6 * total * tokens * width,
        moved=4 * total * width + 8 * tokens * width,
        vmem=16,
        held=True,
    )
    return (output[None], stream_grad[None])


def solution(mesh):
    placed = (
        P("exp", "seq", None),
        P("exp", "seq", None),
        P("exp", "seq", None),
        P("exp", "seq", None),
        P(),
        P("exp", "seq", None),
        P("exp", "seq", None),
        P("exp", None, "seq"),
        P("exp", "seq", None),
        P("exp", "seq", None),
        P("exp", "seq", None),
    )
    return jax.shard_map(
        per_device,
        mesh=mesh,
        in_specs=placed,
        out_specs=(P("exp", "seq", None), P("exp", "seq", None)),
        check_vma=False,
    )
```

```python
import functools

import jax
import jax.numpy as jnp
from jax import lax
from jax.experimental import pallas as pl
from jax.experimental.pallas import tpu as pltpu
from jax.sharding import PartitionSpec as P

HD = 128
BF = jnp.bfloat16
F32 = jnp.float32
MIB = 1 << 20
HBM = pl.BlockSpec(memory_space=pltpu.HBM)
VMEM = pl.BlockSpec(memory_space=pltpu.VMEM)
SMEM = pl.BlockSpec(memory_space=pltpu.SMEM)
NT = (((1,), (1,)), ((), ()))
NN = (((1,), (0,)), ((), ()))


def mm(a, b, dims):
    return lax.dot_general(a, b, dims, preferred_element_type=F32)


def whole(array):
    return pl.BlockSpec(array.shape, lambda i: (0,) * len(array.shape))


def call(kernel, outs, args, in_specs, scratch=(), flops=0, moved=0, vmem=56, after=(), held=False):
    count, extra = len(args), len(after)

    def body(*refs):
        kernel(*refs[:count], *refs[count + extra :])

    return pl.pallas_call(
        body,
        grid=() if held else (1,),
        out_shape=outs,
        in_specs=[
            *[
                whole(arg) if spec is VMEM and not held else spec
                for arg, spec in zip(args, in_specs)
            ],
            *[HBM] * extra,
        ],
        out_specs=jax.tree.map(lambda out: VMEM if held else whole(out), outs),
        scratch_shapes=list(scratch),
        compiler_params=pltpu.CompilerParams(vmem_limit_bytes=vmem * MIB),
        cost_estimate=pl.CostEstimate(flops=flops, bytes_accessed=moved, transcendentals=0),
    )(*args, *after)


def gated(array, *first):
    return lax.optimization_barrier((array, *first))[0] if first else array


def sds(shape, dtype=BF):
    return jax.ShapeDtypeStruct(shape, dtype)


def pack_kernel(q_ref, k_ref, v_ref, o_ref):
    rows = q_ref.shape[0]
    o_ref[0, 0:rows] = q_ref[...]
    o_ref[0, rows : 2 * rows] = k_ref[...]
    o_ref[0, 2 * rows : 3 * rows] = v_ref[...]


def pack(q, k, v, groups):
    rows, width = q.shape
    part = width // groups
    spec = pl.BlockSpec((rows, part), lambda g: (0, g))
    return pl.pallas_call(
        pack_kernel,
        grid=(groups,),
        out_shape=sds((groups, 3 * rows, part)),
        in_specs=[spec] * 3,
        out_specs=pl.BlockSpec((1, 3 * rows, part), lambda g: (g, 0, 0)),
        cost_estimate=pl.CostEstimate(
            flops=0, bytes_accessed=12 * rows * width, transcendentals=0
        ),
    )(q, k, v)


def attend_head(query, keys, vals, store):
    length = keys.shape[0]
    block = min(512, length)
    scale = HD ** (-0.5)
    row_ids = lax.broadcasted_iota(jnp.int32, (block, block), 0)
    col_ids = lax.broadcasted_iota(jnp.int32, (block, block), 1)
    keep = col_ids <= row_ids
    for start in range(0, length, block):
        end = start + block
        scores = mm(query[start:end], keys[:end], NT) * scale
        diag = jnp.where(keep, scores[:, start:], -jnp.inf)
        scores = jnp.concatenate([scores[:, :start], diag], axis=1) if start else diag
        exps = jnp.exp(scores - jnp.max(scores, axis=-1, keepdims=True))
        inverse = 1.0 / jnp.sum(exps, axis=-1, keepdims=True)
        store(start, end, mm((exps * inverse).astype(BF), vals[:end], NN).astype(BF))


def attend_columns(x_ref, cols, o_ref):
    blocks, three, _ = x_ref.shape
    rows = three // 3
    query, keys, vals = [
        x_ref[:, i * rows : (i + 1) * rows, cols].reshape(blocks * rows, HD) for i in range(3)
    ]

    def store(start, end, ctx):
        first, last = start // rows, end // rows
        o_ref[first:last, :, cols] = ctx.reshape(last - first, rows, HD)

    attend_head(query, keys, vals, store)


def attend_kernel(x_ref, o_ref):
    attend_columns(x_ref, slice(0, HD), o_ref)


def attend(x):
    blocks, three, part = x.shape
    rows = three // 3
    length = blocks * rows
    return pl.pallas_call(
        attend_kernel,
        grid=(part // HD,),
        out_shape=sds((blocks, rows, part)),
        in_specs=[pl.BlockSpec((blocks, three, HD), lambda h: (0, 0, h))],
        out_specs=pl.BlockSpec((blocks, rows, HD), lambda h: (0, 0, h)),
        compiler_params=pltpu.CompilerParams(vmem_limit_bytes=40 * MIB),
        cost_estimate=pl.CostEstimate(
            flops=4 * length * length * part,
            bytes_accessed=8 * length * part,
            transcendentals=length * length * part // HD,
        ),
    )(x)


INNER, COLS, PLANE, ATTEND = 0, 1, 5, 6


def halves_kernel(place_ref, q_ref, k_ref, v_ref, first_ref, second_ref):
    rows, width = q_ref.shape
    half = width // 2

    def copy(lower, upper):
        for i, ref in enumerate((q_ref, k_ref, v_ref)):
            lower[i * rows : (i + 1) * rows] = ref[:, :half]
            upper[i * rows : (i + 1) * rows] = ref[:, half:]

    @pl.when(place_ref[PLANE] < 2)
    def _():
        copy(first_ref, second_ref)

    @pl.when(place_ref[PLANE] >= 2)
    def _():
        copy(second_ref, first_ref)


def middle_kernel(place_ref, own_in, near_in, mid_in, far_in, *refs):
    *outs, x_ref, ctx_ref, sems = refs
    blocks, three, half = x_ref.shape
    rows = three // 3

    @pl.when(place_ref[INNER] == 1)
    def _():
        copies = [
            pltpu.make_async_copy(ref, x_ref.at[place_ref[ATTEND + i]], sems.at[i])
            for i, ref in enumerate((own_in, near_in, mid_in, far_in))
        ]
        for copy in copies:
            copy.start()
        for copy in copies:
            copy.wait()

        def step(i, carry):
            for j in range(2):
                cols = pl.ds(pl.multiple_of((2 * i + j) * HD, HD), HD)
                attend_columns(x_ref, cols, ctx_ref)
            return carry

        lax.fori_loop(0, half // HD // 2, step, 0)
        for i, out in enumerate(outs):
            out[...] = ctx_ref[place_ref[ATTEND + i]]


def line_of_four(place, queries, keys, values, gate, up, down, cot_rows):
    rows, width = queries.shape
    half = width // 2
    block = sds((3 * rows, half))
    first, second = call(
        halves_kernel,
        (block, block),
        (place, queries, keys, values),
        [SMEM, VMEM, VMEM, VMEM],
        moved=12 * rows * width,
    )
    gate_end = send(gate, OUTWARD)
    up_end = send(up, OUTWARD)
    down_end = send(down, OUTWARD, gate_end)
    near = send(first, INWARD)
    mid = send(second, MIDDLE)
    far = send(second, [(0, 2), (3, 1)])
    piece = sds((rows, half))
    pieces = call(
        middle_kernel,
        (piece,) * 4,
        (place, first, near, mid, far),
        [SMEM] + [HBM] * 4,
        [
            pltpu.VMEM((4, 3 * rows, half), BF),
            pltpu.VMEM((4, rows, half), BF),
            pltpu.SemaphoreType.DMA((4,)),
        ],
        flops=64 * rows * rows * half,
        moved=32 * rows * half,
        after=(gate_end, up_end, cot_rows),
    )
    gate_mid = send(gate, MIDDLE, near, mid, far)
    up_mid = send(up, MIDDLE, near, mid, far)
    gate_inner = send(gate, INWARD, near, far, gate_end, up_end)
    up_inner = send(up, INWARD, near, far, gate_end, up_end)
    down_inner = send(down, INWARD, gate_inner)
    own, near, mid, far = lax.optimization_barrier((*pieces, gate_inner, up_inner, down_end))[:4]
    mid = send(mid, MIDDLE)
    far = send(far, [(2, 0), (1, 3)])
    up_far = send(up_mid, OUTWARD, own)
    near = send(near, OUTWARD, up_far)
    gate_mid_near = send(gate_inner, MIDDLE)
    gate_far = send(gate_mid, OUTWARD, own)
    up_mid_near = send(up_inner, MIDDLE, own)
    down_mid = send(down, MIDDLE, gate_mid_near)
    down_mid_near = send(down_inner, MIDDLE, up_mid_near)
    gate_far_near = send(gate_mid_near, OUTWARD)
    up_far_near = send(up_mid_near, OUTWARD, gate_far_near)
    down_far = send(down_mid, OUTWARD, gate_far_near)
    down_far_near = send(down_mid_near, OUTWARD, up_far_near)
    norm_after = (gate_mid_near, gate_far)
    up_after = (down_mid_near,)
    gate_in = [
        [gate],
        [gate_inner, gate_end],
        [gate_mid, gate_far],
        [gate_mid_near, gate_far_near],
    ]
    up_in = [[up], [up_inner, up_end], [up_mid, up_far], [up_mid_near, up_far_near]]
    down_in = [
        [down],
        [down_inner, down_end],
        [down_mid, down_far],
        [down_mid_near, down_far_near],
    ]
    return (own, near, mid, far), gate_in, up_in, down_in, norm_after, up_after


def join_middle(place_ref, pieces, ctx_ref):
    own, near, mid, far = pieces
    half = own.shape[1]
    for plane, (lower, upper) in enumerate(((near, far), (own, mid), (mid, own), (far, near))):

        @pl.when(place_ref[PLANE] == plane)
        def _(lower=lower, upper=upper):
            ctx_ref[:, :half] = lower[...]
            ctx_ref[:, half:] = upper[...]


def join_groups(place_ref, pieces, ctx_ref):
    (ctx,) = pieces
    groups, _, part = ctx.shape
    for g in range(groups):
        ctx_ref[:, g * part : (g + 1) * part] = ctx[g]


def slot_rows(ids_t, owners, cap):
    tokens = ids_t.shape[1]
    experts = lax.broadcasted_iota(jnp.int32, (owners, tokens), 0)
    first = (experts == ids_t[0:1]).astype(F32)
    second = (experts == ids_t[1:2]).astype(F32)
    src = lax.broadcasted_iota(jnp.int32, (tokens, tokens), 0)
    dst = lax.broadcasted_iota(jnp.int32, (tokens, tokens), 1)
    earlier = (src < dst).astype(F32).astype(BF)
    count = mm((first + second).astype(BF), earlier, NN)
    slot0 = jnp.sum(first * count, axis=0, keepdims=True).astype(jnp.int32)
    slot1 = jnp.sum(second * count, axis=0, keepdims=True).astype(jnp.int32)
    return ids_t[0:1] * cap + slot0, ids_t[1:2] * cap + slot1


def slot_cols(ids, owners, cap):
    tokens = ids.shape[0]
    experts = lax.broadcasted_iota(jnp.int32, (tokens, owners), 1)
    first = (experts == ids[:, 0:1]).astype(F32)
    second = (experts == ids[:, 1:2]).astype(F32)
    dst = lax.broadcasted_iota(jnp.int32, (tokens, tokens), 0)
    src = lax.broadcasted_iota(jnp.int32, (tokens, tokens), 1)
    earlier = (src < dst).astype(F32).astype(BF)
    count = mm(earlier, (first + second).astype(BF), NN)
    slot0 = jnp.sum(first * count, axis=1, keepdims=True).astype(jnp.int32)
    slot1 = jnp.sum(second * count, axis=1, keepdims=True).astype(jnp.int32)
    return ids[:, 0:1] * cap + slot0, ids[:, 1:2] * cap + slot1


def one_hot(hit):
    return jnp.where(hit, 1.0, 0.0).astype(BF)


def send_cot_kernel(owners, cap, ids_ref, w_ref, cot_ref, o_ref):
    tokens = cot_ref.shape[0]
    at0, at1 = slot_rows(ids_ref[...], owners, cap)
    rows = lax.broadcasted_iota(jnp.int32, (owners * cap, tokens), 0)
    cot = cot_ref[...].astype(F32)
    o_ref[...] = (
        mm(one_hot(rows == at0), (w_ref[:, 0:1] * cot).astype(BF), NN)
        + mm(one_hot(rows == at1), (w_ref[:, 1:2] * cot).astype(BF), NN)
    ).astype(BF)


def norm_kernel(owners, cap, join, place_ref, ids_ref, resid_ref, gain_ref, *refs):
    *pieces, stream_ref, o_ref, ctx_ref = refs
    tokens, width = resid_ref.shape
    join(place_ref, pieces, ctx_ref)
    stream = (resid_ref[...].astype(F32) + ctx_ref[...].astype(F32)).astype(BF)
    stream_ref[...] = stream
    stream = stream.astype(F32)
    square = jnp.sum(stream * stream, axis=-1, keepdims=True)
    inv_rms = lax.rsqrt(square / width + 1e-05)
    at0, at1 = slot_rows(ids_ref[...], owners, cap)
    rows = lax.broadcasted_iota(jnp.int32, (owners * cap, tokens), 0)
    pick = one_hot((rows == at0) | (rows == at1))
    normed = ((stream_ref[...].astype(F32) * inv_rms) * gain_ref[...]).astype(BF)
    o_ref[...] = mm(pick, normed, NN).astype(BF)


def fetch(inner, choices, dst, sem):
    if len(choices) == 1:
        pltpu.make_async_copy(choices[0], dst, sem).start()
        return

    @pl.when(inner == 1)
    def _():
        pltpu.make_async_copy(choices[0], dst, sem).start()

    @pl.when(inner == 0)
    def _():
        pltpu.make_async_copy(choices[1], dst, sem).start()


def arrived(choices, dst, sem):
    pltpu.make_async_copy(choices[0], dst, sem).wait()


def regroup(refs, shape):
    refs = list(refs)
    return [[refs.pop(0) for _ in range(size)] for size in shape], refs


def cols_of(place_ref, slot, part):
    return pl.ds(pl.multiple_of(place_ref[COLS + slot] * part, part), part)


def gate_kernel(shape, place_ref, x_ref, *refs):
    slots = len(shape)
    gate_in, refs = regroup(refs, shape)
    o_ref, gate_w, sems = refs
    inner = place_ref[INNER]
    for j in range(slots):
        fetch(inner, gate_in[j], gate_w.at[j], sems.at[j])
    o_ref[...] = by_slots(place_ref, x_ref, gate_in, gate_w, sems)


def by_slots(place_ref, x_ref, weight_in, weight, sems):
    slots, _, part = weight.shape
    total = None
    for j in range(slots):
        rows = x_ref[:, cols_of(place_ref, j, part)]
        arrived(weight_in[j], weight.at[j], sems.at[j])
        term = mm(rows, weight[j], NT)
        total = term if total is None else total + term
    return total


def up_kernel(shape, place_ref, x_ref, gate_ref, *refs):
    slots = len(shape)
    up_in, refs = regroup(refs, shape)
    hidden_ref, to_gate_ref, to_up_ref, up_w, sems = refs
    inner = place_ref[INNER]
    for j in range(slots):
        fetch(inner, up_in[j], up_w.at[j], sems.at[j])
    gate = gate_ref[...]
    sigma = 1.0 / (1.0 + jnp.exp(-gate))
    silu = gate * sigma
    to_up_ref[...] = silu
    to_gate_ref[...] = sigma * (1.0 + gate * (1.0 - sigma))
    up = by_slots(place_ref, x_ref, up_in, up_w, sems)
    hidden_ref[...] = (to_up_ref[...] * up).astype(BF)
    to_gate_ref[...] = up * to_gate_ref[...]


def down_kernel(shape, place_ref, hidden_ref, cot_ref, *refs):
    slots = len(shape)
    down_in, refs = regroup(refs, shape)
    out_ref, d_hidden_ref, down_w, sems = refs
    part = down_w.shape[2]
    inner = place_ref[INNER]
    for j in range(slots):
        fetch(inner, down_in[j], down_w.at[j], sems.at[j])
    total = None
    for j in range(slots):
        rows = cot_ref[:, cols_of(place_ref, j, part)]
        arrived(down_in[j], down_w.at[j], sems.at[j])
        term = mm(rows, down_w[j], NT)
        total = term if total is None else total + term
        out_ref[:, j * part : (j + 1) * part] = mm(hidden_ref[...], down_w[j], NN).astype(BF)
    d_hidden_ref[...] = total


def grad_kernel(
    shape, place_ref, hidden_in, cot_in, d_hidden_in, to_gate_in, to_up_in, *refs
):
    slots = len(shape) - 1
    down_in, refs = regroup(refs, shape[-1:])
    gate_in, refs = regroup(refs, shape[:-1])
    up_in, refs = regroup(refs, shape[:-1])
    o_ref, down_w, gate_w, up_w, sems = refs[:5]
    hidden_ref, cot_ref, d_hidden_ref, to_gate_ref, to_up_ref = refs[5:]
    part = down_w.shape[1]
    inner = place_ref[INNER]
    last = place_ref[COLS + cot_in.shape[1] // part - 1]
    pairs = [
        (cot_in.at[:, pl.ds(pl.multiple_of(last * part, part), part)], cot_ref),
        (d_hidden_in, d_hidden_ref),
        (to_gate_in, to_gate_ref),
        (to_up_in, to_up_ref),
        (hidden_in, hidden_ref),
    ]
    fetch(inner, down_in[0], down_w, sems.at[2, 0])
    copies = [
        pltpu.make_async_copy(src, dst, sems.at[3 + i, 0]) for i, (src, dst) in enumerate(pairs)
    ]
    for copy in copies:
        copy.start()
    for j in range(slots):
        fetch(inner, gate_in[j], gate_w.at[j], sems.at[0, j])
        fetch(inner, up_in[j], up_w.at[j], sems.at[1, j])
    arrived(down_in[0], down_w, sems.at[2, 0])
    for copy in copies:
        copy.wait()
    d_hidden = d_hidden_ref[...] + mm(cot_ref[...], down_w[...], NT)
    d_gate = (d_hidden * to_gate_ref[...]).astype(BF)
    d_up = (d_hidden * to_up_ref[...]).astype(BF)
    o_ref[:, slots * part :] = mm(hidden_ref[...], down_w[...], NN).astype(BF)
    for j in range(slots):
        arrived(gate_in[j], gate_w.at[j], sems.at[0, j])
        arrived(up_in[j], up_w.at[j], sems.at[1, j])
        o_ref[:, j * part : (j + 1) * part] = (
            mm(d_gate, gate_w[j], NN) + mm(d_up, up_w[j], NN)
        ).astype(BF)


def final_kernel(
    owners,
    cap,
    place_ref,
    ids_ref,
    w_ref,
    gain_ref,
    stream_ref,
    cot_ref,
    first_ref,
    last_ref,
    output_ref,
    grad_ref,
    d_normed_ref,
):
    tokens, width = stream_ref.shape
    done = first_ref.shape[1]
    part = width - done
    slots = width // part
    at0, at1 = slot_cols(ids_ref[...], owners, cap)
    rows = lax.broadcasted_iota(jnp.int32, (tokens, owners * cap), 1)
    pick0, pick1 = one_hot(rows == at0), one_hot(rows == at1)
    both = pick0 + pick1
    w0, w1 = w_ref[:, 0:1], w_ref[:, 1:2]
    square = jnp.zeros((tokens, 1), F32)
    dot = jnp.zeros((tokens, 1), F32)
    for j in range(slots):
        cols = cols_of(place_ref, j, part)
        if j < slots - 1:
            pairs = first_ref[:, j * part : (j + 1) * part]
        else:
            pairs = last_ref[:, width:]
        stream = stream_ref[:, cols].astype(F32)
        mixed = w0 * mm(pick0, pairs, NN) + w1 * mm(pick1, pairs, NN)
        output_ref[:, cols] = (stream + mixed).astype(BF)
        grads = last_ref[:, j * part : (j + 1) * part]
        gained = mm(both, grads, NN) * gain_ref[:, cols]
        d_normed_ref[:, cols] = gained
        square = square + jnp.sum(stream * stream, axis=-1, keepdims=True)
        dot = dot + jnp.sum(gained * stream, axis=-1, keepdims=True)
    inv_rms = lax.rsqrt(square / width + 1e-05)
    mean = dot * inv_rms / width
    unit_rows = stream_ref[...].astype(F32) * inv_rms
    d_stream = inv_rms * (d_normed_ref[...] - unit_rows * mean)
    grad_ref[...] = (cot_ref[...].astype(F32) + d_stream).astype(BF)


MIDDLE = [(1, 2), (2, 1)]
OUTWARD = [(1, 0), (2, 3)]
INWARD = [(0, 1), (3, 2)]


def gather_all(shard, groups):
    whole_weight = lax.all_gather(shard, "seq", axis=0)
    return [[whole_weight[j]] for j in range(groups)]


def send(array, pairs, *first):
    return lax.ppermute(gated(array, *first), "seq", pairs)


def places(groups):
    if groups == 4:
        own = lax.axis_index("seq")
        table = jnp.array(
            [
                [0, 0, 1, 2, 3, 0, 0, 0, 0, 0],
                [1, 1, 0, 2, 3, 1, 1, 0, 2, 3],
                [1, 2, 3, 1, 0, 2, 2, 3, 1, 0],
                [0, 3, 2, 1, 0, 3, 0, 0, 0, 0],
            ],
            jnp.int32,
        )
        return table[own]
    return jnp.arange(-1, groups, dtype=jnp.int32)


def exchange(rows, owners, axis):
    total, width = rows.shape
    rows = rows.reshape(owners, total // owners, width)
    rows = lax.all_to_all(rows, axis, split_axis=0, concat_axis=0, tiled=True)
    return rows.reshape(total, width)


def flat(slots):
    return [ref for choices in slots for ref in choices]


def per_device(
    queries,
    keys,
    values,
    resid,
    norm_gain,
    w_gate,
    w_up,
    w_down,
    expert_ids,
    route_weights,
    cotangent,
):
    groups = lax.axis_size("seq")
    owners = lax.axis_size("exp")
    tokens, width = queries.shape[1:]
    ffw = w_gate.shape[2]
    part = width // groups
    cap = max(2, tokens * 10 // (4 * owners))
    total = owners * cap
    ids = expert_ids[0]
    ids_t = ids.T
    weights = route_weights[0]
    gain = norm_gain[None]
    cot = cotangent[0]
    place = places(groups)

    one = 2 * total * width * ffw
    send_cot = call(
        functools.partial(send_cot_kernel, owners, cap),
        sds((total, width)),
        (ids_t, weights, cot),
        [VMEM] * 3,
        flops=4 * total * tokens * width,
        moved=2 * (total + tokens) * width,
    )
    cot_rows = exchange(send_cot, owners, "exp")
    shards = (w_gate[0].T, w_up[0].T, w_down[0])
    if groups == 4:
        join = join_middle
        pieces, gate_in, up_in, down_in, norm_after, up_after = line_of_four(
            place, queries[0], keys[0], values[0], *shards, cot_rows
        )
    else:
        join = join_groups
        gate_in, up_in, down_in = [gather_all(shard, groups) for shard in shards]
        packed = pack(queries[0], keys[0], values[0], groups)
        heads = lax.all_to_all(packed, "seq", split_axis=0, concat_axis=0, tiled=True)
        ctx = attend(heads)
        pieces = (lax.all_to_all(ctx, "seq", split_axis=0, concat_axis=0, tiled=True),)
        norm_after = up_after = ()
    shape = [len(choices) for choices in gate_in]

    stream, send_rows = call(
        functools.partial(norm_kernel, owners, cap, join),
        (sds((tokens, width)), sds((total, width))),
        (place, ids_t, resid[0], gain, *pieces),
        [SMEM] + [VMEM] * (3 + len(pieces)),
        [pltpu.VMEM((tokens, width), BF)],
        flops=2 * total * tokens * width,
        moved=2 * (total + 3 * tokens) * width,
        after=norm_after,
    )
    rows = exchange(send_rows, owners, "exp")

    full_w = pltpu.VMEM((groups, ffw, part), BF)
    gate_pre = call(
        functools.partial(gate_kernel, shape),
        sds((total, ffw), F32),
        (place, rows, *flat(gate_in)),
        [SMEM, VMEM] + [HBM] * sum(shape),
        [full_w, pltpu.SemaphoreType.DMA((groups,))],
        flops=one,
        moved=2 * width * ffw + 2 * total * width + 4 * total * ffw,
    )
    hidden, to_gate, to_up = call(
        functools.partial(up_kernel, shape),
        (sds((total, ffw)), sds((total, ffw), F32), sds((total, ffw), F32)),
        (place, rows, gate_pre, *flat(up_in)),
        [SMEM, VMEM, VMEM] + [HBM] * sum(shape),
        [full_w, pltpu.SemaphoreType.DMA((groups,))],
        flops=one,
        moved=2 * width * ffw + 2 * total * width + 14 * total * ffw,
        after=up_after,
    )
    out_first, d_hidden = call(
        functools.partial(down_kernel, shape[:-1]),
        (sds((total, width - part)), sds((total, ffw), F32)),
        (place, hidden, cot_rows, *flat(down_in[:-1])),
        [SMEM, VMEM, VMEM] + [HBM] * sum(shape[:-1]),
        [
            pltpu.VMEM((groups - 1, ffw, part), BF),
            pltpu.SemaphoreType.DMA((groups - 1,)),
        ],
        flops=2 * one * (groups - 1) // groups,
        moved=2 * width * ffw + 4 * total * width + 6 * total * ffw,
    )
    back_first = exchange(out_first, owners, "exp")
    back = call(
        functools.partial(grad_kernel, [*shape, shape[-1]]),
        sds((total, width + part)),
        (
            place,
            hidden,
            cot_rows,
            d_hidden,
            to_gate,
            to_up,
            *flat(down_in[-1:]),
            *flat(gate_in),
            *flat(up_in),
        ),
        [SMEM] + [HBM] * (5 + shape[-1] + 2 * sum(shape)),
        [
            pltpu.VMEM((ffw, part), BF),
            full_w,
            full_w,
            pltpu.SemaphoreType.DMA((8, groups)),
            pltpu.VMEM((total, ffw), BF),
            pltpu.VMEM((total, part), BF),
            pltpu.VMEM((total, ffw), F32),
            pltpu.VMEM((total, ffw), F32),
            pltpu.VMEM((total, ffw), F32),
        ],
        flops=2 * one + 2 * one // groups,
        moved=4 * width * ffw + 4 * total * width + 14 * total * ffw,
    )
    back_last = exchange(back, owners, "exp")
    output, stream_grad = call(
        functools.partial(final_kernel, owners, cap),
        (sds((tokens, width)), sds((tokens, width))),
        (place, ids, weights, gain, stream, cot, back_first, back_last),
        [SMEM] + [VMEM] * 7,
        [pltpu.VMEM((tokens, width), F32)],
        flops=6 * total * tokens * width,
        moved=4 * total * width + 8 * tokens * width,
        vmem=16,
        held=True,
    )
    return (output[None], stream_grad[None])


def solution(mesh):
    placed = (
        P("exp", "seq", None),
        P("exp", "seq", None),
        P("exp", "seq", None),
        P("exp", "seq", None),
        P(),
        P("exp", "seq", None),
        P("exp", "seq", None),
        P("exp", None, "seq"),
        P("exp", "seq", None),
        P("exp", "seq", None),
        P("exp", "seq", None),
    )
    return jax.shard_map(
        per_device,
        mesh=mesh,
        in_specs=placed,
        out_specs=(P("exp", "seq", None), P("exp", "seq", None)),
        check_vma=False,
    )
```

```python
import functools

import jax
import jax.numpy as jnp
from jax import lax
from jax.experimental import pallas as pl
from jax.experimental.pallas import tpu as pltpu
from jax.sharding import PartitionSpec as P

HD = 128
BF = jnp.bfloat16
F32 = jnp.float32
MIB = 1 << 20
HBM = pl.BlockSpec(memory_space=pltpu.HBM)
VMEM = pl.BlockSpec(memory_space=pltpu.VMEM)
SMEM = pl.BlockSpec(memory_space=pltpu.SMEM)
NT = (((1,), (1,)), ((), ()))
NN = (((1,), (0,)), ((), ()))


def mm(a, b, dims):
    return lax.dot_general(a, b, dims, preferred_element_type=F32)


def whole(array):
    return pl.BlockSpec(array.shape, lambda i: (0,) * len(array.shape))


def call(kernel, outs, args, in_specs, scratch=(), flops=0, moved=0, vmem=56, after=(), held=False):
    count, extra = len(args), len(after)

    def body(*refs):
        kernel(*refs[:count], *refs[count + extra :])

    return pl.pallas_call(
        body,
        grid=() if held else (1,),
        out_shape=outs,
        in_specs=[
            *[
                whole(arg) if spec is VMEM and not held else spec
                for arg, spec in zip(args, in_specs)
            ],
            *[HBM] * extra,
        ],
        out_specs=jax.tree.map(lambda out: VMEM if held else whole(out), outs),
        scratch_shapes=list(scratch),
        compiler_params=pltpu.CompilerParams(vmem_limit_bytes=vmem * MIB),
        cost_estimate=pl.CostEstimate(flops=flops, bytes_accessed=moved, transcendentals=0),
    )(*args, *after)


def gated(array, *first):
    return lax.optimization_barrier((array, *first))[0] if first else array


def sds(shape, dtype=BF):
    return jax.ShapeDtypeStruct(shape, dtype)


def pack_kernel(q_ref, k_ref, v_ref, o_ref):
    rows = q_ref.shape[0]
    o_ref[0, 0:rows] = q_ref[...]
    o_ref[0, rows : 2 * rows] = k_ref[...]
    o_ref[0, 2 * rows : 3 * rows] = v_ref[...]


def pack(q, k, v, groups):
    rows, width = q.shape
    part = width // groups
    spec = pl.BlockSpec((rows, part), lambda g: (0, g))
    return pl.pallas_call(
        pack_kernel,
        grid=(groups,),
        out_shape=sds((groups, 3 * rows, part)),
        in_specs=[spec] * 3,
        out_specs=pl.BlockSpec((1, 3 * rows, part), lambda g: (g, 0, 0)),
        cost_estimate=pl.CostEstimate(
            flops=0, bytes_accessed=12 * rows * width, transcendentals=0
        ),
    )(q, k, v)


def attend_head(query, keys, vals, store):
    length = keys.shape[0]
    block = min(512, length)
    scale = HD ** (-0.5)
    row_ids = lax.broadcasted_iota(jnp.int32, (block, block), 0)
    col_ids = lax.broadcasted_iota(jnp.int32, (block, block), 1)
    keep = col_ids <= row_ids
    for start in range(0, length, block):
        end = start + block
        scores = mm(query[start:end], keys[:end], NT) * scale
        diag = jnp.where(keep, scores[:, start:], -jnp.inf)
        scores = jnp.concatenate([scores[:, :start], diag], axis=1) if start else diag
        exps = jnp.exp(scores - jnp.max(scores, axis=-1, keepdims=True))
        inverse = 1.0 / jnp.sum(exps, axis=-1, keepdims=True)
        store(start, end, mm((exps * inverse).astype(BF), vals[:end], NN).astype(BF))


def attend_columns(x_ref, cols, o_ref):
    blocks, three, _ = x_ref.shape
    rows = three // 3
    query, keys, vals = [
        x_ref[:, i * rows : (i + 1) * rows, cols].reshape(blocks * rows, HD) for i in range(3)
    ]

    def store(start, end, ctx):
        first, last = start // rows, end // rows
        o_ref[first:last, :, cols] = ctx.reshape(last - first, rows, HD)

    attend_head(query, keys, vals, store)


def attend_kernel(x_ref, o_ref):
    attend_columns(x_ref, slice(0, HD), o_ref)


def attend(x):
    blocks, three, part = x.shape
    rows = three // 3
    length = blocks * rows
    return pl.pallas_call(
        attend_kernel,
        grid=(part // HD,),
        out_shape=sds((blocks, rows, part)),
        in_specs=[pl.BlockSpec((blocks, three, HD), lambda h: (0, 0, h))],
        out_specs=pl.BlockSpec((blocks, rows, HD), lambda h: (0, 0, h)),
        compiler_params=pltpu.CompilerParams(vmem_limit_bytes=40 * MIB),
        cost_estimate=pl.CostEstimate(
            flops=4 * length * length * part,
            bytes_accessed=8 * length * part,
            transcendentals=length * length * part // HD,
        ),
    )(x)


INNER, COLS, PLANE, ATTEND = 0, 1, 5, 6


def halves_kernel(place_ref, q_ref, k_ref, v_ref, first_ref, second_ref):
    rows, width = q_ref.shape
    half = width // 2

    def copy(lower, upper):
        for i, ref in enumerate((q_ref, k_ref, v_ref)):
            lower[i * rows : (i + 1) * rows] = ref[:, :half]
            upper[i * rows : (i + 1) * rows] = ref[:, half:]

    @pl.when(place_ref[PLANE] < 2)
    def _():
        copy(first_ref, second_ref)

    @pl.when(place_ref[PLANE] >= 2)
    def _():
        copy(second_ref, first_ref)


def middle_kernel(place_ref, own_in, near_in, mid_in, far_in, *refs):
    *outs, x_ref, ctx_ref, sems = refs
    blocks, three, half = x_ref.shape
    rows = three // 3

    @pl.when(place_ref[INNER] == 1)
    def _():
        copies = [
            pltpu.make_async_copy(ref, x_ref.at[place_ref[ATTEND + i]], sems.at[i])
            for i, ref in enumerate((own_in, near_in, mid_in, far_in))
        ]
        for copy in copies:
            copy.start()
        for copy in copies:
            copy.wait()

        def step(i, carry):
            for j in range(2):
                cols = pl.ds(pl.multiple_of((2 * i + j) * HD, HD), HD)
                attend_columns(x_ref, cols, ctx_ref)
            return carry

        lax.fori_loop(0, half // HD // 2, step, 0)
        for i, out in enumerate(outs):
            out[...] = ctx_ref[place_ref[ATTEND + i]]


def line_of_four(place, queries, keys, values, gate, up, down, cot_rows):
    rows, width = queries.shape
    half = width // 2
    block = sds((3 * rows, half))
    first, second = call(
        halves_kernel,
        (block, block),
        (place, queries, keys, values),
        [SMEM, VMEM, VMEM, VMEM],
        moved=12 * rows * width,
    )
    gate_end = send(gate, OUTWARD)
    up_end = send(up, OUTWARD)
    down_end = send(down, OUTWARD, gate_end)
    gate_mid = send(gate, MIDDLE)
    gate_far = send(gate_mid, OUTWARD)
    near = send(first, INWARD, gate_mid, gate_end)
    mid = send(second, MIDDLE, gate_mid, gate_end)
    far = send(second, [(0, 2), (3, 1)], gate_mid, gate_end)
    piece = sds((rows, half))
    pieces = call(
        middle_kernel,
        (piece,) * 4,
        (place, first, near, mid, far),
        [SMEM] + [HBM] * 4,
        [
            pltpu.VMEM((4, 3 * rows, half), BF),
            pltpu.VMEM((4, rows, half), BF),
            pltpu.SemaphoreType.DMA((4,)),
        ],
        flops=64 * rows * rows * half,
        moved=32 * rows * half,
        after=(gate_end, up_end, gate_far, cot_rows),
    )
    up_mid = send(up, MIDDLE, near, mid, far)
    gate_inner = send(gate, INWARD, near, far, gate_end, up_end)
    up_inner = send(up, INWARD, near, far, gate_end, up_end)
    down_inner = send(down, INWARD, gate_inner)
    own, near, mid, far = lax.optimization_barrier((*pieces, gate_inner, down_end))[:4]
    mid = send(mid, MIDDLE)
    far = send(far, [(2, 0), (1, 3)])
    up_far = send(up_mid, OUTWARD, pieces[0])
    near = send(near, OUTWARD, up_far)
    gate_mid_near = send(gate_inner, MIDDLE)
    up_mid_near = send(up_inner, MIDDLE, pieces[0])
    down_mid = send(down, MIDDLE, gate_mid_near)
    down_mid_near = send(down_inner, MIDDLE, up_mid_near)
    gate_far_near = send(gate_mid_near, OUTWARD)
    up_far_near = send(up_mid_near, OUTWARD, gate_far_near)
    down_far = send(down_mid, OUTWARD, gate_far_near)
    down_far_near = send(down_mid_near, OUTWARD, up_far_near)
    norm_after = (gate_mid_near,)
    up_after = (down_mid_near,)
    gate_in = [
        [gate],
        [gate_inner, gate_end],
        [gate_mid, gate_far],
        [gate_mid_near, gate_far_near],
    ]
    up_in = [[up], [up_inner, up_end], [up_mid, up_far], [up_mid_near, up_far_near]]
    down_in = [
        [down],
        [down_inner, down_end],
        [down_mid, down_far],
        [down_mid_near, down_far_near],
    ]
    return (own, near, mid, far), gate_in, up_in, down_in, norm_after, up_after


def join_middle(place_ref, pieces, ctx_ref):
    own, near, mid, far = pieces
    half = own.shape[1]
    for plane, (lower, upper) in enumerate(((near, far), (own, mid), (mid, own), (far, near))):

        @pl.when(place_ref[PLANE] == plane)
        def _(lower=lower, upper=upper):
            ctx_ref[:, :half] = lower[...]
            ctx_ref[:, half:] = upper[...]


def join_groups(place_ref, pieces, ctx_ref):
    (ctx,) = pieces
    groups, _, part = ctx.shape
    for g in range(groups):
        ctx_ref[:, g * part : (g + 1) * part] = ctx[g]


def slot_rows(ids_t, owners, cap):
    tokens = ids_t.shape[1]
    experts = lax.broadcasted_iota(jnp.int32, (owners, tokens), 0)
    first = (experts == ids_t[0:1]).astype(F32)
    second = (experts == ids_t[1:2]).astype(F32)
    src = lax.broadcasted_iota(jnp.int32, (tokens, tokens), 0)
    dst = lax.broadcasted_iota(jnp.int32, (tokens, tokens), 1)
    earlier = (src < dst).astype(F32).astype(BF)
    count = mm((first + second).astype(BF), earlier, NN)
    slot0 = jnp.sum(first * count, axis=0, keepdims=True).astype(jnp.int32)
    slot1 = jnp.sum(second * count, axis=0, keepdims=True).astype(jnp.int32)
    return ids_t[0:1] * cap + slot0, ids_t[1:2] * cap + slot1


def slot_cols(ids, owners, cap):
    tokens = ids.shape[0]
    experts = lax.broadcasted_iota(jnp.int32, (tokens, owners), 1)
    first = (experts == ids[:, 0:1]).astype(F32)
    second = (experts == ids[:, 1:2]).astype(F32)
    dst = lax.broadcasted_iota(jnp.int32, (tokens, tokens), 0)
    src = lax.broadcasted_iota(jnp.int32, (tokens, tokens), 1)
    earlier = (src < dst).astype(F32).astype(BF)
    count = mm(earlier, (first + second).astype(BF), NN)
    slot0 = jnp.sum(first * count, axis=1, keepdims=True).astype(jnp.int32)
    slot1 = jnp.sum(second * count, axis=1, keepdims=True).astype(jnp.int32)
    return ids[:, 0:1] * cap + slot0, ids[:, 1:2] * cap + slot1


def one_hot(hit):
    return jnp.where(hit, 1.0, 0.0).astype(BF)


def send_cot_kernel(owners, cap, ids_ref, w_ref, cot_ref, o_ref):
    tokens = cot_ref.shape[0]
    at0, at1 = slot_rows(ids_ref[...], owners, cap)
    rows = lax.broadcasted_iota(jnp.int32, (owners * cap, tokens), 0)
    cot = cot_ref[...].astype(F32)
    o_ref[...] = (
        mm(one_hot(rows == at0), (w_ref[:, 0:1] * cot).astype(BF), NN)
        + mm(one_hot(rows == at1), (w_ref[:, 1:2] * cot).astype(BF), NN)
    ).astype(BF)


def norm_kernel(owners, cap, join, place_ref, ids_ref, resid_ref, gain_ref, *refs):
    *pieces, stream_ref, o_ref, ctx_ref = refs
    tokens, width = resid_ref.shape
    join(place_ref, pieces, ctx_ref)
    stream = (resid_ref[...].astype(F32) + ctx_ref[...].astype(F32)).astype(BF)
    stream_ref[...] = stream
    stream = stream.astype(F32)
    square = jnp.sum(stream * stream, axis=-1, keepdims=True)
    inv_rms = lax.rsqrt(square / width + 1e-05)
    at0, at1 = slot_rows(ids_ref[...], owners, cap)
    rows = lax.broadcasted_iota(jnp.int32, (owners * cap, tokens), 0)
    pick = one_hot((rows == at0) | (rows == at1))
    normed = ((stream_ref[...].astype(F32) * inv_rms) * gain_ref[...]).astype(BF)
    o_ref[...] = mm(pick, normed, NN).astype(BF)


def fetch(inner, choices, dst, sem):
    if len(choices) == 1:
        pltpu.make_async_copy(choices[0], dst, sem).start()
        return

    @pl.when(inner == 1)
    def _():
        pltpu.make_async_copy(choices[0], dst, sem).start()

    @pl.when(inner == 0)
    def _():
        pltpu.make_async_copy(choices[1], dst, sem).start()


def arrived(choices, dst, sem):
    pltpu.make_async_copy(choices[0], dst, sem).wait()


def regroup(refs, shape):
    refs = list(refs)
    return [[refs.pop(0) for _ in range(size)] for size in shape], refs


def cols_of(place_ref, slot, part):
    return pl.ds(pl.multiple_of(place_ref[COLS + slot] * part, part), part)


def gate_kernel(shape, place_ref, x_ref, *refs):
    slots = len(shape)
    gate_in, refs = regroup(refs, shape)
    o_ref, gate_w, sems = refs
    inner = place_ref[INNER]
    for j in range(slots):
        fetch(inner, gate_in[j], gate_w.at[j], sems.at[j])
    o_ref[...] = by_slots(place_ref, x_ref, gate_in, gate_w, sems)


def by_slots(place_ref, x_ref, weight_in, weight, sems):
    slots, _, part = weight.shape
    total = None
    for j in range(slots):
        rows = x_ref[:, cols_of(place_ref, j, part)]
        arrived(weight_in[j], weight.at[j], sems.at[j])
        term = mm(rows, weight[j], NT)
        total = term if total is None else total + term
    return total


def up_kernel(shape, place_ref, x_ref, gate_ref, *refs):
    slots = len(shape)
    up_in, refs = regroup(refs, shape)
    hidden_ref, to_gate_ref, to_up_ref, up_w, sems = refs
    inner = place_ref[INNER]
    for j in range(slots):
        fetch(inner, up_in[j], up_w.at[j], sems.at[j])
    gate = gate_ref[...]
    sigma = 1.0 / (1.0 + jnp.exp(-gate))
    silu = gate * sigma
    to_up_ref[...] = silu
    to_gate_ref[...] = sigma * (1.0 + gate * (1.0 - sigma))
    up = by_slots(place_ref, x_ref, up_in, up_w, sems)
    hidden_ref[...] = (to_up_ref[...] * up).astype(BF)
    to_gate_ref[...] = up * to_gate_ref[...]


def down_kernel(shape, place_ref, hidden_ref, cot_ref, *refs):
    slots = len(shape)
    down_in, refs = regroup(refs, shape)
    out_ref, d_hidden_ref, down_w, sems = refs
    part = down_w.shape[2]
    inner = place_ref[INNER]
    for j in range(slots):
        fetch(inner, down_in[j], down_w.at[j], sems.at[j])
    total = None
    for j in range(slots):
        rows = cot_ref[:, cols_of(place_ref, j, part)]
        arrived(down_in[j], down_w.at[j], sems.at[j])
        term = mm(rows, down_w[j], NT)
        total = term if total is None else total + term
        out_ref[:, j * part : (j + 1) * part] = mm(hidden_ref[...], down_w[j], NN).astype(BF)
    d_hidden_ref[...] = total


def grad_kernel(
    shape, place_ref, hidden_in, cot_in, d_hidden_in, to_gate_in, to_up_in, *refs
):
    slots = len(shape) - 1
    down_in, refs = regroup(refs, shape[-1:])
    gate_in, refs = regroup(refs, shape[:-1])
    up_in, refs = regroup(refs, shape[:-1])
    o_ref, down_w, gate_w, up_w, sems = refs[:5]
    hidden_ref, cot_ref, d_hidden_ref, to_gate_ref, to_up_ref = refs[5:]
    part = down_w.shape[1]
    inner = place_ref[INNER]
    last = place_ref[COLS + cot_in.shape[1] // part - 1]
    pairs = [
        (cot_in.at[:, pl.ds(pl.multiple_of(last * part, part), part)], cot_ref),
        (d_hidden_in, d_hidden_ref),
        (to_gate_in, to_gate_ref),
        (to_up_in, to_up_ref),
        (hidden_in, hidden_ref),
    ]
    fetch(inner, down_in[0], down_w, sems.at[2, 0])
    copies = [
        pltpu.make_async_copy(src, dst, sems.at[3 + i, 0]) for i, (src, dst) in enumerate(pairs)
    ]
    for copy in copies:
        copy.start()
    for j in range(slots):
        fetch(inner, gate_in[j], gate_w.at[j], sems.at[0, j])
        fetch(inner, up_in[j], up_w.at[j], sems.at[1, j])
    arrived(down_in[0], down_w, sems.at[2, 0])
    for copy in copies:
        copy.wait()
    d_hidden = d_hidden_ref[...] + mm(cot_ref[...], down_w[...], NT)
    d_gate = (d_hidden * to_gate_ref[...]).astype(BF)
    d_up = (d_hidden * to_up_ref[...]).astype(BF)
    o_ref[:, slots * part :] = mm(hidden_ref[...], down_w[...], NN).astype(BF)
    for j in range(slots):
        arrived(gate_in[j], gate_w.at[j], sems.at[0, j])
        arrived(up_in[j], up_w.at[j], sems.at[1, j])
        o_ref[:, j * part : (j + 1) * part] = (
            mm(d_gate, gate_w[j], NN) + mm(d_up, up_w[j], NN)
        ).astype(BF)


def final_kernel(
    owners,
    cap,
    place_ref,
    ids_ref,
    w_ref,
    gain_ref,
    stream_ref,
    cot_ref,
    first_ref,
    last_ref,
    output_ref,
    grad_ref,
    d_normed_ref,
):
    tokens, width = stream_ref.shape
    done = first_ref.shape[1]
    part = width - done
    slots = width // part
    at0, at1 = slot_cols(ids_ref[...], owners, cap)
    rows = lax.broadcasted_iota(jnp.int32, (tokens, owners * cap), 1)
    pick0, pick1 = one_hot(rows == at0), one_hot(rows == at1)
    both = pick0 + pick1
    w0, w1 = w_ref[:, 0:1], w_ref[:, 1:2]
    square = jnp.zeros((tokens, 1), F32)
    dot = jnp.zeros((tokens, 1), F32)
    for j in range(slots):
        cols = cols_of(place_ref, j, part)
        if j < slots - 1:
            pairs = first_ref[:, j * part : (j + 1) * part]
        else:
            pairs = last_ref[:, width:]
        stream = stream_ref[:, cols].astype(F32)
        mixed = w0 * mm(pick0, pairs, NN) + w1 * mm(pick1, pairs, NN)
        output_ref[:, cols] = (stream + mixed).astype(BF)
        grads = last_ref[:, j * part : (j + 1) * part]
        gained = mm(both, grads, NN) * gain_ref[:, cols]
        d_normed_ref[:, cols] = gained
        square = square + jnp.sum(stream * stream, axis=-1, keepdims=True)
        dot = dot + jnp.sum(gained * stream, axis=-1, keepdims=True)
    inv_rms = lax.rsqrt(square / width + 1e-05)
    mean = dot * inv_rms / width
    unit_rows = stream_ref[...].astype(F32) * inv_rms
    d_stream = inv_rms * (d_normed_ref[...] - unit_rows * mean)
    grad_ref[...] = (cot_ref[...].astype(F32) + d_stream).astype(BF)


MIDDLE = [(1, 2), (2, 1)]
OUTWARD = [(1, 0), (2, 3)]
INWARD = [(0, 1), (3, 2)]


def gather_all(shard, groups):
    whole_weight = lax.all_gather(shard, "seq", axis=0)
    return [[whole_weight[j]] for j in range(groups)]


def send(array, pairs, *first):
    return lax.ppermute(gated(array, *first), "seq", pairs)


def places(groups):
    if groups == 4:
        own = lax.axis_index("seq")
        table = jnp.array(
            [
                [0, 0, 1, 2, 3, 0, 0, 0, 0, 0],
                [1, 1, 0, 2, 3, 1, 1, 0, 2, 3],
                [1, 2, 3, 1, 0, 2, 2, 3, 1, 0],
                [0, 3, 2, 1, 0, 3, 0, 0, 0, 0],
            ],
            jnp.int32,
        )
        return table[own]
    return jnp.arange(-1, groups, dtype=jnp.int32)


def exchange(rows, owners, axis):
    total, width = rows.shape
    rows = rows.reshape(owners, total // owners, width)
    rows = lax.all_to_all(rows, axis, split_axis=0, concat_axis=0, tiled=True)
    return rows.reshape(total, width)


def flat(slots):
    return [ref for choices in slots for ref in choices]


def per_device(
    queries,
    keys,
    values,
    resid,
    norm_gain,
    w_gate,
    w_up,
    w_down,
    expert_ids,
    route_weights,
    cotangent,
):
    groups = lax.axis_size("seq")
    owners = lax.axis_size("exp")
    tokens, width = queries.shape[1:]
    ffw = w_gate.shape[2]
    part = width // groups
    cap = max(2, tokens * 10 // (4 * owners))
    total = owners * cap
    ids = expert_ids[0]
    ids_t = ids.T
    weights = route_weights[0]
    gain = norm_gain[None]
    cot = cotangent[0]
    place = places(groups)

    one = 2 * total * width * ffw
    send_cot = call(
        functools.partial(send_cot_kernel, owners, cap),
        sds((total, width)),
        (ids_t, weights, cot),
        [VMEM] * 3,
        flops=4 * total * tokens * width,
        moved=2 * (total + tokens) * width,
    )
    cot_rows = exchange(send_cot, owners, "exp")
    shards = (w_gate[0].T, w_up[0].T, w_down[0])
    if groups == 4:
        join = join_middle
        pieces, gate_in, up_in, down_in, norm_after, up_after = line_of_four(
            place, queries[0], keys[0], values[0], *shards, cot_rows
        )
    else:
        join = join_groups
        gate_in, up_in, down_in = [gather_all(shard, groups) for shard in shards]
        packed = pack(queries[0], keys[0], values[0], groups)
        heads = lax.all_to_all(packed, "seq", split_axis=0, concat_axis=0, tiled=True)
        ctx = attend(heads)
        pieces = (lax.all_to_all(ctx, "seq", split_axis=0, concat_axis=0, tiled=True),)
        norm_after = up_after = ()
    shape = [len(choices) for choices in gate_in]

    stream, send_rows = call(
        functools.partial(norm_kernel, owners, cap, join),
        (sds((tokens, width)), sds((total, width))),
        (place, ids_t, resid[0], gain, *pieces),
        [SMEM] + [VMEM] * (3 + len(pieces)),
        [pltpu.VMEM((tokens, width), BF)],
        flops=2 * total * tokens * width,
        moved=2 * (total + 3 * tokens) * width,
        after=norm_after,
    )
    rows = exchange(send_rows, owners, "exp")

    full_w = pltpu.VMEM((groups, ffw, part), BF)
    gate_pre = call(
        functools.partial(gate_kernel, shape),
        sds((total, ffw), F32),
        (place, rows, *flat(gate_in)),
        [SMEM, VMEM] + [HBM] * sum(shape),
        [full_w, pltpu.SemaphoreType.DMA((groups,))],
        flops=one,
        moved=2 * width * ffw + 2 * total * width + 4 * total * ffw,
    )
    hidden, to_gate, to_up = call(
        functools.partial(up_kernel, shape),
        (sds((total, ffw)), sds((total, ffw), F32), sds((total, ffw), F32)),
        (place, rows, gate_pre, *flat(up_in)),
        [SMEM, VMEM, VMEM] + [HBM] * sum(shape),
        [full_w, pltpu.SemaphoreType.DMA((groups,))],
        flops=one,
        moved=2 * width * ffw + 2 * total * width + 14 * total * ffw,
        after=up_after,
    )
    out_first, d_hidden = call(
        functools.partial(down_kernel, shape[:-1]),
        (sds((total, width - part)), sds((total, ffw), F32)),
        (place, hidden, cot_rows, *flat(down_in[:-1])),
        [SMEM, VMEM, VMEM] + [HBM] * sum(shape[:-1]),
        [
            pltpu.VMEM((groups - 1, ffw, part), BF),
            pltpu.SemaphoreType.DMA((groups - 1,)),
        ],
        flops=2 * one * (groups - 1) // groups,
        moved=2 * width * ffw + 4 * total * width + 6 * total * ffw,
    )
    back_first = exchange(out_first, owners, "exp")
    back = call(
        functools.partial(grad_kernel, [*shape, shape[-1]]),
        sds((total, width + part)),
        (
            place,
            hidden,
            cot_rows,
            d_hidden,
            to_gate,
            to_up,
            *flat(down_in[-1:]),
            *flat(gate_in),
            *flat(up_in),
        ),
        [SMEM] + [HBM] * (5 + shape[-1] + 2 * sum(shape)),
        [
            pltpu.VMEM((ffw, part), BF),
            full_w,
            full_w,
            pltpu.SemaphoreType.DMA((8, groups)),
            pltpu.VMEM((total, ffw), BF),
            pltpu.VMEM((total, part), BF),
            pltpu.VMEM((total, ffw), F32),
            pltpu.VMEM((total, ffw), F32),
            pltpu.VMEM((total, ffw), F32),
        ],
        flops=2 * one + 2 * one // groups,
        moved=4 * width * ffw + 4 * total * width + 14 * total * ffw,
    )
    back_last = exchange(back, owners, "exp")
    output, stream_grad = call(
        functools.partial(final_kernel, owners, cap),
        (sds((tokens, width)), sds((tokens, width))),
        (place, ids, weights, gain, stream, cot, back_first, back_last),
        [SMEM] + [VMEM] * 7,
        [pltpu.VMEM((tokens, width), F32)],
        flops=6 * total * tokens * width,
        moved=4 * total * width + 8 * tokens * width,
        vmem=16,
        held=True,
    )
    return (output[None], stream_grad[None])


def solution(mesh):
    placed = (
        P("exp", "seq", None),
        P("exp", "seq", None),
        P("exp", "seq", None),
        P("exp", "seq", None),
        P(),
        P("exp", "seq", None),
        P("exp", "seq", None),
        P("exp", None, "seq"),
        P("exp", "seq", None),
        P("exp", "seq", None),
        P("exp", "seq", None),
    )
    return jax.shard_map(
        per_device,
        mesh=mesh,
        in_specs=placed,
        out_specs=(P("exp", "seq", None), P("exp", "seq", None)),
        check_vma=False,
    )
```

```python
import functools

import jax
import jax.numpy as jnp
from jax import lax
from jax.experimental import pallas as pl
from jax.experimental.pallas import tpu as pltpu
from jax.sharding import PartitionSpec as P

HD = 128
BF = jnp.bfloat16
F32 = jnp.float32
MIB = 1 << 20
HBM = pl.BlockSpec(memory_space=pltpu.HBM)
VMEM = pl.BlockSpec(memory_space=pltpu.VMEM)
SMEM = pl.BlockSpec(memory_space=pltpu.SMEM)
NT = (((1,), (1,)), ((), ()))
NN = (((1,), (0,)), ((), ()))


def mm(a, b, dims):
    return lax.dot_general(a, b, dims, preferred_element_type=F32)


def whole(array):
    return pl.BlockSpec(array.shape, lambda i: (0,) * len(array.shape))


def call(kernel, outs, args, in_specs, scratch=(), flops=0, moved=0, vmem=56, after=(), held=False):
    count, extra = len(args), len(after)

    def body(*refs):
        kernel(*refs[:count], *refs[count + extra :])

    return pl.pallas_call(
        body,
        grid=() if held else (1,),
        out_shape=outs,
        in_specs=[
            *[
                whole(arg) if spec is VMEM and not held else spec
                for arg, spec in zip(args, in_specs)
            ],
            *[HBM] * extra,
        ],
        out_specs=jax.tree.map(lambda out: VMEM if held else whole(out), outs),
        scratch_shapes=list(scratch),
        compiler_params=pltpu.CompilerParams(vmem_limit_bytes=vmem * MIB),
        cost_estimate=pl.CostEstimate(flops=flops, bytes_accessed=moved, transcendentals=0),
    )(*args, *after)


def gated(array, *first):
    return lax.optimization_barrier((array, *first))[0] if first else array


def sds(shape, dtype=BF):
    return jax.ShapeDtypeStruct(shape, dtype)


def pack_kernel(q_ref, k_ref, v_ref, o_ref):
    rows = q_ref.shape[0]
    o_ref[0, 0:rows] = q_ref[...]
    o_ref[0, rows : 2 * rows] = k_ref[...]
    o_ref[0, 2 * rows : 3 * rows] = v_ref[...]


def pack(q, k, v, groups):
    rows, width = q.shape
    part = width // groups
    spec = pl.BlockSpec((rows, part), lambda g: (0, g))
    return pl.pallas_call(
        pack_kernel,
        grid=(groups,),
        out_shape=sds((groups, 3 * rows, part)),
        in_specs=[spec] * 3,
        out_specs=pl.BlockSpec((1, 3 * rows, part), lambda g: (g, 0, 0)),
        cost_estimate=pl.CostEstimate(
            flops=0, bytes_accessed=12 * rows * width, transcendentals=0
        ),
    )(q, k, v)


def attend_head(query, keys, vals, store):
    length = keys.shape[0]
    block = min(512, length)
    scale = HD ** (-0.5)
    row_ids = lax.broadcasted_iota(jnp.int32, (block, block), 0)
    col_ids = lax.broadcasted_iota(jnp.int32, (block, block), 1)
    keep = col_ids <= row_ids
    for start in range(0, length, block):
        end = start + block
        scores = mm(query[start:end], keys[:end], NT) * scale
        diag = jnp.where(keep, scores[:, start:], -jnp.inf)
        scores = jnp.concatenate([scores[:, :start], diag], axis=1) if start else diag
        exps = jnp.exp(scores - jnp.max(scores, axis=-1, keepdims=True))
        inverse = 1.0 / jnp.sum(exps, axis=-1, keepdims=True)
        store(start, end, mm((exps * inverse).astype(BF), vals[:end], NN).astype(BF))


def attend_columns(x_ref, cols, o_ref):
    blocks, three, _ = x_ref.shape
    rows = three // 3
    query, keys, vals = [
        x_ref[:, i * rows : (i + 1) * rows, cols].reshape(blocks * rows, HD) for i in range(3)
    ]

    def store(start, end, ctx):
        first, last = start // rows, end // rows
        o_ref[first:last, :, cols] = ctx.reshape(last - first, rows, HD)

    attend_head(query, keys, vals, store)


def attend_kernel(x_ref, o_ref):
    attend_columns(x_ref, slice(0, HD), o_ref)


def attend(x):
    blocks, three, part = x.shape
    rows = three // 3
    length = blocks * rows
    return pl.pallas_call(
        attend_kernel,
        grid=(part // HD,),
        out_shape=sds((blocks, rows, part)),
        in_specs=[pl.BlockSpec((blocks, three, HD), lambda h: (0, 0, h))],
        out_specs=pl.BlockSpec((blocks, rows, HD), lambda h: (0, 0, h)),
        compiler_params=pltpu.CompilerParams(vmem_limit_bytes=40 * MIB),
        cost_estimate=pl.CostEstimate(
            flops=4 * length * length * part,
            bytes_accessed=8 * length * part,
            transcendentals=length * length * part // HD,
        ),
    )(x)


INNER, COLS, PLANE, ATTEND = 0, 1, 5, 6


def halves_kernel(place_ref, q_ref, k_ref, v_ref, first_ref, second_ref):
    rows, width = q_ref.shape
    half = width // 2

    def copy(lower, upper):
        for i, ref in enumerate((q_ref, k_ref, v_ref)):
            lower[i * rows : (i + 1) * rows] = ref[:, :half]
            upper[i * rows : (i + 1) * rows] = ref[:, half:]

    @pl.when(place_ref[PLANE] < 2)
    def _():
        copy(first_ref, second_ref)

    @pl.when(place_ref[PLANE] >= 2)
    def _():
        copy(second_ref, first_ref)


def middle_kernel(place_ref, own_in, near_in, mid_in, far_in, *refs):
    *outs, x_ref, ctx_ref, sems = refs
    blocks, three, half = x_ref.shape
    rows = three // 3

    @pl.when(place_ref[INNER] == 1)
    def _():
        copies = [
            pltpu.make_async_copy(ref, x_ref.at[place_ref[ATTEND + i]], sems.at[i])
            for i, ref in enumerate((own_in, near_in, mid_in, far_in))
        ]
        for copy in copies:
            copy.start()
        for copy in copies:
            copy.wait()

        def step(i, carry):
            for j in range(2):
                cols = pl.ds(pl.multiple_of((2 * i + j) * HD, HD), HD)
                attend_columns(x_ref, cols, ctx_ref)
            return carry

        lax.fori_loop(0, half // HD // 2, step, 0)
        for i, out in enumerate(outs):
            out[...] = ctx_ref[place_ref[ATTEND + i]]


def line_of_four(place, queries, keys, values, gate, up, down, cot_rows):
    rows, width = queries.shape
    half = width // 2
    block = sds((3 * rows, half))
    first, second = call(
        halves_kernel,
        (block, block),
        (place, queries, keys, values),
        [SMEM, VMEM, VMEM, VMEM],
        moved=12 * rows * width,
    )
    gate_end = send(gate, OUTWARD)
    up_end = send(up, OUTWARD)
    down_end = send(down, OUTWARD, gate_end)
    gate_mid = send(gate, MIDDLE)
    gate_far = send(gate_mid, OUTWARD)
    near = send(first, INWARD, gate_mid, gate_end)
    mid = send(second, MIDDLE, gate_mid, gate_end)
    far = send(second, [(0, 2), (3, 1)], gate_mid, gate_end)
    piece = sds((rows, half))
    pieces = call(
        middle_kernel,
        (piece,) * 4,
        (place, first, near, mid, far),
        [SMEM] + [HBM] * 4,
        [
            pltpu.VMEM((4, 3 * rows, half), BF),
            pltpu.VMEM((4, rows, half), BF),
            pltpu.SemaphoreType.DMA((4,)),
        ],
        flops=64 * rows * rows * half,
        moved=32 * rows * half,
        after=(gate_end, up_end, gate_far, cot_rows),
    )
    up_mid = send(up, MIDDLE, near, mid, far)
    gate_inner = send(gate, INWARD, near, far, gate_end, up_end)
    up_inner = send(up, INWARD, near, far, gate_end, up_end)
    down_inner = send(down, INWARD, gate_inner)
    own, near, mid, far = lax.optimization_barrier((*pieces, gate_inner, down_end))[:4]
    mid = send(mid, MIDDLE)
    far = send(far, [(2, 0), (1, 3)])
    up_far = send(up_mid, OUTWARD, pieces[0])
    near = send(near, OUTWARD, up_far)
    gate_mid_near = send(gate_inner, MIDDLE)
    up_mid_near = send(up_inner, MIDDLE, pieces[0])
    down_mid = send(down, MIDDLE, gate_mid_near)
    down_mid_near = send(down_inner, MIDDLE, up_mid_near)
    gate_far_near = send(gate_mid_near, OUTWARD)
    up_far_near = send(up_mid_near, OUTWARD, gate_far_near)
    down_far = send(down_mid, OUTWARD, gate_far_near)
    down_far_near = send(down_mid_near, OUTWARD, up_far_near)
    norm_after = (gate_mid_near,)
    up_after = (down_mid_near,)
    gate_in = [
        [gate],
        [gate_inner, gate_end],
        [gate_mid, gate_far],
        [gate_mid_near, gate_far_near],
    ]
    up_in = [[up], [up_inner, up_end], [up_mid, up_far], [up_mid_near, up_far_near]]
    down_in = [
        [down],
        [down_inner, down_end],
        [down_mid, down_far],
        [down_mid_near, down_far_near],
    ]
    return (own, near, mid, far), gate_in, up_in, down_in, norm_after, up_after


def join_middle(place_ref, pieces, ctx_ref):
    own, near, mid, far = pieces
    half = own.shape[1]
    for plane, (lower, upper) in enumerate(((near, far), (own, mid), (mid, own), (far, near))):

        @pl.when(place_ref[PLANE] == plane)
        def _(lower=lower, upper=upper):
            ctx_ref[:, :half] = lower[...]
            ctx_ref[:, half:] = upper[...]


def join_groups(place_ref, pieces, ctx_ref):
    (ctx,) = pieces
    groups, _, part = ctx.shape
    for g in range(groups):
        ctx_ref[:, g * part : (g + 1) * part] = ctx[g]


def slot_rows(ids_t, owners, cap):
    tokens = ids_t.shape[1]
    experts = lax.broadcasted_iota(jnp.int32, (owners, tokens), 0)
    first = (experts == ids_t[0:1]).astype(F32)
    second = (experts == ids_t[1:2]).astype(F32)
    src = lax.broadcasted_iota(jnp.int32, (tokens, tokens), 0)
    dst = lax.broadcasted_iota(jnp.int32, (tokens, tokens), 1)
    earlier = (src < dst).astype(F32).astype(BF)
    count = mm((first + second).astype(BF), earlier, NN)
    slot0 = jnp.sum(first * count, axis=0, keepdims=True).astype(jnp.int32)
    slot1 = jnp.sum(second * count, axis=0, keepdims=True).astype(jnp.int32)
    return ids_t[0:1] * cap + slot0, ids_t[1:2] * cap + slot1


def slot_cols(ids, owners, cap):
    tokens = ids.shape[0]
    experts = lax.broadcasted_iota(jnp.int32, (tokens, owners), 1)
    first = (experts == ids[:, 0:1]).astype(F32)
    second = (experts == ids[:, 1:2]).astype(F32)
    dst = lax.broadcasted_iota(jnp.int32, (tokens, tokens), 0)
    src = lax.broadcasted_iota(jnp.int32, (tokens, tokens), 1)
    earlier = (src < dst).astype(F32).astype(BF)
    count = mm(earlier, (first + second).astype(BF), NN)
    slot0 = jnp.sum(first * count, axis=1, keepdims=True).astype(jnp.int32)
    slot1 = jnp.sum(second * count, axis=1, keepdims=True).astype(jnp.int32)
    return ids[:, 0:1] * cap + slot0, ids[:, 1:2] * cap + slot1


def one_hot(hit):
    return jnp.where(hit, 1.0, 0.0).astype(BF)


def send_cot_kernel(owners, cap, ids_ref, w_ref, cot_ref, o_ref):
    tokens = cot_ref.shape[0]
    at0, at1 = slot_rows(ids_ref[...], owners, cap)
    rows = lax.broadcasted_iota(jnp.int32, (owners * cap, tokens), 0)
    cot = cot_ref[...].astype(F32)
    o_ref[...] = (
        mm(one_hot(rows == at0), (w_ref[:, 0:1] * cot).astype(BF), NN)
        + mm(one_hot(rows == at1), (w_ref[:, 1:2] * cot).astype(BF), NN)
    ).astype(BF)


def norm_kernel(owners, cap, join, place_ref, ids_ref, resid_ref, gain_ref, *refs):
    *pieces, stream_ref, o_ref, ctx_ref = refs
    tokens, width = resid_ref.shape
    join(place_ref, pieces, ctx_ref)
    stream = (resid_ref[...].astype(F32) + ctx_ref[...].astype(F32)).astype(BF)
    stream_ref[...] = stream
    stream = stream.astype(F32)
    square = jnp.sum(stream * stream, axis=-1, keepdims=True)
    inv_rms = lax.rsqrt(square / width + 1e-05)
    at0, at1 = slot_rows(ids_ref[...], owners, cap)
    rows = lax.broadcasted_iota(jnp.int32, (owners * cap, tokens), 0)
    pick = one_hot((rows == at0) | (rows == at1))
    normed = ((stream_ref[...].astype(F32) * inv_rms) * gain_ref[...]).astype(BF)
    o_ref[...] = mm(pick, normed, NN).astype(BF)


def fetch(inner, choices, dst, sem):
    if len(choices) == 1:
        pltpu.make_async_copy(choices[0], dst, sem).start()
        return

    @pl.when(inner == 1)
    def _():
        pltpu.make_async_copy(choices[0], dst, sem).start()

    @pl.when(inner == 0)
    def _():
        pltpu.make_async_copy(choices[1], dst, sem).start()


def arrived(choices, dst, sem):
    pltpu.make_async_copy(choices[0], dst, sem).wait()


def regroup(refs, shape):
    refs = list(refs)
    return [[refs.pop(0) for _ in range(size)] for size in shape], refs


def cols_of(place_ref, slot, part):
    return pl.ds(pl.multiple_of(place_ref[COLS + slot] * part, part), part)


def gate_kernel(shape, place_ref, x_ref, *refs):
    slots = len(shape)
    gate_in, refs = regroup(refs, shape)
    o_ref, gate_w, sems = refs
    inner = place_ref[INNER]
    for j in range(slots):
        fetch(inner, gate_in[j], gate_w.at[j], sems.at[j])
    o_ref[...] = by_slots(place_ref, x_ref, gate_in, gate_w, sems)


def by_slots(place_ref, x_ref, weight_in, weight, sems):
    slots, _, part = weight.shape
    total = None
    for j in range(slots):
        rows = x_ref[:, cols_of(place_ref, j, part)]
        arrived(weight_in[j], weight.at[j], sems.at[j])
        term = mm(rows, weight[j], NT)
        total = term if total is None else total + term
    return total


def up_kernel(shape, place_ref, x_ref, gate_ref, *refs):
    slots = len(shape)
    up_in, refs = regroup(refs, shape)
    hidden_ref, to_gate_ref, to_up_ref, up_w, sems = refs
    inner = place_ref[INNER]
    for j in range(slots):
        fetch(inner, up_in[j], up_w.at[j], sems.at[j])
    gate = gate_ref[...]
    sigma = 1.0 / (1.0 + jnp.exp(-gate))
    silu = gate * sigma
    to_up_ref[...] = silu
    to_gate_ref[...] = sigma * (1.0 + gate * (1.0 - sigma))
    up = by_slots(place_ref, x_ref, up_in, up_w, sems)
    hidden_ref[...] = (to_up_ref[...] * up).astype(BF)
    to_gate_ref[...] = up * to_gate_ref[...]


def down_kernel(shape, first, place_ref, hidden_ref, cot_ref, *refs):
    slots = len(shape)
    refs = list(refs)
    total = refs.pop(0)[...] if first else None
    down_in, refs = regroup(refs, shape)
    out_ref, d_hidden_ref, down_w, sems = refs
    part = down_w.shape[2]
    inner = place_ref[INNER]
    for j in range(slots):
        fetch(inner, down_in[j], down_w.at[j], sems.at[j])
    for j in range(slots):
        rows = cot_ref[:, cols_of(place_ref, first + j, part)]
        arrived(down_in[j], down_w.at[j], sems.at[j])
        term = mm(rows, down_w[j], NT)
        total = term if total is None else total + term
        out_ref[:, j * part : (j + 1) * part] = mm(hidden_ref[...], down_w[j], NN).astype(BF)
    d_hidden_ref[...] = total


def grad_kernel(
    shape, place_ref, hidden_in, cot_in, d_hidden_in, to_gate_in, to_up_in, *refs
):
    slots = len(shape) - 1
    down_in, refs = regroup(refs, shape[-1:])
    gate_in, refs = regroup(refs, shape[:-1])
    up_in, refs = regroup(refs, shape[:-1])
    o_ref, down_w, gate_w, up_w, sems = refs[:5]
    hidden_ref, cot_ref, d_hidden_ref, to_gate_ref, to_up_ref = refs[5:]
    part = down_w.shape[1]
    inner = place_ref[INNER]
    last = place_ref[COLS + cot_in.shape[1] // part - 1]
    pairs = [
        (cot_in.at[:, pl.ds(pl.multiple_of(last * part, part), part)], cot_ref),
        (d_hidden_in, d_hidden_ref),
        (to_gate_in, to_gate_ref),
        (to_up_in, to_up_ref),
        (hidden_in, hidden_ref),
    ]
    fetch(inner, down_in[0], down_w, sems.at[2, 0])
    copies = [
        pltpu.make_async_copy(src, dst, sems.at[3 + i, 0]) for i, (src, dst) in enumerate(pairs)
    ]
    for copy in copies:
        copy.start()
    for j in range(slots):
        fetch(inner, gate_in[j], gate_w.at[j], sems.at[0, j])
        fetch(inner, up_in[j], up_w.at[j], sems.at[1, j])
    arrived(down_in[0], down_w, sems.at[2, 0])
    for copy in copies:
        copy.wait()
    d_hidden = d_hidden_ref[...] + mm(cot_ref[...], down_w[...], NT)
    d_gate = (d_hidden * to_gate_ref[...]).astype(BF)
    d_up = (d_hidden * to_up_ref[...]).astype(BF)
    o_ref[:, slots * part :] = mm(hidden_ref[...], down_w[...], NN).astype(BF)
    for j in range(slots):
        arrived(gate_in[j], gate_w.at[j], sems.at[0, j])
        arrived(up_in[j], up_w.at[j], sems.at[1, j])
        o_ref[:, j * part : (j + 1) * part] = (
            mm(d_gate, gate_w[j], NN) + mm(d_up, up_w[j], NN)
        ).astype(BF)


def final_kernel(
    owners,
    cap,
    place_ref,
    ids_ref,
    w_ref,
    gain_ref,
    stream_ref,
    cot_ref,
    first_ref,
    second_ref,
    last_ref,
    output_ref,
    grad_ref,
    d_normed_ref,
):
    tokens, width = stream_ref.shape
    done = first_ref.shape[1] + second_ref.shape[1]
    part = width - done
    slots = width // part
    early = first_ref.shape[1] // part
    at0, at1 = slot_cols(ids_ref[...], owners, cap)
    rows = lax.broadcasted_iota(jnp.int32, (tokens, owners * cap), 1)
    pick0, pick1 = one_hot(rows == at0), one_hot(rows == at1)
    both = pick0 + pick1
    w0, w1 = w_ref[:, 0:1], w_ref[:, 1:2]
    square = jnp.zeros((tokens, 1), F32)
    dot = jnp.zeros((tokens, 1), F32)
    for j in range(slots):
        cols = cols_of(place_ref, j, part)
        if j < early:
            pairs = first_ref[:, j * part : (j + 1) * part]
        elif j < slots - 1:
            pairs = second_ref[:, (j - early) * part : (j - early + 1) * part]
        else:
            pairs = last_ref[:, width:]
        stream = stream_ref[:, cols].astype(F32)
        mixed = w0 * mm(pick0, pairs, NN) + w1 * mm(pick1, pairs, NN)
        output_ref[:, cols] = (stream + mixed).astype(BF)
        grads = last_ref[:, j * part : (j + 1) * part]
        gained = mm(both, grads, NN) * gain_ref[:, cols]
        d_normed_ref[:, cols] = gained
        square = square + jnp.sum(stream * stream, axis=-1, keepdims=True)
        dot = dot + jnp.sum(gained * stream, axis=-1, keepdims=True)
    inv_rms = lax.rsqrt(square / width + 1e-05)
    mean = dot * inv_rms / width
    unit_rows = stream_ref[...].astype(F32) * inv_rms
    d_stream = inv_rms * (d_normed_ref[...] - unit_rows * mean)
    grad_ref[...] = (cot_ref[...].astype(F32) + d_stream).astype(BF)


MIDDLE = [(1, 2), (2, 1)]
OUTWARD = [(1, 0), (2, 3)]
INWARD = [(0, 1), (3, 2)]


def gather_all(shard, groups):
    whole_weight = lax.all_gather(shard, "seq", axis=0)
    return [[whole_weight[j]] for j in range(groups)]


def send(array, pairs, *first):
    return lax.ppermute(gated(array, *first), "seq", pairs)


def places(groups):
    if groups == 4:
        own = lax.axis_index("seq")
        table = jnp.array(
            [
                [0, 0, 1, 2, 3, 0, 0, 0, 0, 0],
                [1, 1, 0, 2, 3, 1, 1, 0, 2, 3],
                [1, 2, 3, 1, 0, 2, 2, 3, 1, 0],
                [0, 3, 2, 1, 0, 3, 0, 0, 0, 0],
            ],
            jnp.int32,
        )
        return table[own]
    return jnp.arange(-1, groups, dtype=jnp.int32)


def exchange(rows, owners, axis):
    total, width = rows.shape
    rows = rows.reshape(owners, total // owners, width)
    rows = lax.all_to_all(rows, axis, split_axis=0, concat_axis=0, tiled=True)
    return rows.reshape(total, width)


def flat(slots):
    return [ref for choices in slots for ref in choices]


def per_device(
    queries,
    keys,
    values,
    resid,
    norm_gain,
    w_gate,
    w_up,
    w_down,
    expert_ids,
    route_weights,
    cotangent,
):
    groups = lax.axis_size("seq")
    owners = lax.axis_size("exp")
    tokens, width = queries.shape[1:]
    ffw = w_gate.shape[2]
    part = width // groups
    cap = max(2, tokens * 10 // (4 * owners))
    total = owners * cap
    ids = expert_ids[0]
    ids_t = ids.T
    weights = route_weights[0]
    gain = norm_gain[None]
    cot = cotangent[0]
    place = places(groups)

    one = 2 * total * width * ffw
    send_cot = call(
        functools.partial(send_cot_kernel, owners, cap),
        sds((total, width)),
        (ids_t, weights, cot),
        [VMEM] * 3,
        flops=4 * total * tokens * width,
        moved=2 * (total + tokens) * width,
    )
    cot_rows = exchange(send_cot, owners, "exp")
    shards = (w_gate[0].T, w_up[0].T, w_down[0])
    if groups == 4:
        join = join_middle
        pieces, gate_in, up_in, down_in, norm_after, up_after = line_of_four(
            place, queries[0], keys[0], values[0], *shards, cot_rows
        )
    else:
        join = join_groups
        gate_in, up_in, down_in = [gather_all(shard, groups) for shard in shards]
        packed = pack(queries[0], keys[0], values[0], groups)
        heads = lax.all_to_all(packed, "seq", split_axis=0, concat_axis=0, tiled=True)
        ctx = attend(heads)
        pieces = (lax.all_to_all(ctx, "seq", split_axis=0, concat_axis=0, tiled=True),)
        norm_after = up_after = ()
    shape = [len(choices) for choices in gate_in]

    stream, send_rows = call(
        functools.partial(norm_kernel, owners, cap, join),
        (sds((tokens, width)), sds((total, width))),
        (place, ids_t, resid[0], gain, *pieces),
        [SMEM] + [VMEM] * (3 + len(pieces)),
        [pltpu.VMEM((tokens, width), BF)],
        flops=2 * total * tokens * width,
        moved=2 * (total + 3 * tokens) * width,
        after=norm_after,
    )
    rows = exchange(send_rows, owners, "exp")

    full_w = pltpu.VMEM((groups, ffw, part), BF)
    gate_pre = call(
        functools.partial(gate_kernel, shape),
        sds((total, ffw), F32),
        (place, rows, *flat(gate_in)),
        [SMEM, VMEM] + [HBM] * sum(shape),
        [full_w, pltpu.SemaphoreType.DMA((groups,))],
        flops=one,
        moved=2 * width * ffw + 2 * total * width + 4 * total * ffw,
    )
    hidden, to_gate, to_up = call(
        functools.partial(up_kernel, shape),
        (sds((total, ffw)), sds((total, ffw), F32), sds((total, ffw), F32)),
        (place, rows, gate_pre, *flat(up_in)),
        [SMEM, VMEM, VMEM] + [HBM] * sum(shape),
        [full_w, pltpu.SemaphoreType.DMA((groups,))],
        flops=one,
        moved=2 * width * ffw + 2 * total * width + 14 * total * ffw,
        after=up_after,
    )
    d_hidden = ()
    backs = []
    early = groups // 2
    for first, end in ((0, early), (early, groups - 1)):
        here = shape[first:end]
        out, d_hidden = call(
            functools.partial(down_kernel, here, first),
            (sds((total, len(here) * part)), sds((total, ffw), F32)),
            (place, hidden, cot_rows, *([d_hidden] if first else []), *flat(down_in[first:end])),
            [SMEM] + [VMEM] * (3 if first else 2) + [HBM] * sum(here),
            [
                pltpu.VMEM((len(here), ffw, part), BF),
                pltpu.SemaphoreType.DMA((len(here),)),
            ],
            flops=2 * one * len(here) // groups,
            moved=2 * width * ffw * len(here) // groups + 4 * total * width + 10 * total * ffw,
        )
        backs.append(exchange(out, owners, "exp"))
    back = call(
        functools.partial(grad_kernel, [*shape, shape[-1]]),
        sds((total, width + part)),
        (
            place,
            hidden,
            cot_rows,
            d_hidden,
            to_gate,
            to_up,
            *flat(down_in[-1:]),
            *flat(gate_in),
            *flat(up_in),
        ),
        [SMEM] + [HBM] * (5 + shape[-1] + 2 * sum(shape)),
        [
            pltpu.VMEM((ffw, part), BF),
            full_w,
            full_w,
            pltpu.SemaphoreType.DMA((8, groups)),
            pltpu.VMEM((total, ffw), BF),
            pltpu.VMEM((total, part), BF),
            pltpu.VMEM((total, ffw), F32),
            pltpu.VMEM((total, ffw), F32),
            pltpu.VMEM((total, ffw), F32),
        ],
        flops=2 * one + 2 * one // groups,
        moved=4 * width * ffw + 4 * total * width + 14 * total * ffw,
    )
    back_last = exchange(back, owners, "exp")
    output, stream_grad = call(
        functools.partial(final_kernel, owners, cap),
        (sds((tokens, width)), sds((tokens, width))),
        (place, ids, weights, gain, stream, cot, *backs, back_last),
        [SMEM] + [VMEM] * 8,
        [pltpu.VMEM((tokens, width), F32)],
        flops=6 * total * tokens * width,
        moved=4 * total * width + 8 * tokens * width,
        vmem=16,
        held=True,
    )
    return (output[None], stream_grad[None])


def solution(mesh):
    placed = (
        P("exp", "seq", None),
        P("exp", "seq", None),
        P("exp", "seq", None),
        P("exp", "seq", None),
        P(),
        P("exp", "seq", None),
        P("exp", "seq", None),
        P("exp", None, "seq"),
        P("exp", "seq", None),
        P("exp", "seq", None),
        P("exp", "seq", None),
    )
    return jax.shard_map(
        per_device,
        mesh=mesh,
        in_specs=placed,
        out_specs=(P("exp", "seq", None), P("exp", "seq", None)),
        check_vma=False,
    )
```

```python
import functools

import jax
import jax.numpy as jnp
from jax import lax
from jax.experimental import pallas as pl
from jax.experimental.pallas import tpu as pltpu
from jax.sharding import PartitionSpec as P

HD = 128
BF = jnp.bfloat16
F32 = jnp.float32
MIB = 1 << 20
HBM = pl.BlockSpec(memory_space=pltpu.HBM)
VMEM = pl.BlockSpec(memory_space=pltpu.VMEM)
SMEM = pl.BlockSpec(memory_space=pltpu.SMEM)
NT = (((1,), (1,)), ((), ()))
NN = (((1,), (0,)), ((), ()))


def mm(a, b, dims):
    return lax.dot_general(a, b, dims, preferred_element_type=F32)


def whole(array):
    return pl.BlockSpec(array.shape, lambda i: (0,) * len(array.shape))


def call(kernel, outs, args, in_specs, scratch=(), flops=0, moved=0, vmem=56, after=(), held=False):
    count, extra = len(args), len(after)

    def body(*refs):
        kernel(*refs[:count], *refs[count + extra :])

    return pl.pallas_call(
        body,
        grid=() if held else (1,),
        out_shape=outs,
        in_specs=[
            *[
                whole(arg) if spec is VMEM and not held else spec
                for arg, spec in zip(args, in_specs)
            ],
            *[HBM] * extra,
        ],
        out_specs=jax.tree.map(lambda out: VMEM if held else whole(out), outs),
        scratch_shapes=list(scratch),
        compiler_params=pltpu.CompilerParams(vmem_limit_bytes=vmem * MIB),
        cost_estimate=pl.CostEstimate(flops=flops, bytes_accessed=moved, transcendentals=0),
    )(*args, *after)


def gated(array, *first):
    return lax.optimization_barrier((array, *first))[0] if first else array


def sds(shape, dtype=BF):
    return jax.ShapeDtypeStruct(shape, dtype)


def pack_kernel(q_ref, k_ref, v_ref, o_ref):
    rows = q_ref.shape[0]
    o_ref[0, 0:rows] = q_ref[...]
    o_ref[0, rows : 2 * rows] = k_ref[...]
    o_ref[0, 2 * rows : 3 * rows] = v_ref[...]


def pack(q, k, v, groups):
    rows, width = q.shape
    part = width // groups
    spec = pl.BlockSpec((rows, part), lambda g: (0, g))
    return pl.pallas_call(
        pack_kernel,
        grid=(groups,),
        out_shape=sds((groups, 3 * rows, part)),
        in_specs=[spec] * 3,
        out_specs=pl.BlockSpec((1, 3 * rows, part), lambda g: (g, 0, 0)),
        cost_estimate=pl.CostEstimate(
            flops=0, bytes_accessed=12 * rows * width, transcendentals=0
        ),
    )(q, k, v)


def attend_head(query, keys, vals, store):
    length = keys.shape[0]
    block = min(512, length)
    scale = HD ** (-0.5)
    row_ids = lax.broadcasted_iota(jnp.int32, (block, block), 0)
    col_ids = lax.broadcasted_iota(jnp.int32, (block, block), 1)
    keep = col_ids <= row_ids
    for start in range(0, length, block):
        end = start + block
        scores = mm(query[start:end], keys[:end], NT) * scale
        diag = jnp.where(keep, scores[:, start:], -jnp.inf)
        scores = jnp.concatenate([scores[:, :start], diag], axis=1) if start else diag
        exps = jnp.exp(scores - jnp.max(scores, axis=-1, keepdims=True))
        inverse = 1.0 / jnp.sum(exps, axis=-1, keepdims=True)
        store(start, end, mm((exps * inverse).astype(BF), vals[:end], NN).astype(BF))


def attend_columns(x_ref, cols, o_ref):
    blocks, three, _ = x_ref.shape
    rows = three // 3
    query, keys, vals = [
        x_ref[:, i * rows : (i + 1) * rows, cols].reshape(blocks * rows, HD) for i in range(3)
    ]

    def store(start, end, ctx):
        first, last = start // rows, end // rows
        o_ref[first:last, :, cols] = ctx.reshape(last - first, rows, HD)

    attend_head(query, keys, vals, store)


def attend_kernel(x_ref, o_ref):
    attend_columns(x_ref, slice(0, HD), o_ref)


def attend(x):
    blocks, three, part = x.shape
    rows = three // 3
    length = blocks * rows
    return pl.pallas_call(
        attend_kernel,
        grid=(part // HD,),
        out_shape=sds((blocks, rows, part)),
        in_specs=[pl.BlockSpec((blocks, three, HD), lambda h: (0, 0, h))],
        out_specs=pl.BlockSpec((blocks, rows, HD), lambda h: (0, 0, h)),
        compiler_params=pltpu.CompilerParams(vmem_limit_bytes=40 * MIB),
        cost_estimate=pl.CostEstimate(
            flops=4 * length * length * part,
            bytes_accessed=8 * length * part,
            transcendentals=length * length * part // HD,
        ),
    )(x)


INNER, COLS, PLANE, ATTEND = 0, 1, 5, 6


def halves_kernel(place_ref, q_ref, k_ref, v_ref, first_ref, second_ref):
    rows, width = q_ref.shape
    half = width // 2

    def copy(lower, upper):
        for i, ref in enumerate((q_ref, k_ref, v_ref)):
            lower[i * rows : (i + 1) * rows] = ref[:, :half]
            upper[i * rows : (i + 1) * rows] = ref[:, half:]

    @pl.when(place_ref[PLANE] < 2)
    def _():
        copy(first_ref, second_ref)

    @pl.when(place_ref[PLANE] >= 2)
    def _():
        copy(second_ref, first_ref)


def middle_kernel(place_ref, own_in, near_in, mid_in, far_in, *refs):
    *outs, x_ref, ctx_ref, sems = refs
    blocks, three, half = x_ref.shape
    rows = three // 3

    @pl.when(place_ref[INNER] == 1)
    def _():
        copies = [
            pltpu.make_async_copy(ref, x_ref.at[place_ref[ATTEND + i]], sems.at[i])
            for i, ref in enumerate((own_in, near_in, mid_in, far_in))
        ]
        for copy in copies:
            copy.start()
        for copy in copies:
            copy.wait()

        def step(i, carry):
            for j in range(2):
                cols = pl.ds(pl.multiple_of((2 * i + j) * HD, HD), HD)
                attend_columns(x_ref, cols, ctx_ref)
            return carry

        lax.fori_loop(0, half // HD // 2, step, 0)
        for i, out in enumerate(outs):
            out[...] = ctx_ref[place_ref[ATTEND + i]]


def line_of_four(place, queries, keys, values, gate, up, down, cot_rows):
    rows, width = queries.shape
    half = width // 2
    block = sds((3 * rows, half))
    first, second = call(
        halves_kernel,
        (block, block),
        (place, queries, keys, values),
        [SMEM, VMEM, VMEM, VMEM],
        moved=12 * rows * width,
    )
    gate_end = send(gate, OUTWARD)
    up_end = send(up, OUTWARD)
    down_end = send(down, OUTWARD, gate_end)
    gate_mid = send(gate, MIDDLE)
    gate_far = send(gate_mid, OUTWARD)
    near = send(first, INWARD, gate_mid, gate_end)
    mid = send(second, MIDDLE, gate_mid, gate_end)
    far = send(second, [(0, 2), (3, 1)], gate_mid, gate_end)
    piece = sds((rows, half))
    pieces = call(
        middle_kernel,
        (piece,) * 4,
        (place, first, near, mid, far),
        [SMEM] + [HBM] * 4,
        [
            pltpu.VMEM((4, 3 * rows, half), BF),
            pltpu.VMEM((4, rows, half), BF),
            pltpu.SemaphoreType.DMA((4,)),
        ],
        flops=64 * rows * rows * half,
        moved=32 * rows * half,
        after=(gate_end, up_end, gate_far, cot_rows),
    )
    up_mid = send(up, MIDDLE, near, mid, far)
    gate_inner = send(gate, INWARD, near, far, gate_end, up_end)
    up_inner = send(up, INWARD, near, far, gate_end, up_end)
    down_inner = send(down, INWARD, gate_inner)
    own, near, mid, far = lax.optimization_barrier((*pieces, gate_inner, down_end))[:4]
    mid = send(mid, MIDDLE)
    far = send(far, [(2, 0), (1, 3)])
    up_far = send(up_mid, OUTWARD, pieces[0])
    near = send(near, OUTWARD, up_far)
    gate_mid_near = send(gate_inner, MIDDLE)
    up_mid_near = send(up_inner, MIDDLE, pieces[0])
    down_mid = send(down, MIDDLE, gate_mid_near)
    down_mid_near = send(down_inner, MIDDLE, up_mid_near)
    gate_far_near = send(gate_mid_near, OUTWARD)
    up_far_near = send(up_mid_near, OUTWARD, gate_far_near)
    down_far = send(down_mid, OUTWARD, gate_far_near)
    down_far_near = send(down_mid_near, OUTWARD, up_far_near)
    norm_after = (gate_mid_near,)
    up_after = (down_mid_near,)
    gate_in = [
        [gate],
        [gate_inner, gate_end],
        [gate_mid, gate_far],
        [gate_mid_near, gate_far_near],
    ]
    up_in = [[up], [up_inner, up_end], [up_mid, up_far], [up_mid_near, up_far_near]]
    down_in = [
        [down],
        [down_inner, down_end],
        [down_mid, down_far],
        [down_mid_near, down_far_near],
    ]
    return (own, near, mid, far), gate_in, up_in, down_in, norm_after, up_after


def join_middle(place_ref, pieces, ctx_ref):
    own, near, mid, far = pieces
    half = own.shape[1]
    for plane, (lower, upper) in enumerate(((near, far), (own, mid), (mid, own), (far, near))):

        @pl.when(place_ref[PLANE] == plane)
        def _(lower=lower, upper=upper):
            ctx_ref[:, :half] = lower[...]
            ctx_ref[:, half:] = upper[...]


def join_groups(place_ref, pieces, ctx_ref):
    (ctx,) = pieces
    groups, _, part = ctx.shape
    for g in range(groups):
        ctx_ref[:, g * part : (g + 1) * part] = ctx[g]


def slot_rows(ids_t, owners, cap):
    tokens = ids_t.shape[1]
    experts = lax.broadcasted_iota(jnp.int32, (owners, tokens), 0)
    first = (experts == ids_t[0:1]).astype(F32)
    second = (experts == ids_t[1:2]).astype(F32)
    src = lax.broadcasted_iota(jnp.int32, (tokens, tokens), 0)
    dst = lax.broadcasted_iota(jnp.int32, (tokens, tokens), 1)
    earlier = (src < dst).astype(F32).astype(BF)
    count = mm((first + second).astype(BF), earlier, NN)
    slot0 = jnp.sum(first * count, axis=0, keepdims=True).astype(jnp.int32)
    slot1 = jnp.sum(second * count, axis=0, keepdims=True).astype(jnp.int32)
    return ids_t[0:1] * cap + slot0, ids_t[1:2] * cap + slot1


def slot_cols(ids, owners, cap):
    tokens = ids.shape[0]
    experts = lax.broadcasted_iota(jnp.int32, (tokens, owners), 1)
    first = (experts == ids[:, 0:1]).astype(F32)
    second = (experts == ids[:, 1:2]).astype(F32)
    dst = lax.broadcasted_iota(jnp.int32, (tokens, tokens), 0)
    src = lax.broadcasted_iota(jnp.int32, (tokens, tokens), 1)
    earlier = (src < dst).astype(F32).astype(BF)
    count = mm(earlier, (first + second).astype(BF), NN)
    slot0 = jnp.sum(first * count, axis=1, keepdims=True).astype(jnp.int32)
    slot1 = jnp.sum(second * count, axis=1, keepdims=True).astype(jnp.int32)
    return ids[:, 0:1] * cap + slot0, ids[:, 1:2] * cap + slot1


def one_hot(hit):
    return jnp.where(hit, 1.0, 0.0).astype(BF)


def send_cot_kernel(owners, cap, ids_ref, w_ref, cot_ref, o_ref):
    tokens = cot_ref.shape[0]
    at0, at1 = slot_rows(ids_ref[...], owners, cap)
    rows = lax.broadcasted_iota(jnp.int32, (owners * cap, tokens), 0)
    cot = cot_ref[...].astype(F32)
    o_ref[...] = (
        mm(one_hot(rows == at0), (w_ref[:, 0:1] * cot).astype(BF), NN)
        + mm(one_hot(rows == at1), (w_ref[:, 1:2] * cot).astype(BF), NN)
    ).astype(BF)


def norm_kernel(owners, cap, join, place_ref, ids_ref, resid_ref, gain_ref, *refs):
    *pieces, stream_ref, o_ref, ctx_ref = refs
    tokens, width = resid_ref.shape
    join(place_ref, pieces, ctx_ref)
    stream = (resid_ref[...].astype(F32) + ctx_ref[...].astype(F32)).astype(BF)
    stream_ref[...] = stream
    stream = stream.astype(F32)
    square = jnp.sum(stream * stream, axis=-1, keepdims=True)
    inv_rms = lax.rsqrt(square / width + 1e-05)
    at0, at1 = slot_rows(ids_ref[...], owners, cap)
    rows = lax.broadcasted_iota(jnp.int32, (owners * cap, tokens), 0)
    pick = one_hot((rows == at0) | (rows == at1))
    normed = ((stream_ref[...].astype(F32) * inv_rms) * gain_ref[...]).astype(BF)
    o_ref[...] = mm(pick, normed, NN).astype(BF)


def fetch(inner, choices, dst, sem):
    if len(choices) == 1:
        pltpu.make_async_copy(choices[0], dst, sem).start()
        return

    @pl.when(inner == 1)
    def _():
        pltpu.make_async_copy(choices[0], dst, sem).start()

    @pl.when(inner == 0)
    def _():
        pltpu.make_async_copy(choices[1], dst, sem).start()


def arrived(choices, dst, sem):
    pltpu.make_async_copy(choices[0], dst, sem).wait()


def regroup(refs, shape):
    refs = list(refs)
    return [[refs.pop(0) for _ in range(size)] for size in shape], refs


def cols_of(place_ref, slot, part):
    return pl.ds(pl.multiple_of(place_ref[COLS + slot] * part, part), part)


def gate_kernel(shape, place_ref, x_ref, *refs):
    slots = len(shape)
    gate_in, refs = regroup(refs, shape)
    o_ref, gate_w, sems = refs
    inner = place_ref[INNER]
    for j in range(slots):
        fetch(inner, gate_in[j], gate_w.at[j], sems.at[j])
    o_ref[...] = by_slots(place_ref, x_ref, gate_in, gate_w, sems)


def by_slots(place_ref, x_ref, weight_in, weight, sems):
    slots, _, part = weight.shape
    total = None
    for j in range(slots):
        rows = x_ref[:, cols_of(place_ref, j, part)]
        arrived(weight_in[j], weight.at[j], sems.at[j])
        term = mm(rows, weight[j], NT)
        total = term if total is None else total + term
    return total


def up_kernel(shape, place_ref, x_ref, gate_ref, *refs):
    slots = len(shape)
    up_in, refs = regroup(refs, shape)
    hidden_ref, to_gate_ref, to_up_ref, up_w, sems = refs
    inner = place_ref[INNER]
    for j in range(slots):
        fetch(inner, up_in[j], up_w.at[j], sems.at[j])
    gate = gate_ref[...]
    sigma = 1.0 / (1.0 + jnp.exp(-gate))
    silu = gate * sigma
    to_up_ref[...] = silu
    to_gate_ref[...] = sigma * (1.0 + gate * (1.0 - sigma))
    up = by_slots(place_ref, x_ref, up_in, up_w, sems)
    hidden_ref[...] = (to_up_ref[...] * up).astype(BF)
    to_gate_ref[...] = up * to_gate_ref[...]


def down_kernel(shape, place_ref, hidden_ref, cot_ref, *refs):
    slots = len(shape)
    down_in, refs = regroup(refs, shape)
    out_ref, d_hidden_ref, down_w, sems = refs
    part = down_w.shape[2]
    inner = place_ref[INNER]
    for j in range(slots):
        fetch(inner, down_in[j], down_w.at[j], sems.at[j])
    total = None
    for j in range(slots):
        rows = cot_ref[:, cols_of(place_ref, j, part)]
        arrived(down_in[j], down_w.at[j], sems.at[j])
        term = mm(rows, down_w[j], NT)
        total = term if total is None else total + term
        out_ref[:, j * part : (j + 1) * part] = mm(hidden_ref[...], down_w[j], NN).astype(BF)
    d_hidden_ref[...] = total


def grad_kernel(
    shape, late, place_ref, hidden_in, cot_in, d_hidden_in, to_gate_in, to_up_in, *refs
):
    slots = len(shape)
    down_in, refs = regroup(refs, shape[slots - late :])
    gate_in, refs = regroup(refs, shape)
    up_in, refs = regroup(refs, shape)
    o_ref, down_w, gate_w, up_w, sems = refs[:5]
    hidden_ref, cot_ref, d_hidden_ref, to_gate_ref, to_up_ref = refs[5:]
    part = down_w.shape[2]
    inner = place_ref[INNER]
    pairs = [
        (cot_in.at[:, cols_of(place_ref, slots - late + j, part)], cot_ref.at[j])
        for j in range(late)
    ]
    pairs += [
        (d_hidden_in, d_hidden_ref),
        (to_gate_in, to_gate_ref),
        (to_up_in, to_up_ref),
        (hidden_in, hidden_ref),
    ]
    for j in range(late):
        fetch(inner, down_in[j], down_w.at[j], sems.at[2, j])
    copies = [
        pltpu.make_async_copy(src, dst, sems.at[3 + i, 0]) for i, (src, dst) in enumerate(pairs)
    ]
    for copy in copies:
        copy.start()
    for j in range(slots):
        fetch(inner, gate_in[j], gate_w.at[j], sems.at[0, j])
        fetch(inner, up_in[j], up_w.at[j], sems.at[1, j])
    for j in range(late):
        arrived(down_in[j], down_w.at[j], sems.at[2, j])
    for copy in copies:
        copy.wait()
    d_hidden = d_hidden_ref[...]
    for j in range(late):
        d_hidden = d_hidden + mm(cot_ref[j], down_w[j], NT)
    d_gate = (d_hidden * to_gate_ref[...]).astype(BF)
    d_up = (d_hidden * to_up_ref[...]).astype(BF)
    for j in range(late):
        o_ref[:, (slots + j) * part : (slots + j + 1) * part] = mm(
            hidden_ref[...], down_w[j], NN
        ).astype(BF)
    for j in range(slots):
        arrived(gate_in[j], gate_w.at[j], sems.at[0, j])
        arrived(up_in[j], up_w.at[j], sems.at[1, j])
        o_ref[:, j * part : (j + 1) * part] = (
            mm(d_gate, gate_w[j], NN) + mm(d_up, up_w[j], NN)
        ).astype(BF)


def final_kernel(
    owners,
    cap,
    slots,
    place_ref,
    ids_ref,
    w_ref,
    gain_ref,
    stream_ref,
    cot_ref,
    first_ref,
    last_ref,
    output_ref,
    grad_ref,
    d_normed_ref,
):
    tokens, width = stream_ref.shape
    part = width // slots
    early = slots // 2
    at0, at1 = slot_cols(ids_ref[...], owners, cap)
    rows = lax.broadcasted_iota(jnp.int32, (tokens, owners * cap), 1)
    pick0, pick1 = one_hot(rows == at0), one_hot(rows == at1)
    both = pick0 + pick1
    w0, w1 = w_ref[:, 0:1], w_ref[:, 1:2]
    square = jnp.zeros((tokens, 1), F32)
    dot = jnp.zeros((tokens, 1), F32)
    for j in range(slots):
        cols = cols_of(place_ref, j, part)
        if j < early:
            pairs = first_ref[:, j * part : (j + 1) * part]
        else:
            at = width + (j - early) * part
            pairs = last_ref[:, at : at + part]
        stream = stream_ref[:, cols].astype(F32)
        mixed = w0 * mm(pick0, pairs, NN) + w1 * mm(pick1, pairs, NN)
        output_ref[:, cols] = (stream + mixed).astype(BF)
        grads = last_ref[:, j * part : (j + 1) * part]
        gained = mm(both, grads, NN) * gain_ref[:, cols]
        d_normed_ref[:, cols] = gained
        square = square + jnp.sum(stream * stream, axis=-1, keepdims=True)
        dot = dot + jnp.sum(gained * stream, axis=-1, keepdims=True)
    inv_rms = lax.rsqrt(square / width + 1e-05)
    mean = dot * inv_rms / width
    unit_rows = stream_ref[...].astype(F32) * inv_rms
    d_stream = inv_rms * (d_normed_ref[...] - unit_rows * mean)
    grad_ref[...] = (cot_ref[...].astype(F32) + d_stream).astype(BF)


MIDDLE = [(1, 2), (2, 1)]
OUTWARD = [(1, 0), (2, 3)]
INWARD = [(0, 1), (3, 2)]


def gather_all(shard, groups):
    whole_weight = lax.all_gather(shard, "seq", axis=0)
    return [[whole_weight[j]] for j in range(groups)]


def send(array, pairs, *first):
    return lax.ppermute(gated(array, *first), "seq", pairs)


def places(groups):
    if groups == 4:
        own = lax.axis_index("seq")
        table = jnp.array(
            [
                [0, 0, 1, 2, 3, 0, 0, 0, 0, 0],
                [1, 1, 0, 2, 3, 1, 1, 0, 2, 3],
                [1, 2, 3, 1, 0, 2, 2, 3, 1, 0],
                [0, 3, 2, 1, 0, 3, 0, 0, 0, 0],
            ],
            jnp.int32,
        )
        return table[own]
    return jnp.arange(-1, groups, dtype=jnp.int32)


def exchange(rows, owners, axis):
    total, width = rows.shape
    rows = rows.reshape(owners, total // owners, width)
    rows = lax.all_to_all(rows, axis, split_axis=0, concat_axis=0, tiled=True)
    return rows.reshape(total, width)


def flat(slots):
    return [ref for choices in slots for ref in choices]


def per_device(
    queries,
    keys,
    values,
    resid,
    norm_gain,
    w_gate,
    w_up,
    w_down,
    expert_ids,
    route_weights,
    cotangent,
):
    groups = lax.axis_size("seq")
    owners = lax.axis_size("exp")
    tokens, width = queries.shape[1:]
    ffw = w_gate.shape[2]
    part = width // groups
    cap = max(2, tokens * 10 // (4 * owners))
    total = owners * cap
    ids = expert_ids[0]
    ids_t = ids.T
    weights = route_weights[0]
    gain = norm_gain[None]
    cot = cotangent[0]
    place = places(groups)

    one = 2 * total * width * ffw
    send_cot = call(
        functools.partial(send_cot_kernel, owners, cap),
        sds((total, width)),
        (ids_t, weights, cot),
        [VMEM] * 3,
        flops=4 * total * tokens * width,
        moved=2 * (total + tokens) * width,
    )
    cot_rows = exchange(send_cot, owners, "exp")
    shards = (w_gate[0].T, w_up[0].T, w_down[0])
    if groups == 4:
        join = join_middle
        pieces, gate_in, up_in, down_in, norm_after, up_after = line_of_four(
            place, queries[0], keys[0], values[0], *shards, cot_rows
        )
    else:
        join = join_groups
        gate_in, up_in, down_in = [gather_all(shard, groups) for shard in shards]
        packed = pack(queries[0], keys[0], values[0], groups)
        heads = lax.all_to_all(packed, "seq", split_axis=0, concat_axis=0, tiled=True)
        ctx = attend(heads)
        pieces = (lax.all_to_all(ctx, "seq", split_axis=0, concat_axis=0, tiled=True),)
        norm_after = up_after = ()
    shape = [len(choices) for choices in gate_in]

    stream, send_rows = call(
        functools.partial(norm_kernel, owners, cap, join),
        (sds((tokens, width)), sds((total, width))),
        (place, ids_t, resid[0], gain, *pieces),
        [SMEM] + [VMEM] * (3 + len(pieces)),
        [pltpu.VMEM((tokens, width), BF)],
        flops=2 * total * tokens * width,
        moved=2 * (total + 3 * tokens) * width,
        after=norm_after,
    )
    rows = exchange(send_rows, owners, "exp")

    full_w = pltpu.VMEM((groups, ffw, part), BF)
    gate_pre = call(
        functools.partial(gate_kernel, shape),
        sds((total, ffw), F32),
        (place, rows, *flat(gate_in)),
        [SMEM, VMEM] + [HBM] * sum(shape),
        [full_w, pltpu.SemaphoreType.DMA((groups,))],
        flops=one,
        moved=2 * width * ffw + 2 * total * width + 4 * total * ffw,
    )
    hidden, to_gate, to_up = call(
        functools.partial(up_kernel, shape),
        (sds((total, ffw)), sds((total, ffw), F32), sds((total, ffw), F32)),
        (place, rows, gate_pre, *flat(up_in)),
        [SMEM, VMEM, VMEM] + [HBM] * sum(shape),
        [full_w, pltpu.SemaphoreType.DMA((groups,))],
        flops=one,
        moved=2 * width * ffw + 2 * total * width + 14 * total * ffw,
        after=up_after,
    )
    early = groups // 2
    late = groups - early
    out_first, d_hidden = call(
        functools.partial(down_kernel, shape[:early]),
        (sds((total, early * part)), sds((total, ffw), F32)),
        (place, hidden, cot_rows, *flat(down_in[:early])),
        [SMEM, VMEM, VMEM] + [HBM] * sum(shape[:early]),
        [pltpu.VMEM((early, ffw, part), BF), pltpu.SemaphoreType.DMA((early,))],
        flops=2 * one * early // groups,
        moved=width * ffw + 3 * total * width + 6 * total * ffw,
    )
    back_first = exchange(out_first, owners, "exp")
    back = call(
        functools.partial(grad_kernel, shape, late),
        sds((total, width + late * part)),
        (
            place,
            hidden,
            cot_rows,
            d_hidden,
            to_gate,
            to_up,
            *flat(down_in[early:]),
            *flat(gate_in),
            *flat(up_in),
        ),
        [SMEM] + [HBM] * (5 + sum(shape[early:]) + 2 * sum(shape)),
        [
            pltpu.VMEM((late, ffw, part), BF),
            full_w,
            full_w,
            pltpu.SemaphoreType.DMA((7 + late, groups)),
            pltpu.VMEM((total, ffw), BF),
            pltpu.VMEM((late, total, part), BF),
            pltpu.VMEM((total, ffw), F32),
            pltpu.VMEM((total, ffw), F32),
            pltpu.VMEM((total, ffw), F32),
        ],
        flops=2 * one + 2 * one * late // groups,
        moved=5 * width * ffw + 4 * total * width + 14 * total * ffw,
    )
    back_last = exchange(back, owners, "exp")
    output, stream_grad = call(
        functools.partial(final_kernel, owners, cap, groups),
        (sds((tokens, width)), sds((tokens, width))),
        (place, ids, weights, gain, stream, cot, back_first, back_last),
        [SMEM] + [VMEM] * 7,
        [pltpu.VMEM((tokens, width), F32)],
        flops=6 * total * tokens * width,
        moved=4 * total * width + 8 * tokens * width,
        vmem=16,
        held=True,
    )
    return (output[None], stream_grad[None])


def solution(mesh):
    placed = (
        P("exp", "seq", None),
        P("exp", "seq", None),
        P("exp", "seq", None),
        P("exp", "seq", None),
        P(),
        P("exp", "seq", None),
        P("exp", "seq", None),
        P("exp", None, "seq"),
        P("exp", "seq", None),
        P("exp", "seq", None),
        P("exp", "seq", None),
    )
    return jax.shard_map(
        per_device,
        mesh=mesh,
        in_specs=placed,
        out_specs=(P("exp", "seq", None), P("exp", "seq", None)),
        check_vma=False,
    )
```

```python
import functools

import jax
import jax.numpy as jnp
from jax import lax
from jax.experimental import pallas as pl
from jax.experimental.pallas import tpu as pltpu
from jax.sharding import PartitionSpec as P

HD = 128
BF = jnp.bfloat16
F32 = jnp.float32
MIB = 1 << 20
HBM = pl.BlockSpec(memory_space=pltpu.HBM)
VMEM = pl.BlockSpec(memory_space=pltpu.VMEM)
SMEM = pl.BlockSpec(memory_space=pltpu.SMEM)
NT = (((1,), (1,)), ((), ()))
NN = (((1,), (0,)), ((), ()))


def mm(a, b, dims):
    return lax.dot_general(a, b, dims, preferred_element_type=F32)


def whole(array):
    return pl.BlockSpec(array.shape, lambda i: (0,) * len(array.shape))


def call(kernel, outs, args, in_specs, scratch=(), flops=0, moved=0, vmem=56, after=(), held=False):
    count, extra = len(args), len(after)

    def body(*refs):
        kernel(*refs[:count], *refs[count + extra :])

    return pl.pallas_call(
        body,
        grid=() if held else (1,),
        out_shape=outs,
        in_specs=[
            *[
                whole(arg) if spec is VMEM and not held else spec
                for arg, spec in zip(args, in_specs)
            ],
            *[HBM] * extra,
        ],
        out_specs=jax.tree.map(lambda out: VMEM if held else whole(out), outs),
        scratch_shapes=list(scratch),
        compiler_params=pltpu.CompilerParams(vmem_limit_bytes=vmem * MIB),
        cost_estimate=pl.CostEstimate(flops=flops, bytes_accessed=moved, transcendentals=0),
    )(*args, *after)


def gated(array, *first):
    return lax.optimization_barrier((array, *first))[0] if first else array


def sds(shape, dtype=BF):
    return jax.ShapeDtypeStruct(shape, dtype)


def pack_kernel(q_ref, k_ref, v_ref, o_ref):
    rows = q_ref.shape[0]
    o_ref[0, 0:rows] = q_ref[...]
    o_ref[0, rows : 2 * rows] = k_ref[...]
    o_ref[0, 2 * rows : 3 * rows] = v_ref[...]


def pack(q, k, v, groups):
    rows, width = q.shape
    part = width // groups
    spec = pl.BlockSpec((rows, part), lambda g: (0, g))
    return pl.pallas_call(
        pack_kernel,
        grid=(groups,),
        out_shape=sds((groups, 3 * rows, part)),
        in_specs=[spec] * 3,
        out_specs=pl.BlockSpec((1, 3 * rows, part), lambda g: (g, 0, 0)),
        cost_estimate=pl.CostEstimate(
            flops=0, bytes_accessed=12 * rows * width, transcendentals=0
        ),
    )(q, k, v)


def attend_head(query, keys, vals, store):
    length = keys.shape[0]
    block = min(512, length)
    scale = HD ** (-0.5)
    row_ids = lax.broadcasted_iota(jnp.int32, (block, block), 0)
    col_ids = lax.broadcasted_iota(jnp.int32, (block, block), 1)
    keep = col_ids <= row_ids
    for start in range(0, length, block):
        end = start + block
        scores = mm(query[start:end], keys[:end], NT) * scale
        diag = jnp.where(keep, scores[:, start:], -jnp.inf)
        scores = jnp.concatenate([scores[:, :start], diag], axis=1) if start else diag
        exps = jnp.exp(scores - jnp.max(scores, axis=-1, keepdims=True))
        inverse = 1.0 / jnp.sum(exps, axis=-1, keepdims=True)
        store(start, end, mm((exps * inverse).astype(BF), vals[:end], NN).astype(BF))


def attend_columns(x_ref, cols, o_ref):
    blocks, three, _ = x_ref.shape
    rows = three // 3
    query, keys, vals = [
        x_ref[:, i * rows : (i + 1) * rows, cols].reshape(blocks * rows, HD) for i in range(3)
    ]

    def store(start, end, ctx):
        first, last = start // rows, end // rows
        o_ref[first:last, :, cols] = ctx.reshape(last - first, rows, HD)

    attend_head(query, keys, vals, store)


def attend_kernel(x_ref, o_ref):
    attend_columns(x_ref, slice(0, HD), o_ref)


def attend(x):
    blocks, three, part = x.shape
    rows = three // 3
    length = blocks * rows
    return pl.pallas_call(
        attend_kernel,
        grid=(part // HD,),
        out_shape=sds((blocks, rows, part)),
        in_specs=[pl.BlockSpec((blocks, three, HD), lambda h: (0, 0, h))],
        out_specs=pl.BlockSpec((blocks, rows, HD), lambda h: (0, 0, h)),
        compiler_params=pltpu.CompilerParams(vmem_limit_bytes=40 * MIB),
        cost_estimate=pl.CostEstimate(
            flops=4 * length * length * part,
            bytes_accessed=8 * length * part,
            transcendentals=length * length * part // HD,
        ),
    )(x)


INNER, COLS, PLANE, ATTEND = 0, 1, 5, 6


def halves_kernel(place_ref, q_ref, k_ref, v_ref, first_ref, second_ref):
    rows, width = q_ref.shape
    half = width // 2

    def copy(lower, upper):
        for i, ref in enumerate((q_ref, k_ref, v_ref)):
            lower[i * rows : (i + 1) * rows] = ref[:, :half]
            upper[i * rows : (i + 1) * rows] = ref[:, half:]

    @pl.when(place_ref[PLANE] < 2)
    def _():
        copy(first_ref, second_ref)

    @pl.when(place_ref[PLANE] >= 2)
    def _():
        copy(second_ref, first_ref)


def middle_kernel(place_ref, own_in, near_in, mid_in, far_in, *refs):
    *outs, x_ref, ctx_ref, sems = refs
    blocks, three, half = x_ref.shape
    rows = three // 3

    @pl.when(place_ref[INNER] == 1)
    def _():
        copies = [
            pltpu.make_async_copy(ref, x_ref.at[place_ref[ATTEND + i]], sems.at[i])
            for i, ref in enumerate((own_in, near_in, mid_in, far_in))
        ]
        for copy in copies:
            copy.start()
        for copy in copies:
            copy.wait()

        def step(i, carry):
            for j in range(2):
                cols = pl.ds(pl.multiple_of((2 * i + j) * HD, HD), HD)
                attend_columns(x_ref, cols, ctx_ref)
            return carry

        lax.fori_loop(0, half // HD // 2, step, 0)
        for i, out in enumerate(outs):
            out[...] = ctx_ref[place_ref[ATTEND + i]]


def line_of_four(place, queries, keys, values, gate, up, down, cot_rows):
    rows, width = queries.shape
    half = width // 2
    block = sds((3 * rows, half))
    first, second = call(
        halves_kernel,
        (block, block),
        (place, queries, keys, values),
        [SMEM, VMEM, VMEM, VMEM],
        moved=12 * rows * width,
    )
    gate_end = send(gate, OUTWARD)
    up_end = send(up, OUTWARD)
    down_end = send(down, OUTWARD, gate_end)
    gate_mid = send(gate, MIDDLE)
    gate_far = send(gate_mid, OUTWARD)
    near = send(first, INWARD, gate_mid, gate_end)
    mid = send(second, MIDDLE, gate_mid, gate_end)
    far = send(second, [(0, 2), (3, 1)], gate_mid, gate_end)
    piece = sds((rows, half))
    pieces = call(
        middle_kernel,
        (piece,) * 4,
        (place, first, near, mid, far),
        [SMEM] + [HBM] * 4,
        [
            pltpu.VMEM((4, 3 * rows, half), BF),
            pltpu.VMEM((4, rows, half), BF),
            pltpu.SemaphoreType.DMA((4,)),
        ],
        flops=64 * rows * rows * half,
        moved=32 * rows * half,
        after=(gate_end, up_end, gate_far, cot_rows),
    )
    up_mid = send(up, MIDDLE, near, mid, far)
    gate_inner = send(gate, INWARD, near, far, gate_end, up_end)
    up_inner = send(up, INWARD, near, far, gate_end, up_end)
    down_inner = send(down, INWARD, gate_inner)
    own, near, mid, far = lax.optimization_barrier((*pieces, gate_inner, down_end))[:4]
    mid = send(mid, MIDDLE)
    far = send(far, [(2, 0), (1, 3)])
    up_far = send(up_mid, OUTWARD, pieces[0])
    near = send(near, OUTWARD, up_far, far)
    gate_mid_near = send(gate_inner, MIDDLE, pieces[0])
    up_mid_near = send(up_inner, MIDDLE, pieces[0])
    down_mid = send(down, MIDDLE, gate_mid_near)
    down_mid_near = send(down_inner, MIDDLE, up_mid_near)
    gate_far_near = send(gate_mid_near, OUTWARD)
    up_far_near = send(up_mid_near, OUTWARD, gate_far_near)
    down_far = send(down_mid, OUTWARD, gate_far_near)
    norm_after = (gate_mid_near,)
    up_after = (down_mid_near,)
    gate_in = [
        [gate],
        [gate_inner, gate_end],
        [gate_mid, gate_far],
        [gate_mid_near, gate_far_near],
    ]
    up_in = [[up], [up_inner, up_end], [up_mid, up_far], [up_mid_near, up_far_near]]
    down_in = [
        [down],
        [down_inner, down_end],
        [down_mid, down_far],
        [down_mid_near],
    ]
    return (own, near, mid, far), gate_in, up_in, down_in, norm_after, up_after


def join_middle(place_ref, pieces, ctx_ref):
    own, near, mid, far = pieces
    half = own.shape[1]
    for plane, (lower, upper) in enumerate(((near, far), (own, mid), (mid, own), (far, near))):

        @pl.when(place_ref[PLANE] == plane)
        def _(lower=lower, upper=upper):
            ctx_ref[:, :half] = lower[...]
            ctx_ref[:, half:] = upper[...]


def join_groups(place_ref, pieces, ctx_ref):
    (ctx,) = pieces
    groups, _, part = ctx.shape
    for g in range(groups):
        ctx_ref[:, g * part : (g + 1) * part] = ctx[g]


def slot_rows(ids_t, owners, cap):
    tokens = ids_t.shape[1]
    experts = lax.broadcasted_iota(jnp.int32, (owners, tokens), 0)
    first = (experts == ids_t[0:1]).astype(F32)
    second = (experts == ids_t[1:2]).astype(F32)
    src = lax.broadcasted_iota(jnp.int32, (tokens, tokens), 0)
    dst = lax.broadcasted_iota(jnp.int32, (tokens, tokens), 1)
    earlier = (src < dst).astype(F32).astype(BF)
    count = mm((first + second).astype(BF), earlier, NN)
    slot0 = jnp.sum(first * count, axis=0, keepdims=True).astype(jnp.int32)
    slot1 = jnp.sum(second * count, axis=0, keepdims=True).astype(jnp.int32)
    return ids_t[0:1] * cap + slot0, ids_t[1:2] * cap + slot1


def slot_cols(ids, owners, cap):
    tokens = ids.shape[0]
    experts = lax.broadcasted_iota(jnp.int32, (tokens, owners), 1)
    first = (experts == ids[:, 0:1]).astype(F32)
    second = (experts == ids[:, 1:2]).astype(F32)
    dst = lax.broadcasted_iota(jnp.int32, (tokens, tokens), 0)
    src = lax.broadcasted_iota(jnp.int32, (tokens, tokens), 1)
    earlier = (src < dst).astype(F32).astype(BF)
    count = mm(earlier, (first + second).astype(BF), NN)
    slot0 = jnp.sum(first * count, axis=1, keepdims=True).astype(jnp.int32)
    slot1 = jnp.sum(second * count, axis=1, keepdims=True).astype(jnp.int32)
    return ids[:, 0:1] * cap + slot0, ids[:, 1:2] * cap + slot1


def one_hot(hit):
    return jnp.where(hit, 1.0, 0.0).astype(BF)


def send_cot_kernel(owners, cap, ids_ref, w_ref, cot_ref, o_ref):
    tokens = cot_ref.shape[0]
    at0, at1 = slot_rows(ids_ref[...], owners, cap)
    rows = lax.broadcasted_iota(jnp.int32, (owners * cap, tokens), 0)
    cot = cot_ref[...].astype(F32)
    o_ref[...] = (
        mm(one_hot(rows == at0), (w_ref[:, 0:1] * cot).astype(BF), NN)
        + mm(one_hot(rows == at1), (w_ref[:, 1:2] * cot).astype(BF), NN)
    ).astype(BF)


def norm_kernel(owners, cap, join, place_ref, ids_ref, resid_ref, gain_ref, *refs):
    *pieces, stream_ref, o_ref, ctx_ref = refs
    tokens, width = resid_ref.shape
    join(place_ref, pieces, ctx_ref)
    stream = (resid_ref[...].astype(F32) + ctx_ref[...].astype(F32)).astype(BF)
    stream_ref[...] = stream
    stream = stream.astype(F32)
    square = jnp.sum(stream * stream, axis=-1, keepdims=True)
    inv_rms = lax.rsqrt(square / width + 1e-05)
    at0, at1 = slot_rows(ids_ref[...], owners, cap)
    rows = lax.broadcasted_iota(jnp.int32, (owners * cap, tokens), 0)
    pick = one_hot((rows == at0) | (rows == at1))
    normed = ((stream_ref[...].astype(F32) * inv_rms) * gain_ref[...]).astype(BF)
    o_ref[...] = mm(pick, normed, NN).astype(BF)


def fetch(inner, choices, dst, sem):
    if len(choices) == 1:
        pltpu.make_async_copy(choices[0], dst, sem).start()
        return

    @pl.when(inner == 1)
    def _():
        pltpu.make_async_copy(choices[0], dst, sem).start()

    @pl.when(inner == 0)
    def _():
        pltpu.make_async_copy(choices[1], dst, sem).start()


def arrived(choices, dst, sem):
    pltpu.make_async_copy(choices[0], dst, sem).wait()


def regroup(refs, shape):
    refs = list(refs)
    return [[refs.pop(0) for _ in range(size)] for size in shape], refs


def cols_of(place_ref, slot, part):
    return pl.ds(pl.multiple_of(place_ref[COLS + slot] * part, part), part)


def gate_kernel(shape, place_ref, x_ref, *refs):
    slots = len(shape)
    gate_in, refs = regroup(refs, shape)
    o_ref, gate_w, sems = refs
    inner = place_ref[INNER]
    for j in range(slots):
        fetch(inner, gate_in[j], gate_w.at[j], sems.at[j])
    o_ref[...] = by_slots(place_ref, x_ref, gate_in, gate_w, sems)


def by_slots(place_ref, x_ref, weight_in, weight, sems):
    slots, _, part = weight.shape
    total = None
    for j in range(slots):
        rows = x_ref[:, cols_of(place_ref, j, part)]
        arrived(weight_in[j], weight.at[j], sems.at[j])
        term = mm(rows, weight[j], NT)
        total = term if total is None else total + term
    return total


def up_kernel(shape, place_ref, x_ref, gate_ref, *refs):
    slots = len(shape)
    up_in, refs = regroup(refs, shape)
    hidden_ref, to_gate_ref, to_up_ref, up_w, sems = refs
    inner = place_ref[INNER]
    for j in range(slots):
        fetch(inner, up_in[j], up_w.at[j], sems.at[j])
    gate = gate_ref[...]
    sigma = 1.0 / (1.0 + jnp.exp(-gate))
    silu = gate * sigma
    to_up_ref[...] = silu
    to_gate_ref[...] = sigma * (1.0 + gate * (1.0 - sigma))
    up = by_slots(place_ref, x_ref, up_in, up_w, sems)
    hidden_ref[...] = (to_up_ref[...] * up).astype(BF)
    to_gate_ref[...] = up * to_gate_ref[...]


def down_kernel(shape, place_ref, hidden_ref, cot_ref, *refs):
    slots = len(shape)
    down_in, refs = regroup(refs, shape)
    out_ref, d_hidden_ref, down_w, sems = refs
    part = down_w.shape[2]
    inner = place_ref[INNER]
    for j in range(slots):
        fetch(inner, down_in[j], down_w.at[j], sems.at[j])
    total = None
    for j in range(slots):
        rows = cot_ref[:, cols_of(place_ref, j, part)]
        arrived(down_in[j], down_w.at[j], sems.at[j])
        term = mm(rows, down_w[j], NT)
        total = term if total is None else total + term
        out_ref[:, j * part : (j + 1) * part] = mm(hidden_ref[...], down_w[j], NN).astype(BF)
    d_hidden_ref[...] = total


def grad_kernel(
    shape, late, place_ref, hidden_in, cot_in, d_hidden_in, to_gate_in, to_up_in, *refs
):
    slots = len(shape)
    down_in, refs = regroup(refs, shape[slots - late :])
    gate_in, refs = regroup(refs, shape)
    up_in, refs = regroup(refs, shape)
    o_ref, down_w, gate_w, up_w, sems = refs[:5]
    hidden_ref, cot_ref, d_hidden_ref, to_gate_ref, to_up_ref = refs[5:]
    part = down_w.shape[2]
    inner = place_ref[INNER]
    pairs = [
        (cot_in.at[:, cols_of(place_ref, slots - late + j, part)], cot_ref.at[j])
        for j in range(late)
    ]
    pairs += [
        (d_hidden_in, d_hidden_ref),
        (to_gate_in, to_gate_ref),
        (to_up_in, to_up_ref),
        (hidden_in, hidden_ref),
    ]
    for j in range(late):
        fetch(inner, down_in[j], down_w.at[j], sems.at[2, j])
    copies = [
        pltpu.make_async_copy(src, dst, sems.at[3 + i, 0]) for i, (src, dst) in enumerate(pairs)
    ]
    for copy in copies:
        copy.start()
    for j in range(slots):
        fetch(inner, gate_in[j], gate_w.at[j], sems.at[0, j])
        fetch(inner, up_in[j], up_w.at[j], sems.at[1, j])
    for j in range(late):
        arrived(down_in[j], down_w.at[j], sems.at[2, j])
    for copy in copies:
        copy.wait()
    d_hidden = d_hidden_ref[...]
    for j in range(late):
        d_hidden = d_hidden + mm(cot_ref[j], down_w[j], NT)
    d_gate = (d_hidden * to_gate_ref[...]).astype(BF)
    d_up = (d_hidden * to_up_ref[...]).astype(BF)
    for j in range(late):
        o_ref[:, (slots + j) * part : (slots + j + 1) * part] = mm(
            hidden_ref[...], down_w[j], NN
        ).astype(BF)
    for j in range(slots):
        arrived(gate_in[j], gate_w.at[j], sems.at[0, j])
        arrived(up_in[j], up_w.at[j], sems.at[1, j])
        o_ref[:, j * part : (j + 1) * part] = (
            mm(d_gate, gate_w[j], NN) + mm(d_up, up_w[j], NN)
        ).astype(BF)


def final_kernel(
    owners,
    cap,
    slots,
    place_ref,
    ids_ref,
    w_ref,
    gain_ref,
    stream_ref,
    cot_ref,
    first_ref,
    last_ref,
    output_ref,
    grad_ref,
    d_normed_ref,
):
    tokens, width = stream_ref.shape
    part = width // slots
    early = slots // 2
    at0, at1 = slot_cols(ids_ref[...], owners, cap)
    rows = lax.broadcasted_iota(jnp.int32, (tokens, owners * cap), 1)
    pick0, pick1 = one_hot(rows == at0), one_hot(rows == at1)
    both = pick0 + pick1
    w0, w1 = w_ref[:, 0:1], w_ref[:, 1:2]
    square = jnp.zeros((tokens, 1), F32)
    dot = jnp.zeros((tokens, 1), F32)
    for j in range(slots):
        cols = cols_of(place_ref, j, part)
        if j < early:
            pairs = first_ref[:, j * part : (j + 1) * part]
        else:
            at = width + (j - early) * part
            pairs = last_ref[:, at : at + part]
        stream = stream_ref[:, cols].astype(F32)
        mixed = w0 * mm(pick0, pairs, NN) + w1 * mm(pick1, pairs, NN)
        output_ref[:, cols] = (stream + mixed).astype(BF)
        grads = last_ref[:, j * part : (j + 1) * part]
        gained = mm(both, grads, NN) * gain_ref[:, cols]
        d_normed_ref[:, cols] = gained
        square = square + jnp.sum(stream * stream, axis=-1, keepdims=True)
        dot = dot + jnp.sum(gained * stream, axis=-1, keepdims=True)
    inv_rms = lax.rsqrt(square / width + 1e-05)
    mean = dot * inv_rms / width
    unit_rows = stream_ref[...].astype(F32) * inv_rms
    d_stream = inv_rms * (d_normed_ref[...] - unit_rows * mean)
    grad_ref[...] = (cot_ref[...].astype(F32) + d_stream).astype(BF)


MIDDLE = [(1, 2), (2, 1)]
OUTWARD = [(1, 0), (2, 3)]
INWARD = [(0, 1), (3, 2)]


def gather_all(shard, groups):
    whole_weight = lax.all_gather(shard, "seq", axis=0)
    return [[whole_weight[j]] for j in range(groups)]


def send(array, pairs, *first):
    return lax.ppermute(gated(array, *first), "seq", pairs)


def places(groups):
    if groups == 4:
        own = lax.axis_index("seq")
        table = jnp.array(
            [
                [0, 0, 1, 2, 3, 0, 0, 0, 0, 0],
                [1, 1, 0, 2, 3, 1, 1, 0, 2, 3],
                [1, 2, 3, 1, 0, 2, 2, 3, 1, 0],
                [0, 3, 2, 1, 0, 3, 0, 0, 0, 0],
            ],
            jnp.int32,
        )
        return table[own]
    return jnp.arange(-1, groups, dtype=jnp.int32)


def exchange(rows, owners, axis):
    total, width = rows.shape
    rows = rows.reshape(owners, total // owners, width)
    rows = lax.all_to_all(rows, axis, split_axis=0, concat_axis=0, tiled=True)
    return rows.reshape(total, width)


def flat(slots):
    return [ref for choices in slots for ref in choices]


def per_device(
    queries,
    keys,
    values,
    resid,
    norm_gain,
    w_gate,
    w_up,
    w_down,
    expert_ids,
    route_weights,
    cotangent,
):
    groups = lax.axis_size("seq")
    owners = lax.axis_size("exp")
    tokens, width = queries.shape[1:]
    ffw = w_gate.shape[2]
    part = width // groups
    cap = max(2, tokens * 10 // (4 * owners))
    total = owners * cap
    ids = expert_ids[0]
    ids_t = ids.T
    weights = route_weights[0]
    gain = norm_gain[None]
    cot = cotangent[0]
    place = places(groups)

    one = 2 * total * width * ffw
    send_cot = call(
        functools.partial(send_cot_kernel, owners, cap),
        sds((total, width)),
        (ids_t, weights, cot),
        [VMEM] * 3,
        flops=4 * total * tokens * width,
        moved=2 * (total + tokens) * width,
    )
    cot_rows = exchange(send_cot, owners, "exp")
    shards = (w_gate[0].T, w_up[0].T, w_down[0])
    if groups == 4:
        join = join_middle
        pieces, gate_in, up_in, down_in, norm_after, up_after = line_of_four(
            place, queries[0], keys[0], values[0], *shards, cot_rows
        )
    else:
        join = join_groups
        gate_in, up_in, down_in = [gather_all(shard, groups) for shard in shards]
        packed = pack(queries[0], keys[0], values[0], groups)
        heads = lax.all_to_all(packed, "seq", split_axis=0, concat_axis=0, tiled=True)
        ctx = attend(heads)
        pieces = (lax.all_to_all(ctx, "seq", split_axis=0, concat_axis=0, tiled=True),)
        norm_after = up_after = ()
    shape = [len(choices) for choices in gate_in]

    stream, send_rows = call(
        functools.partial(norm_kernel, owners, cap, join),
        (sds((tokens, width)), sds((total, width))),
        (place, ids_t, resid[0], gain, *pieces),
        [SMEM] + [VMEM] * (3 + len(pieces)),
        [pltpu.VMEM((tokens, width), BF)],
        flops=2 * total * tokens * width,
        moved=2 * (total + 3 * tokens) * width,
        after=norm_after,
    )
    rows = exchange(send_rows, owners, "exp")

    full_w = pltpu.VMEM((groups, ffw, part), BF)
    gate_pre = call(
        functools.partial(gate_kernel, shape),
        sds((total, ffw), F32),
        (place, rows, *flat(gate_in)),
        [SMEM, VMEM] + [HBM] * sum(shape),
        [full_w, pltpu.SemaphoreType.DMA((groups,))],
        flops=one,
        moved=2 * width * ffw + 2 * total * width + 4 * total * ffw,
    )
    if groups == 4:
        down_in[3].append(send(down_in[3][0], OUTWARD, up_in[3][1], gate_pre))
    hidden, to_gate, to_up = call(
        functools.partial(up_kernel, shape),
        (sds((total, ffw)), sds((total, ffw), F32), sds((total, ffw), F32)),
        (place, rows, gate_pre, *flat(up_in)),
        [SMEM, VMEM, VMEM] + [HBM] * sum(shape),
        [full_w, pltpu.SemaphoreType.DMA((groups,))],
        flops=one,
        moved=2 * width * ffw + 2 * total * width + 14 * total * ffw,
        after=up_after,
    )
    early = groups // 2
    late = groups - early
    out_first, d_hidden = call(
        functools.partial(down_kernel, shape[:early]),
        (sds((total, early * part)), sds((total, ffw), F32)),
        (place, hidden, cot_rows, *flat(down_in[:early])),
        [SMEM, VMEM, VMEM] + [HBM] * sum(shape[:early]),
        [pltpu.VMEM((early, ffw, part), BF), pltpu.SemaphoreType.DMA((early,))],
        flops=2 * one * early // groups,
        moved=width * ffw + 3 * total * width + 6 * total * ffw,
    )
    back_first = exchange(out_first, owners, "exp")
    back = call(
        functools.partial(grad_kernel, shape, late),
        sds((total, width + late * part)),
        (
            place,
            hidden,
            cot_rows,
            d_hidden,
            to_gate,
            to_up,
            *flat(down_in[early:]),
            *flat(gate_in),
            *flat(up_in),
        ),
        [SMEM] + [HBM] * (5 + sum(shape[early:]) + 2 * sum(shape)),
        [
            pltpu.VMEM((late, ffw, part), BF),
            full_w,
            full_w,
            pltpu.SemaphoreType.DMA((7 + late, groups)),
            pltpu.VMEM((total, ffw), BF),
            pltpu.VMEM((late, total, part), BF),
            pltpu.VMEM((total, ffw), F32),
            pltpu.VMEM((total, ffw), F32),
            pltpu.VMEM((total, ffw), F32),
        ],
        flops=2 * one + 2 * one * late // groups,
        moved=5 * width * ffw + 4 * total * width + 14 * total * ffw,
    )
    back_last = exchange(back, owners, "exp")
    output, stream_grad = call(
        functools.partial(final_kernel, owners, cap, groups),
        (sds((tokens, width)), sds((tokens, width))),
        (place, ids, weights, gain, stream, cot, back_first, back_last),
        [SMEM] + [VMEM] * 7,
        [pltpu.VMEM((tokens, width), F32)],
        flops=6 * total * tokens * width,
        moved=4 * total * width + 8 * tokens * width,
        vmem=16,
        held=True,
    )
    return (output[None], stream_grad[None])


def solution(mesh):
    placed = (
        P("exp", "seq", None),
        P("exp", "seq", None),
        P("exp", "seq", None),
        P("exp", "seq", None),
        P(),
        P("exp", "seq", None),
        P("exp", "seq", None),
        P("exp", None, "seq"),
        P("exp", "seq", None),
        P("exp", "seq", None),
        P("exp", "seq", None),
    )
    return jax.shard_map(
        per_device,
        mesh=mesh,
        in_specs=placed,
        out_specs=(P("exp", "seq", None), P("exp", "seq", None)),
        check_vma=False,
    )
```

```python
import functools

import jax
import jax.numpy as jnp
from jax import lax
from jax.experimental import pallas as pl
from jax.experimental.pallas import tpu as pltpu
from jax.sharding import PartitionSpec as P

HD = 128
BF = jnp.bfloat16
F32 = jnp.float32
MIB = 1 << 20
HBM = pl.BlockSpec(memory_space=pltpu.HBM)
VMEM = pl.BlockSpec(memory_space=pltpu.VMEM)
SMEM = pl.BlockSpec(memory_space=pltpu.SMEM)
NT = (((1,), (1,)), ((), ()))
NN = (((1,), (0,)), ((), ()))


def mm(a, b, dims):
    return lax.dot_general(a, b, dims, preferred_element_type=F32)


def whole(array):
    return pl.BlockSpec(array.shape, lambda i: (0,) * len(array.shape))


def call(kernel, outs, args, in_specs, scratch=(), flops=0, moved=0, vmem=56, after=(), held=False):
    count, extra = len(args), len(after)

    def body(*refs):
        kernel(*refs[:count], *refs[count + extra :])

    return pl.pallas_call(
        body,
        grid=() if held else (1,),
        out_shape=outs,
        in_specs=[
            *[
                whole(arg) if spec is VMEM and not held else spec
                for arg, spec in zip(args, in_specs)
            ],
            *[HBM] * extra,
        ],
        out_specs=jax.tree.map(lambda out: VMEM if held else whole(out), outs),
        scratch_shapes=list(scratch),
        compiler_params=pltpu.CompilerParams(vmem_limit_bytes=vmem * MIB),
        cost_estimate=pl.CostEstimate(flops=flops, bytes_accessed=moved, transcendentals=0),
    )(*args, *after)


def gated(array, *first):
    return lax.optimization_barrier((array, *first))[0] if first else array


def sds(shape, dtype=BF):
    return jax.ShapeDtypeStruct(shape, dtype)


def pack_kernel(q_ref, k_ref, v_ref, o_ref):
    rows = q_ref.shape[0]
    o_ref[0, 0:rows] = q_ref[...]
    o_ref[0, rows : 2 * rows] = k_ref[...]
    o_ref[0, 2 * rows : 3 * rows] = v_ref[...]


def pack(q, k, v, groups):
    rows, width = q.shape
    part = width // groups
    spec = pl.BlockSpec((rows, part), lambda g: (0, g))
    return pl.pallas_call(
        pack_kernel,
        grid=(groups,),
        out_shape=sds((groups, 3 * rows, part)),
        in_specs=[spec] * 3,
        out_specs=pl.BlockSpec((1, 3 * rows, part), lambda g: (g, 0, 0)),
        cost_estimate=pl.CostEstimate(
            flops=0, bytes_accessed=12 * rows * width, transcendentals=0
        ),
    )(q, k, v)


def attend_head(query, keys, vals, store):
    length = keys.shape[0]
    block = min(512, length)
    scale = HD ** (-0.5)
    row_ids = lax.broadcasted_iota(jnp.int32, (block, block), 0)
    col_ids = lax.broadcasted_iota(jnp.int32, (block, block), 1)
    keep = col_ids <= row_ids
    for start in range(0, length, block):
        end = start + block
        scores = mm(query[start:end], keys[:end], NT) * scale
        diag = jnp.where(keep, scores[:, start:], -jnp.inf)
        scores = jnp.concatenate([scores[:, :start], diag], axis=1) if start else diag
        exps = jnp.exp(scores - jnp.max(scores, axis=-1, keepdims=True))
        inverse = 1.0 / jnp.sum(exps, axis=-1, keepdims=True)
        store(start, end, mm((exps * inverse).astype(BF), vals[:end], NN).astype(BF))


def attend_columns(x_ref, cols, o_ref):
    blocks, three, _ = x_ref.shape
    rows = three // 3
    query, keys, vals = [
        x_ref[:, i * rows : (i + 1) * rows, cols].reshape(blocks * rows, HD) for i in range(3)
    ]

    def store(start, end, ctx):
        first, last = start // rows, end // rows
        o_ref[first:last, :, cols] = ctx.reshape(last - first, rows, HD)

    attend_head(query, keys, vals, store)


def attend_kernel(x_ref, o_ref):
    attend_columns(x_ref, slice(0, HD), o_ref)


def attend(x):
    blocks, three, part = x.shape
    rows = three // 3
    length = blocks * rows
    return pl.pallas_call(
        attend_kernel,
        grid=(part // HD,),
        out_shape=sds((blocks, rows, part)),
        in_specs=[pl.BlockSpec((blocks, three, HD), lambda h: (0, 0, h))],
        out_specs=pl.BlockSpec((blocks, rows, HD), lambda h: (0, 0, h)),
        compiler_params=pltpu.CompilerParams(vmem_limit_bytes=40 * MIB),
        cost_estimate=pl.CostEstimate(
            flops=4 * length * length * part,
            bytes_accessed=8 * length * part,
            transcendentals=length * length * part // HD,
        ),
    )(x)


INNER, COLS, PLANE, ATTEND = 0, 1, 5, 6


def halves_kernel(place_ref, q_ref, k_ref, v_ref, first_ref, second_ref):
    rows, width = q_ref.shape
    half = width // 2

    def copy(lower, upper):
        for i, ref in enumerate((q_ref, k_ref, v_ref)):
            lower[i * rows : (i + 1) * rows] = ref[:, :half]
            upper[i * rows : (i + 1) * rows] = ref[:, half:]

    @pl.when(place_ref[PLANE] < 2)
    def _():
        copy(first_ref, second_ref)

    @pl.when(place_ref[PLANE] >= 2)
    def _():
        copy(second_ref, first_ref)


def middle_kernel(place_ref, own_in, near_in, mid_in, far_in, *refs):
    *outs, x_ref, ctx_ref, sems = refs
    blocks, three, half = x_ref.shape
    rows = three // 3

    @pl.when(place_ref[INNER] == 1)
    def _():
        copies = [
            pltpu.make_async_copy(ref, x_ref.at[place_ref[ATTEND + i]], sems.at[i])
            for i, ref in enumerate((own_in, near_in, mid_in, far_in))
        ]
        for copy in copies:
            copy.start()
        for copy in copies:
            copy.wait()

        def step(i, carry):
            for j in range(2):
                cols = pl.ds(pl.multiple_of((2 * i + j) * HD, HD), HD)
                attend_columns(x_ref, cols, ctx_ref)
            return carry

        lax.fori_loop(0, half // HD // 2, step, 0)
        for i, out in enumerate(outs):
            out[...] = ctx_ref[place_ref[ATTEND + i]]


def line_of_four(place, queries, keys, values, gate, up, down, cot_rows):
    rows, width = queries.shape
    half = width // 2
    block = sds((3 * rows, half))
    first, second = call(
        halves_kernel,
        (block, block),
        (place, queries, keys, values),
        [SMEM, VMEM, VMEM, VMEM],
        moved=12 * rows * width,
    )
    gate_end = send(gate, OUTWARD)
    up_end = send(up, OUTWARD)
    down_end = send(down, OUTWARD, gate_end)
    gate_mid = send(gate, MIDDLE)
    gate_far = send(gate_mid, OUTWARD)
    near = send(first, INWARD, gate_mid, gate_end)
    mid = send(second, MIDDLE, gate_mid, gate_end)
    far = send(second, [(0, 2), (3, 1)], gate_mid, gate_end)
    piece = sds((rows, half))
    pieces = call(
        middle_kernel,
        (piece,) * 4,
        (place, first, near, mid, far),
        [SMEM] + [HBM] * 4,
        [
            pltpu.VMEM((4, 3 * rows, half), BF),
            pltpu.VMEM((4, rows, half), BF),
            pltpu.SemaphoreType.DMA((4,)),
        ],
        flops=64 * rows * rows * half,
        moved=32 * rows * half,
        after=(gate_end, up_end, gate_far, cot_rows),
    )
    up_mid = send(up, MIDDLE, near, mid, far)
    gate_inner = send(gate, INWARD, near, far, gate_end, up_end)
    up_inner = send(up, INWARD, near, far, gate_end, up_end)
    down_inner = send(down, INWARD, gate_inner)
    own, near, mid, far = lax.optimization_barrier((*pieces, gate_inner, down_end))[:4]
    mid = send(mid, MIDDLE)
    far = send(far, [(2, 0), (1, 3)])
    up_far = send(up_mid, OUTWARD, pieces[0])
    near = send(near, OUTWARD, up_far)
    gate_mid_near = send(gate_inner, MIDDLE, pieces[0])
    up_mid_near = send(up_inner, MIDDLE, pieces[0])
    down_mid = send(down, MIDDLE, gate_mid_near)
    down_mid_near = send(down_inner, MIDDLE, up_mid_near)
    gate_far_near = send(gate_mid_near, OUTWARD)
    up_far_near = send(up_mid_near, OUTWARD, gate_far_near)
    down_far = send(down_mid, OUTWARD, gate_far_near)
    norm_after = (gate_mid_near,)
    up_after = (down_mid_near,)
    gate_in = [
        [gate],
        [gate_inner, gate_end],
        [gate_mid, gate_far],
        [gate_mid_near, gate_far_near],
    ]
    up_in = [[up], [up_inner, up_end], [up_mid, up_far], [up_mid_near, up_far_near]]
    down_in = [
        [down],
        [down_inner, down_end],
        [down_mid, down_far],
        [down_mid_near],
    ]
    return (own, near, mid, far), gate_in, up_in, down_in, norm_after, up_after


def join_middle(place_ref, pieces, ctx_ref):
    own, near, mid, far = pieces
    half = own.shape[1]
    for plane, (lower, upper) in enumerate(((near, far), (own, mid), (mid, own), (far, near))):

        @pl.when(place_ref[PLANE] == plane)
        def _(lower=lower, upper=upper):
            ctx_ref[:, :half] = lower[...]
            ctx_ref[:, half:] = upper[...]


def join_groups(place_ref, pieces, ctx_ref):
    (ctx,) = pieces
    groups, _, part = ctx.shape
    for g in range(groups):
        ctx_ref[:, g * part : (g + 1) * part] = ctx[g]


def slot_rows(ids_t, owners, cap):
    tokens = ids_t.shape[1]
    experts = lax.broadcasted_iota(jnp.int32, (owners, tokens), 0)
    first = (experts == ids_t[0:1]).astype(F32)
    second = (experts == ids_t[1:2]).astype(F32)
    src = lax.broadcasted_iota(jnp.int32, (tokens, tokens), 0)
    dst = lax.broadcasted_iota(jnp.int32, (tokens, tokens), 1)
    earlier = (src < dst).astype(F32).astype(BF)
    count = mm((first + second).astype(BF), earlier, NN)
    slot0 = jnp.sum(first * count, axis=0, keepdims=True).astype(jnp.int32)
    slot1 = jnp.sum(second * count, axis=0, keepdims=True).astype(jnp.int32)
    return ids_t[0:1] * cap + slot0, ids_t[1:2] * cap + slot1


def slot_cols(ids, owners, cap):
    tokens = ids.shape[0]
    experts = lax.broadcasted_iota(jnp.int32, (tokens, owners), 1)
    first = (experts == ids[:, 0:1]).astype(F32)
    second = (experts == ids[:, 1:2]).astype(F32)
    dst = lax.broadcasted_iota(jnp.int32, (tokens, tokens), 0)
    src = lax.broadcasted_iota(jnp.int32, (tokens, tokens), 1)
    earlier = (src < dst).astype(F32).astype(BF)
    count = mm(earlier, (first + second).astype(BF), NN)
    slot0 = jnp.sum(first * count, axis=1, keepdims=True).astype(jnp.int32)
    slot1 = jnp.sum(second * count, axis=1, keepdims=True).astype(jnp.int32)
    return ids[:, 0:1] * cap + slot0, ids[:, 1:2] * cap + slot1


def one_hot(hit):
    return jnp.where(hit, 1.0, 0.0).astype(BF)


def send_cot_kernel(owners, cap, ids_ref, w_ref, cot_ref, o_ref):
    tokens = cot_ref.shape[0]
    at0, at1 = slot_rows(ids_ref[...], owners, cap)
    rows = lax.broadcasted_iota(jnp.int32, (owners * cap, tokens), 0)
    cot = cot_ref[...].astype(F32)
    o_ref[...] = (
        mm(one_hot(rows == at0), (w_ref[:, 0:1] * cot).astype(BF), NN)
        + mm(one_hot(rows == at1), (w_ref[:, 1:2] * cot).astype(BF), NN)
    ).astype(BF)


def norm_kernel(owners, cap, join, place_ref, ids_ref, resid_ref, gain_ref, *refs):
    *pieces, stream_ref, o_ref, ctx_ref = refs
    tokens, width = resid_ref.shape
    join(place_ref, pieces, ctx_ref)
    stream = (resid_ref[...].astype(F32) + ctx_ref[...].astype(F32)).astype(BF)
    stream_ref[...] = stream
    stream = stream.astype(F32)
    square = jnp.sum(stream * stream, axis=-1, keepdims=True)
    inv_rms = lax.rsqrt(square / width + 1e-05)
    at0, at1 = slot_rows(ids_ref[...], owners, cap)
    rows = lax.broadcasted_iota(jnp.int32, (owners * cap, tokens), 0)
    pick = one_hot((rows == at0) | (rows == at1))
    normed = ((stream_ref[...].astype(F32) * inv_rms) * gain_ref[...]).astype(BF)
    o_ref[...] = mm(pick, normed, NN).astype(BF)


def fetch(inner, choices, dst, sem):
    if len(choices) == 1:
        pltpu.make_async_copy(choices[0], dst, sem).start()
        return

    @pl.when(inner == 1)
    def _():
        pltpu.make_async_copy(choices[0], dst, sem).start()

    @pl.when(inner == 0)
    def _():
        pltpu.make_async_copy(choices[1], dst, sem).start()


def arrived(choices, dst, sem):
    pltpu.make_async_copy(choices[0], dst, sem).wait()


def regroup(refs, shape):
    refs = list(refs)
    return [[refs.pop(0) for _ in range(size)] for size in shape], refs


def cols_of(place_ref, slot, part):
    return pl.ds(pl.multiple_of(place_ref[COLS + slot] * part, part), part)


def gate_kernel(shape, place_ref, x_ref, *refs):
    slots = len(shape)
    gate_in, refs = regroup(refs, shape)
    o_ref, gate_w, sems = refs
    inner = place_ref[INNER]
    for j in range(slots):
        fetch(inner, gate_in[j], gate_w.at[j], sems.at[j])
    o_ref[...] = by_slots(place_ref, x_ref, gate_in, gate_w, sems)


def by_slots(place_ref, x_ref, weight_in, weight, sems):
    slots, _, part = weight.shape
    total = None
    for j in range(slots):
        rows = x_ref[:, cols_of(place_ref, j, part)]
        arrived(weight_in[j], weight.at[j], sems.at[j])
        term = mm(rows, weight[j], NT)
        total = term if total is None else total + term
    return total


def up_kernel(shape, place_ref, x_ref, gate_ref, *refs):
    slots = len(shape)
    up_in, refs = regroup(refs, shape)
    hidden_ref, to_gate_ref, to_up_ref, up_w, sems = refs
    inner = place_ref[INNER]
    for j in range(slots):
        fetch(inner, up_in[j], up_w.at[j], sems.at[j])
    gate = gate_ref[...]
    sigma = 1.0 / (1.0 + jnp.exp(-gate))
    silu = gate * sigma
    to_up_ref[...] = silu
    to_gate_ref[...] = sigma * (1.0 + gate * (1.0 - sigma))
    up = by_slots(place_ref, x_ref, up_in, up_w, sems)
    hidden_ref[...] = (to_up_ref[...] * up).astype(BF)
    to_gate_ref[...] = up * to_gate_ref[...]


def down_kernel(shape, place_ref, hidden_ref, cot_ref, *refs):
    slots = len(shape)
    down_in, refs = regroup(refs, shape)
    out_ref, d_hidden_ref, down_w, sems = refs
    part = down_w.shape[2]
    inner = place_ref[INNER]
    for j in range(slots):
        fetch(inner, down_in[j], down_w.at[j], sems.at[j])
    total = None
    for j in range(slots):
        rows = cot_ref[:, cols_of(place_ref, j, part)]
        arrived(down_in[j], down_w.at[j], sems.at[j])
        term = mm(rows, down_w[j], NT)
        total = term if total is None else total + term
        out_ref[:, j * part : (j + 1) * part] = mm(hidden_ref[...], down_w[j], NN).astype(BF)
    d_hidden_ref[...] = total


def grad_kernel(
    shape, late, place_ref, hidden_in, cot_in, d_hidden_in, to_gate_in, to_up_in, *refs
):
    slots = len(shape)
    down_in, refs = regroup(refs, shape[slots - late :])
    gate_in, refs = regroup(refs, shape)
    up_in, refs = regroup(refs, shape)
    o_ref, down_w, gate_w, up_w, sems = refs[:5]
    hidden_ref, cot_ref, d_hidden_ref, to_gate_ref, to_up_ref = refs[5:]
    part = down_w.shape[2]
    inner = place_ref[INNER]
    pairs = [
        (cot_in.at[:, cols_of(place_ref, slots - late + j, part)], cot_ref.at[j])
        for j in range(late)
    ]
    pairs += [
        (d_hidden_in, d_hidden_ref),
        (to_gate_in, to_gate_ref),
        (to_up_in, to_up_ref),
        (hidden_in, hidden_ref),
    ]
    for j in range(late):
        fetch(inner, down_in[j], down_w.at[j], sems.at[2, j])
    copies = [
        pltpu.make_async_copy(src, dst, sems.at[3 + i, 0]) for i, (src, dst) in enumerate(pairs)
    ]
    for copy in copies:
        copy.start()
    for j in range(slots):
        fetch(inner, gate_in[j], gate_w.at[j], sems.at[0, j])
        fetch(inner, up_in[j], up_w.at[j], sems.at[1, j])
    for j in range(late):
        arrived(down_in[j], down_w.at[j], sems.at[2, j])
    for copy in copies:
        copy.wait()
    d_hidden = d_hidden_ref[...]
    for j in range(late):
        d_hidden = d_hidden + mm(cot_ref[j], down_w[j], NT)
    d_gate = (d_hidden * to_gate_ref[...]).astype(BF)
    d_up = (d_hidden * to_up_ref[...]).astype(BF)
    for j in range(late):
        o_ref[:, (slots + j) * part : (slots + j + 1) * part] = mm(
            hidden_ref[...], down_w[j], NN
        ).astype(BF)
    for j in range(slots):
        arrived(gate_in[j], gate_w.at[j], sems.at[0, j])
        arrived(up_in[j], up_w.at[j], sems.at[1, j])
        o_ref[:, j * part : (j + 1) * part] = (
            mm(d_gate, gate_w[j], NN) + mm(d_up, up_w[j], NN)
        ).astype(BF)


def final_kernel(
    owners,
    cap,
    slots,
    place_ref,
    ids_ref,
    w_ref,
    gain_ref,
    stream_ref,
    cot_ref,
    first_ref,
    last_ref,
    output_ref,
    grad_ref,
    d_normed_ref,
):
    tokens, width = stream_ref.shape
    part = width // slots
    early = slots // 2
    at0, at1 = slot_cols(ids_ref[...], owners, cap)
    rows = lax.broadcasted_iota(jnp.int32, (tokens, owners * cap), 1)
    pick0, pick1 = one_hot(rows == at0), one_hot(rows == at1)
    both = pick0 + pick1
    w0, w1 = w_ref[:, 0:1], w_ref[:, 1:2]
    square = jnp.zeros((tokens, 1), F32)
    dot = jnp.zeros((tokens, 1), F32)
    for j in range(slots):
        cols = cols_of(place_ref, j, part)
        if j < early:
            pairs = first_ref[:, j * part : (j + 1) * part]
        else:
            at = width + (j - early) * part
            pairs = last_ref[:, at : at + part]
        stream = stream_ref[:, cols].astype(F32)
        mixed = w0 * mm(pick0, pairs, NN) + w1 * mm(pick1, pairs, NN)
        output_ref[:, cols] = (stream + mixed).astype(BF)
        grads = last_ref[:, j * part : (j + 1) * part]
        gained = mm(both, grads, NN) * gain_ref[:, cols]
        d_normed_ref[:, cols] = gained
        square = square + jnp.sum(stream * stream, axis=-1, keepdims=True)
        dot = dot + jnp.sum(gained * stream, axis=-1, keepdims=True)
    inv_rms = lax.rsqrt(square / width + 1e-05)
    mean = dot * inv_rms / width
    unit_rows = stream_ref[...].astype(F32) * inv_rms
    d_stream = inv_rms * (d_normed_ref[...] - unit_rows * mean)
    grad_ref[...] = (cot_ref[...].astype(F32) + d_stream).astype(BF)


MIDDLE = [(1, 2), (2, 1)]
OUTWARD = [(1, 0), (2, 3)]
INWARD = [(0, 1), (3, 2)]


def gather_all(shard, groups):
    whole_weight = lax.all_gather(shard, "seq", axis=0)
    return [[whole_weight[j]] for j in range(groups)]


def send(array, pairs, *first):
    return lax.ppermute(gated(array, *first), "seq", pairs)


def places(groups):
    if groups == 4:
        own = lax.axis_index("seq")
        table = jnp.array(
            [
                [0, 0, 1, 2, 3, 0, 0, 0, 0, 0],
                [1, 1, 0, 2, 3, 1, 1, 0, 2, 3],
                [1, 2, 3, 1, 0, 2, 2, 3, 1, 0],
                [0, 3, 2, 1, 0, 3, 0, 0, 0, 0],
            ],
            jnp.int32,
        )
        return table[own]
    return jnp.arange(-1, groups, dtype=jnp.int32)


def exchange(rows, owners, axis):
    total, width = rows.shape
    rows = rows.reshape(owners, total // owners, width)
    rows = lax.all_to_all(rows, axis, split_axis=0, concat_axis=0, tiled=True)
    return rows.reshape(total, width)


def flat(slots):
    return [ref for choices in slots for ref in choices]


def per_device(
    queries,
    keys,
    values,
    resid,
    norm_gain,
    w_gate,
    w_up,
    w_down,
    expert_ids,
    route_weights,
    cotangent,
):
    groups = lax.axis_size("seq")
    owners = lax.axis_size("exp")
    tokens, width = queries.shape[1:]
    ffw = w_gate.shape[2]
    part = width // groups
    cap = max(2, tokens * 10 // (4 * owners))
    total = owners * cap
    ids = expert_ids[0]
    ids_t = ids.T
    weights = route_weights[0]
    gain = norm_gain[None]
    cot = cotangent[0]
    place = places(groups)

    one = 2 * total * width * ffw
    send_cot = call(
        functools.partial(send_cot_kernel, owners, cap),
        sds((total, width)),
        (ids_t, weights, cot),
        [VMEM] * 3,
        flops=4 * total * tokens * width,
        moved=2 * (total + tokens) * width,
    )
    cot_rows = exchange(send_cot, owners, "exp")
    shards = (w_gate[0].T, w_up[0].T, w_down[0])
    if groups == 4:
        join = join_middle
        pieces, gate_in, up_in, down_in, norm_after, up_after = line_of_four(
            place, queries[0], keys[0], values[0], *shards, cot_rows
        )
    else:
        join = join_groups
        gate_in, up_in, down_in = [gather_all(shard, groups) for shard in shards]
        packed = pack(queries[0], keys[0], values[0], groups)
        heads = lax.all_to_all(packed, "seq", split_axis=0, concat_axis=0, tiled=True)
        ctx = attend(heads)
        pieces = (lax.all_to_all(ctx, "seq", split_axis=0, concat_axis=0, tiled=True),)
        norm_after = up_after = ()
    shape = [len(choices) for choices in gate_in]

    stream, send_rows = call(
        functools.partial(norm_kernel, owners, cap, join),
        (sds((tokens, width)), sds((total, width))),
        (place, ids_t, resid[0], gain, *pieces),
        [SMEM] + [VMEM] * (3 + len(pieces)),
        [pltpu.VMEM((tokens, width), BF)],
        flops=2 * total * tokens * width,
        moved=2 * (total + 3 * tokens) * width,
        after=norm_after,
    )
    rows = exchange(send_rows, owners, "exp")

    full_w = pltpu.VMEM((groups, ffw, part), BF)
    gate_pre = call(
        functools.partial(gate_kernel, shape),
        sds((total, ffw), F32),
        (place, rows, *flat(gate_in)),
        [SMEM, VMEM] + [HBM] * sum(shape),
        [full_w, pltpu.SemaphoreType.DMA((groups,))],
        flops=one,
        moved=2 * width * ffw + 2 * total * width + 4 * total * ffw,
    )
    if groups == 4:
        down_in[3].append(send(down_in[3][0], OUTWARD, up_in[3][1], gate_pre))
    hidden, to_gate, to_up = call(
        functools.partial(up_kernel, shape),
        (sds((total, ffw)), sds((total, ffw), F32), sds((total, ffw), F32)),
        (place, rows, gate_pre, *flat(up_in)),
        [SMEM, VMEM, VMEM] + [HBM] * sum(shape),
        [full_w, pltpu.SemaphoreType.DMA((groups,))],
        flops=one,
        moved=2 * width * ffw + 2 * total * width + 14 * total * ffw,
        after=up_after,
    )
    early = groups // 2
    late = groups - early
    out_first, d_hidden = call(
        functools.partial(down_kernel, shape[:early]),
        (sds((total, early * part)), sds((total, ffw), F32)),
        (place, hidden, cot_rows, *flat(down_in[:early])),
        [SMEM, VMEM, VMEM] + [HBM] * sum(shape[:early]),
        [pltpu.VMEM((early, ffw, part), BF), pltpu.SemaphoreType.DMA((early,))],
        flops=2 * one * early // groups,
        moved=width * ffw + 3 * total * width + 6 * total * ffw,
    )
    back_first = exchange(out_first, owners, "exp")
    back = call(
        functools.partial(grad_kernel, shape, late),
        sds((total, width + late * part)),
        (
            place,
            hidden,
            cot_rows,
            d_hidden,
            to_gate,
            to_up,
            *flat(down_in[early:]),
            *flat(gate_in),
            *flat(up_in),
        ),
        [SMEM] + [HBM] * (5 + sum(shape[early:]) + 2 * sum(shape)),
        [
            pltpu.VMEM((late, ffw, part), BF),
            full_w,
            full_w,
            pltpu.SemaphoreType.DMA((7 + late, groups)),
            pltpu.VMEM((total, ffw), BF),
            pltpu.VMEM((late, total, part), BF),
            pltpu.VMEM((total, ffw), F32),
            pltpu.VMEM((total, ffw), F32),
            pltpu.VMEM((total, ffw), F32),
        ],
        flops=2 * one + 2 * one * late // groups,
        moved=5 * width * ffw + 4 * total * width + 14 * total * ffw,
    )
    back_last = exchange(back, owners, "exp")
    output, stream_grad = call(
        functools.partial(final_kernel, owners, cap, groups),
        (sds((tokens, width)), sds((tokens, width))),
        (place, ids, weights, gain, stream, cot, back_first, back_last),
        [SMEM] + [VMEM] * 7,
        [pltpu.VMEM((tokens, width), F32)],
        flops=6 * total * tokens * width,
        moved=4 * total * width + 8 * tokens * width,
        vmem=16,
        held=True,
    )
    return (output[None], stream_grad[None])


def solution(mesh):
    placed = (
        P("exp", "seq", None),
        P("exp", "seq", None),
        P("exp", "seq", None),
        P("exp", "seq", None),
        P(),
        P("exp", "seq", None),
        P("exp", "seq", None),
        P("exp", None, "seq"),
        P("exp", "seq", None),
        P("exp", "seq", None),
        P("exp", "seq", None),
    )
    return jax.shard_map(
        per_device,
        mesh=mesh,
        in_specs=placed,
        out_specs=(P("exp", "seq", None), P("exp", "seq", None)),
        check_vma=False,
    )
```

```python
import functools

import jax
import jax.numpy as jnp
from jax import lax
from jax.experimental import pallas as pl
from jax.experimental.pallas import tpu as pltpu
from jax.sharding import PartitionSpec as P

HD = 128
BF = jnp.bfloat16
F32 = jnp.float32
MIB = 1 << 20
HBM = pl.BlockSpec(memory_space=pltpu.HBM)
VMEM = pl.BlockSpec(memory_space=pltpu.VMEM)
SMEM = pl.BlockSpec(memory_space=pltpu.SMEM)
NT = (((1,), (1,)), ((), ()))
NN = (((1,), (0,)), ((), ()))


def mm(a, b, dims):
    return lax.dot_general(a, b, dims, preferred_element_type=F32)


def whole(array):
    return pl.BlockSpec(array.shape, lambda i: (0,) * len(array.shape))


def call(kernel, outs, args, in_specs, scratch=(), flops=0, moved=0, vmem=56, after=(), held=False):
    count, extra = len(args), len(after)

    def body(*refs):
        kernel(*refs[:count], *refs[count + extra :])

    return pl.pallas_call(
        body,
        grid=() if held else (1,),
        out_shape=outs,
        in_specs=[
            *[
                whole(arg) if spec is VMEM and not held else spec
                for arg, spec in zip(args, in_specs)
            ],
            *[HBM] * extra,
        ],
        out_specs=jax.tree.map(lambda out: VMEM if held else whole(out), outs),
        scratch_shapes=list(scratch),
        compiler_params=pltpu.CompilerParams(vmem_limit_bytes=vmem * MIB),
        cost_estimate=pl.CostEstimate(flops=flops, bytes_accessed=moved, transcendentals=0),
    )(*args, *after)


def gated(array, *first):
    return lax.optimization_barrier((array, *first))[0] if first else array


def sds(shape, dtype=BF):
    return jax.ShapeDtypeStruct(shape, dtype)


def pack_kernel(q_ref, k_ref, v_ref, o_ref):
    rows = q_ref.shape[0]
    o_ref[0, 0:rows] = q_ref[...]
    o_ref[0, rows : 2 * rows] = k_ref[...]
    o_ref[0, 2 * rows : 3 * rows] = v_ref[...]


def pack(q, k, v, groups):
    rows, width = q.shape
    part = width // groups
    spec = pl.BlockSpec((rows, part), lambda g: (0, g))
    return pl.pallas_call(
        pack_kernel,
        grid=(groups,),
        out_shape=sds((groups, 3 * rows, part)),
        in_specs=[spec] * 3,
        out_specs=pl.BlockSpec((1, 3 * rows, part), lambda g: (g, 0, 0)),
        cost_estimate=pl.CostEstimate(
            flops=0, bytes_accessed=12 * rows * width, transcendentals=0
        ),
    )(q, k, v)


def attend_head(query, keys, vals, store):
    length = keys.shape[0]
    block = min(512, length)
    scale = HD ** (-0.5)
    row_ids = lax.broadcasted_iota(jnp.int32, (block, block), 0)
    col_ids = lax.broadcasted_iota(jnp.int32, (block, block), 1)
    keep = col_ids <= row_ids
    for start in range(0, length, block):
        end = start + block
        scores = mm(query[start:end], keys[:end], NT) * scale
        diag = jnp.where(keep, scores[:, start:], -jnp.inf)
        scores = jnp.concatenate([scores[:, :start], diag], axis=1) if start else diag
        exps = jnp.exp(scores - jnp.max(scores, axis=-1, keepdims=True))
        inverse = 1.0 / jnp.sum(exps, axis=-1, keepdims=True)
        store(start, end, mm((exps * inverse).astype(BF), vals[:end], NN).astype(BF))


def attend_columns(x_ref, cols, o_ref):
    blocks, three, _ = x_ref.shape
    rows = three // 3
    query, keys, vals = [
        x_ref[:, i * rows : (i + 1) * rows, cols].reshape(blocks * rows, HD) for i in range(3)
    ]

    def store(start, end, ctx):
        first, last = start // rows, end // rows
        o_ref[first:last, :, cols] = ctx.reshape(last - first, rows, HD)

    attend_head(query, keys, vals, store)


def attend_kernel(x_ref, o_ref):
    attend_columns(x_ref, slice(0, HD), o_ref)


def attend(x):
    blocks, three, part = x.shape
    rows = three // 3
    length = blocks * rows
    return pl.pallas_call(
        attend_kernel,
        grid=(part // HD,),
        out_shape=sds((blocks, rows, part)),
        in_specs=[pl.BlockSpec((blocks, three, HD), lambda h: (0, 0, h))],
        out_specs=pl.BlockSpec((blocks, rows, HD), lambda h: (0, 0, h)),
        compiler_params=pltpu.CompilerParams(vmem_limit_bytes=40 * MIB),
        cost_estimate=pl.CostEstimate(
            flops=4 * length * length * part,
            bytes_accessed=8 * length * part,
            transcendentals=length * length * part // HD,
        ),
    )(x)


INNER, COLS, PLANE, ATTEND = 0, 1, 5, 6


def halves_kernel(place_ref, q_ref, k_ref, v_ref, first_ref, second_ref):
    rows, width = q_ref.shape
    half = width // 2

    def copy(lower, upper):
        for i, ref in enumerate((q_ref, k_ref, v_ref)):
            lower[i * rows : (i + 1) * rows] = ref[:, :half]
            upper[i * rows : (i + 1) * rows] = ref[:, half:]

    @pl.when(place_ref[PLANE] < 2)
    def _():
        copy(first_ref, second_ref)

    @pl.when(place_ref[PLANE] >= 2)
    def _():
        copy(second_ref, first_ref)


def middle_kernel(place_ref, own_in, near_in, mid_in, far_in, *refs):
    *outs, x_ref, ctx_ref, sems = refs
    blocks, three, half = x_ref.shape
    rows = three // 3

    @pl.when(place_ref[INNER] == 1)
    def _():
        copies = [
            pltpu.make_async_copy(ref, x_ref.at[place_ref[ATTEND + i]], sems.at[i])
            for i, ref in enumerate((own_in, near_in, mid_in, far_in))
        ]
        for copy in copies:
            copy.start()
        for copy in copies:
            copy.wait()

        def step(i, carry):
            for j in range(2):
                cols = pl.ds(pl.multiple_of((2 * i + j) * HD, HD), HD)
                attend_columns(x_ref, cols, ctx_ref)
            return carry

        lax.fori_loop(0, half // HD // 2, step, 0)
        for i, out in enumerate(outs):
            out[...] = ctx_ref[place_ref[ATTEND + i]]


def line_of_four(place, queries, keys, values, gate, up, down, cot_rows):
    rows, width = queries.shape
    half = width // 2
    block = sds((3 * rows, half))
    first, second = call(
        halves_kernel,
        (block, block),
        (place, queries, keys, values),
        [SMEM, VMEM, VMEM, VMEM],
        moved=12 * rows * width,
    )
    gate_end = send(gate, OUTWARD)
    up_end = send(up, OUTWARD)
    down_end = send(down, OUTWARD, gate_end)
    gate_mid = send(gate, MIDDLE)
    gate_far = send(gate_mid, OUTWARD)
    near = send(first, INWARD, gate_mid, gate_end)
    mid = send(second, MIDDLE, gate_mid, gate_end)
    far = send(second, [(0, 2), (3, 1)], gate_mid, gate_end)
    piece = sds((rows, half))
    pieces = call(
        middle_kernel,
        (piece,) * 4,
        (place, first, near, mid, far),
        [SMEM] + [HBM] * 4,
        [
            pltpu.VMEM((4, 3 * rows, half), BF),
            pltpu.VMEM((4, rows, half), BF),
            pltpu.SemaphoreType.DMA((4,)),
        ],
        flops=64 * rows * rows * half,
        moved=32 * rows * half,
        after=(gate_end, up_end, gate_far, cot_rows),
    )
    up_mid = send(up, MIDDLE, near, mid, far)
    gate_inner = send(gate, INWARD, near, far, gate_end, up_end)
    up_inner = send(up, INWARD, near, far, gate_end, up_end)
    down_inner = send(down, INWARD, gate_inner)
    own, near, mid, far = lax.optimization_barrier((*pieces, gate_inner, down_end))[:4]
    mid = send(mid, MIDDLE)
    far = send(far, [(2, 0), (1, 3)])
    up_far = send(up_mid, OUTWARD, pieces[0])
    near = send(near, OUTWARD, up_far)
    gate_mid_near = send(gate_inner, MIDDLE)
    up_mid_near = send(up_inner, MIDDLE, pieces[0])
    down_mid = send(down, MIDDLE, gate_mid_near)
    down_mid_near = send(down_inner, MIDDLE, up_mid_near)
    gate_far_near = send(gate_mid_near, OUTWARD)
    up_far_near = send(up_mid_near, OUTWARD, gate_far_near)
    down_far = send(down_mid, OUTWARD, gate_far_near)
    down_far_near = send(down_mid_near, OUTWARD, up_far_near)
    norm_after = (gate_mid_near,)
    up_after = (down_mid_near,)
    gate_in = [
        [gate],
        [gate_inner, gate_end],
        [gate_mid, gate_far],
        [gate_mid_near, gate_far_near],
    ]
    up_in = [[up], [up_inner, up_end], [up_mid, up_far], [up_mid_near, up_far_near]]
    down_in = [
        [down],
        [down_inner, down_end],
        [down_mid, down_far],
        [down_mid_near, down_far_near],
    ]
    return (own, near, mid, far), gate_in, up_in, down_in, norm_after, up_after


def join_middle(place_ref, pieces, ctx_ref):
    own, near, mid, far = pieces
    half = own.shape[1]
    for plane, (lower, upper) in enumerate(((near, far), (own, mid), (mid, own), (far, near))):

        @pl.when(place_ref[PLANE] == plane)
        def _(lower=lower, upper=upper):
            ctx_ref[:, :half] = lower[...]
            ctx_ref[:, half:] = upper[...]


def join_groups(place_ref, pieces, ctx_ref):
    (ctx,) = pieces
    groups, _, part = ctx.shape
    for g in range(groups):
        ctx_ref[:, g * part : (g + 1) * part] = ctx[g]


def slot_rows(ids_t, owners, cap):
    tokens = ids_t.shape[1]
    experts = lax.broadcasted_iota(jnp.int32, (owners, tokens), 0)
    first = (experts == ids_t[0:1]).astype(F32)
    second = (experts == ids_t[1:2]).astype(F32)
    src = lax.broadcasted_iota(jnp.int32, (tokens, tokens), 0)
    dst = lax.broadcasted_iota(jnp.int32, (tokens, tokens), 1)
    earlier = (src < dst).astype(F32).astype(BF)
    count = mm((first + second).astype(BF), earlier, NN)
    slot0 = jnp.sum(first * count, axis=0, keepdims=True).astype(jnp.int32)
    slot1 = jnp.sum(second * count, axis=0, keepdims=True).astype(jnp.int32)
    return ids_t[0:1] * cap + slot0, ids_t[1:2] * cap + slot1


def slot_cols(ids, owners, cap):
    tokens = ids.shape[0]
    experts = lax.broadcasted_iota(jnp.int32, (tokens, owners), 1)
    first = (experts == ids[:, 0:1]).astype(F32)
    second = (experts == ids[:, 1:2]).astype(F32)
    dst = lax.broadcasted_iota(jnp.int32, (tokens, tokens), 0)
    src = lax.broadcasted_iota(jnp.int32, (tokens, tokens), 1)
    earlier = (src < dst).astype(F32).astype(BF)
    count = mm(earlier, (first + second).astype(BF), NN)
    slot0 = jnp.sum(first * count, axis=1, keepdims=True).astype(jnp.int32)
    slot1 = jnp.sum(second * count, axis=1, keepdims=True).astype(jnp.int32)
    return ids[:, 0:1] * cap + slot0, ids[:, 1:2] * cap + slot1


def one_hot(hit):
    return jnp.where(hit, 1.0, 0.0).astype(BF)


def send_cot_kernel(owners, cap, ids_ref, w_ref, cot_ref, o_ref):
    tokens = cot_ref.shape[0]
    at0, at1 = slot_rows(ids_ref[...], owners, cap)
    rows = lax.broadcasted_iota(jnp.int32, (owners * cap, tokens), 0)
    cot = cot_ref[...].astype(F32)
    o_ref[...] = (
        mm(one_hot(rows == at0), (w_ref[:, 0:1] * cot).astype(BF), NN)
        + mm(one_hot(rows == at1), (w_ref[:, 1:2] * cot).astype(BF), NN)
    ).astype(BF)


def norm_kernel(owners, cap, join, place_ref, ids_ref, resid_ref, gain_ref, *refs):
    *pieces, stream_ref, o_ref, ctx_ref = refs
    tokens, width = resid_ref.shape
    join(place_ref, pieces, ctx_ref)
    stream = (resid_ref[...].astype(F32) + ctx_ref[...].astype(F32)).astype(BF)
    stream_ref[...] = stream
    stream = stream.astype(F32)
    square = jnp.sum(stream * stream, axis=-1, keepdims=True)
    inv_rms = lax.rsqrt(square / width + 1e-05)
    at0, at1 = slot_rows(ids_ref[...], owners, cap)
    rows = lax.broadcasted_iota(jnp.int32, (owners * cap, tokens), 0)
    pick = one_hot((rows == at0) | (rows == at1))
    normed = ((stream_ref[...].astype(F32) * inv_rms) * gain_ref[...]).astype(BF)
    o_ref[...] = mm(pick, normed, NN).astype(BF)


def fetch(inner, choices, dst, sem):
    if len(choices) == 1:
        pltpu.make_async_copy(choices[0], dst, sem).start()
        return

    @pl.when(inner == 1)
    def _():
        pltpu.make_async_copy(choices[0], dst, sem).start()

    @pl.when(inner == 0)
    def _():
        pltpu.make_async_copy(choices[1], dst, sem).start()


def arrived(choices, dst, sem):
    pltpu.make_async_copy(choices[0], dst, sem).wait()


def regroup(refs, shape):
    refs = list(refs)
    return [[refs.pop(0) for _ in range(size)] for size in shape], refs


def cols_of(place_ref, slot, part):
    return pl.ds(pl.multiple_of(place_ref[COLS + slot] * part, part), part)


def gate_kernel(shape, place_ref, x_ref, *refs):
    slots = len(shape)
    gate_in, refs = regroup(refs, shape)
    o_ref, gate_w, sems = refs
    inner = place_ref[INNER]
    for j in range(slots):
        fetch(inner, gate_in[j], gate_w.at[j], sems.at[j])
    o_ref[...] = by_slots(place_ref, x_ref, gate_in, gate_w, sems)


def by_slots(place_ref, x_ref, weight_in, weight, sems):
    slots, _, part = weight.shape
    total = None
    for j in range(slots):
        rows = x_ref[:, cols_of(place_ref, j, part)]
        arrived(weight_in[j], weight.at[j], sems.at[j])
        term = mm(rows, weight[j], NT)
        total = term if total is None else total + term
    return total


def up_kernel(shape, place_ref, x_ref, gate_ref, *refs):
    slots = len(shape)
    up_in, refs = regroup(refs, shape)
    hidden_ref, to_gate_ref, to_up_ref, up_w, sems = refs
    inner = place_ref[INNER]
    for j in range(slots):
        fetch(inner, up_in[j], up_w.at[j], sems.at[j])
    gate = gate_ref[...]
    sigma = 1.0 / (1.0 + jnp.exp(-gate))
    silu = gate * sigma
    to_up_ref[...] = silu
    to_gate_ref[...] = sigma * (1.0 + gate * (1.0 - sigma))
    up = by_slots(place_ref, x_ref, up_in, up_w, sems)
    hidden_ref[...] = (to_up_ref[...] * up).astype(BF)
    to_gate_ref[...] = up * to_gate_ref[...]


def down_kernel(shape, first, place_ref, hidden_ref, cot_ref, *refs):
    slots = len(shape)
    refs = list(refs)
    before_ref = refs.pop(0) if first else None
    total = refs.pop(0)[...] if first else None
    down_in, refs = regroup(refs, shape)
    out_ref, d_hidden_ref, down_w, sems = refs
    part = down_w.shape[2]
    inner = place_ref[INNER]
    for j in range(slots):
        fetch(inner, down_in[j], down_w.at[j], sems.at[j])
    if first:
        out_ref[:, : first * part] = before_ref[...]
    for j in range(slots):
        rows = cot_ref[:, cols_of(place_ref, first + j, part)]
        arrived(down_in[j], down_w.at[j], sems.at[j])
        term = mm(rows, down_w[j], NT)
        total = term if total is None else total + term
        at = (first + j) * part
        out_ref[:, at : at + part] = mm(hidden_ref[...], down_w[j], NN).astype(BF)
    d_hidden_ref[...] = total


def grad_kernel(
    shape, place_ref, hidden_in, cot_in, d_hidden_in, to_gate_in, to_up_in, *refs
):
    slots = len(shape) - 1
    down_in, refs = regroup(refs, shape[-1:])
    gate_in, refs = regroup(refs, shape[:-1])
    up_in, refs = regroup(refs, shape[:-1])
    o_ref, down_w, gate_w, up_w, sems = refs[:5]
    hidden_ref, cot_ref, d_hidden_ref, to_gate_ref, to_up_ref = refs[5:]
    part = down_w.shape[1]
    inner = place_ref[INNER]
    last = place_ref[COLS + cot_in.shape[1] // part - 1]
    pairs = [
        (cot_in.at[:, pl.ds(pl.multiple_of(last * part, part), part)], cot_ref),
        (d_hidden_in, d_hidden_ref),
        (to_gate_in, to_gate_ref),
        (to_up_in, to_up_ref),
        (hidden_in, hidden_ref),
    ]
    fetch(inner, down_in[0], down_w, sems.at[2, 0])
    copies = [
        pltpu.make_async_copy(src, dst, sems.at[3 + i, 0]) for i, (src, dst) in enumerate(pairs)
    ]
    for copy in copies:
        copy.start()
    for j in range(slots):
        fetch(inner, gate_in[j], gate_w.at[j], sems.at[0, j])
        fetch(inner, up_in[j], up_w.at[j], sems.at[1, j])
    arrived(down_in[0], down_w, sems.at[2, 0])
    for copy in copies:
        copy.wait()
    d_hidden = d_hidden_ref[...] + mm(cot_ref[...], down_w[...], NT)
    d_gate = (d_hidden * to_gate_ref[...]).astype(BF)
    d_up = (d_hidden * to_up_ref[...]).astype(BF)
    o_ref[:, slots * part :] = mm(hidden_ref[...], down_w[...], NN).astype(BF)
    for j in range(slots):
        arrived(gate_in[j], gate_w.at[j], sems.at[0, j])
        arrived(up_in[j], up_w.at[j], sems.at[1, j])
        o_ref[:, j * part : (j + 1) * part] = (
            mm(d_gate, gate_w[j], NN) + mm(d_up, up_w[j], NN)
        ).astype(BF)


def final_kernel(
    owners,
    cap,
    place_ref,
    ids_ref,
    w_ref,
    gain_ref,
    stream_ref,
    cot_ref,
    first_ref,
    last_ref,
    output_ref,
    grad_ref,
    d_normed_ref,
):
    tokens, width = stream_ref.shape
    done = first_ref.shape[1]
    part = width - done
    slots = width // part
    at0, at1 = slot_cols(ids_ref[...], owners, cap)
    rows = lax.broadcasted_iota(jnp.int32, (tokens, owners * cap), 1)
    pick0, pick1 = one_hot(rows == at0), one_hot(rows == at1)
    both = pick0 + pick1
    w0, w1 = w_ref[:, 0:1], w_ref[:, 1:2]
    square = jnp.zeros((tokens, 1), F32)
    dot = jnp.zeros((tokens, 1), F32)
    for j in range(slots):
        cols = cols_of(place_ref, j, part)
        if j < slots - 1:
            pairs = first_ref[:, j * part : (j + 1) * part]
        else:
            pairs = last_ref[:, width:]
        stream = stream_ref[:, cols].astype(F32)
        mixed = w0 * mm(pick0, pairs, NN) + w1 * mm(pick1, pairs, NN)
        output_ref[:, cols] = (stream + mixed).astype(BF)
        grads = last_ref[:, j * part : (j + 1) * part]
        gained = mm(both, grads, NN) * gain_ref[:, cols]
        d_normed_ref[:, cols] = gained
        square = square + jnp.sum(stream * stream, axis=-1, keepdims=True)
        dot = dot + jnp.sum(gained * stream, axis=-1, keepdims=True)
    inv_rms = lax.rsqrt(square / width + 1e-05)
    mean = dot * inv_rms / width
    unit_rows = stream_ref[...].astype(F32) * inv_rms
    d_stream = inv_rms * (d_normed_ref[...] - unit_rows * mean)
    grad_ref[...] = (cot_ref[...].astype(F32) + d_stream).astype(BF)


MIDDLE = [(1, 2), (2, 1)]
OUTWARD = [(1, 0), (2, 3)]
INWARD = [(0, 1), (3, 2)]


def gather_all(shard, groups):
    whole_weight = lax.all_gather(shard, "seq", axis=0)
    return [[whole_weight[j]] for j in range(groups)]


def send(array, pairs, *first):
    return lax.ppermute(gated(array, *first), "seq", pairs)


def places(groups):
    if groups == 4:
        own = lax.axis_index("seq")
        table = jnp.array(
            [
                [0, 0, 1, 2, 3, 0, 0, 0, 0, 0],
                [1, 1, 0, 2, 3, 1, 1, 0, 2, 3],
                [1, 2, 3, 1, 0, 2, 2, 3, 1, 0],
                [0, 3, 2, 1, 0, 3, 0, 0, 0, 0],
            ],
            jnp.int32,
        )
        return table[own]
    return jnp.arange(-1, groups, dtype=jnp.int32)


def exchange(rows, owners, axis):
    total, width = rows.shape
    rows = rows.reshape(owners, total // owners, width)
    rows = lax.all_to_all(rows, axis, split_axis=0, concat_axis=0, tiled=True)
    return rows.reshape(total, width)


def flat(slots):
    return [ref for choices in slots for ref in choices]


def per_device(
    queries,
    keys,
    values,
    resid,
    norm_gain,
    w_gate,
    w_up,
    w_down,
    expert_ids,
    route_weights,
    cotangent,
):
    groups = lax.axis_size("seq")
    owners = lax.axis_size("exp")
    tokens, width = queries.shape[1:]
    ffw = w_gate.shape[2]
    part = width // groups
    cap = max(2, tokens * 10 // (4 * owners))
    total = owners * cap
    ids = expert_ids[0]
    ids_t = ids.T
    weights = route_weights[0]
    gain = norm_gain[None]
    cot = cotangent[0]
    place = places(groups)

    one = 2 * total * width * ffw
    send_cot = call(
        functools.partial(send_cot_kernel, owners, cap),
        sds((total, width)),
        (ids_t, weights, cot),
        [VMEM] * 3,
        flops=4 * total * tokens * width,
        moved=2 * (total + tokens) * width,
    )
    cot_rows = exchange(send_cot, owners, "exp")
    shards = (w_gate[0].T, w_up[0].T, w_down[0])
    if groups == 4:
        join = join_middle
        pieces, gate_in, up_in, down_in, norm_after, up_after = line_of_four(
            place, queries[0], keys[0], values[0], *shards, cot_rows
        )
    else:
        join = join_groups
        gate_in, up_in, down_in = [gather_all(shard, groups) for shard in shards]
        packed = pack(queries[0], keys[0], values[0], groups)
        heads = lax.all_to_all(packed, "seq", split_axis=0, concat_axis=0, tiled=True)
        ctx = attend(heads)
        pieces = (lax.all_to_all(ctx, "seq", split_axis=0, concat_axis=0, tiled=True),)
        norm_after = up_after = ()
    shape = [len(choices) for choices in gate_in]

    stream, send_rows = call(
        functools.partial(norm_kernel, owners, cap, join),
        (sds((tokens, width)), sds((total, width))),
        (place, ids_t, resid[0], gain, *pieces),
        [SMEM] + [VMEM] * (3 + len(pieces)),
        [pltpu.VMEM((tokens, width), BF)],
        flops=2 * total * tokens * width,
        moved=2 * (total + 3 * tokens) * width,
        after=norm_after,
    )
    rows = exchange(send_rows, owners, "exp")

    full_w = pltpu.VMEM((groups, ffw, part), BF)
    gate_pre = call(
        functools.partial(gate_kernel, shape),
        sds((total, ffw), F32),
        (place, rows, *flat(gate_in)),
        [SMEM, VMEM] + [HBM] * sum(shape),
        [full_w, pltpu.SemaphoreType.DMA((groups,))],
        flops=one,
        moved=2 * width * ffw + 2 * total * width + 4 * total * ffw,
    )
    hidden, to_gate, to_up = call(
        functools.partial(up_kernel, shape),
        (sds((total, ffw)), sds((total, ffw), F32), sds((total, ffw), F32)),
        (place, rows, gate_pre, *flat(up_in)),
        [SMEM, VMEM, VMEM] + [HBM] * sum(shape),
        [full_w, pltpu.SemaphoreType.DMA((groups,))],
        flops=one,
        moved=2 * width * ffw + 2 * total * width + 14 * total * ffw,
        after=up_after,
    )
    out = d_hidden = None
    early = groups // 2
    for first, end in ((0, early), (early, groups - 1)):
        here = shape[first:end]
        out, d_hidden = call(
            functools.partial(down_kernel, here, first),
            (sds((total, end * part)), sds((total, ffw), F32)),
            (place, hidden, cot_rows, *([out, d_hidden] if first else []), *flat(down_in[first:end])),
            [SMEM] + [VMEM] * (4 if first else 2) + [HBM] * sum(here),
            [
                pltpu.VMEM((len(here), ffw, part), BF),
                pltpu.SemaphoreType.DMA((len(here),)),
            ],
            flops=2 * one * len(here) // groups,
            moved=2 * width * ffw * len(here) // groups + 4 * total * width + 10 * total * ffw,
        )
    back_first = exchange(out, owners, "exp")
    back = call(
        functools.partial(grad_kernel, [*shape, shape[-1]]),
        sds((total, width + part)),
        (
            place,
            hidden,
            cot_rows,
            d_hidden,
            to_gate,
            to_up,
            *flat(down_in[-1:]),
            *flat(gate_in),
            *flat(up_in),
        ),
        [SMEM] + [HBM] * (5 + shape[-1] + 2 * sum(shape)),
        [
            pltpu.VMEM((ffw, part), BF),
            full_w,
            full_w,
            pltpu.SemaphoreType.DMA((8, groups)),
            pltpu.VMEM((total, ffw), BF),
            pltpu.VMEM((total, part), BF),
            pltpu.VMEM((total, ffw), F32),
            pltpu.VMEM((total, ffw), F32),
            pltpu.VMEM((total, ffw), F32),
        ],
        flops=2 * one + 2 * one // groups,
        moved=4 * width * ffw + 4 * total * width + 14 * total * ffw,
    )
    back_last = exchange(back, owners, "exp")
    output, stream_grad = call(
        functools.partial(final_kernel, owners, cap),
        (sds((tokens, width)), sds((tokens, width))),
        (place, ids, weights, gain, stream, cot, back_first, back_last),
        [SMEM] + [VMEM] * 7,
        [pltpu.VMEM((tokens, width), F32)],
        flops=6 * total * tokens * width,
        moved=4 * total * width + 8 * tokens * width,
        vmem=16,
        held=True,
    )
    return (output[None], stream_grad[None])


def solution(mesh):
    placed = (
        P("exp", "seq", None),
        P("exp", "seq", None),
        P("exp", "seq", None),
        P("exp", "seq", None),
        P(),
        P("exp", "seq", None),
        P("exp", "seq", None),
        P("exp", None, "seq"),
        P("exp", "seq", None),
        P("exp", "seq", None),
        P("exp", "seq", None),
    )
    return jax.shard_map(
        per_device,
        mesh=mesh,
        in_specs=placed,
        out_specs=(P("exp", "seq", None), P("exp", "seq", None)),
        check_vma=False,
    )
```
